32 devices in a mesh: sector: 8 (over z, y), radial: 4 (over x, core).
Axes of the slice: x: 2, y: 2, z: 4, core: 2. Of those that a mesh axis runs over, the one named last changes fastest.
Arguments:
- density: float32 [1024, 64, 128], P('sector', 'radial'), may hold values from 0.4 to 1.2
- swirl: float32 [1024, 64, 128], P('sector', 'radial'), may hold values from -4 to 4
- heat_rate: float32 [1024, 64, 128], P('sector', 'radial'), may hold values from 0.1 to 3
- acoustic: float32 [3, 1024, 128], P(None, 'sector'), may hold values from -5 to 5
- mode_impedance: float32 [513], replicated, may hold values from 0.05 to 8
- mouth_azimuth: int32 [16], replicated, may hold values from 0 to 56, as said below
- mouth_radius: int32 [16], replicated, may hold values from 0 to 56, as said below
Outputs:
- density_next: float32 [1024, 64, 128], P('sector', 'radial')
- pressure: float32 [1024, 64, 128], P('sector', 'radial')
- acoustic_next: float32 [3, 1024, 128], P(None, 'sector')
The draws below stay inside these ranges and needn't reach their ends.
Inputs may be any that keep to these rules, and one draw needn't show every extreme that they name: Burner b's mouth starts at azimuthal cell b * 64 + mouth_azimuth[b] and spans 8 cells. Burner b's mouth spans radial cells mouth_radius[b] to mouth_radius[b] + 7.
All inputs are finite; a program needn't handle non-finite values.
Results may differ from the reference program's by a relative error of at most 0.00018.
Values sent between devices are 32-bit elements; how exact they have to be, the bound alone decides.
No kernel may reach another device: no remote copies, remote signals or barrier semaphores. Data moves between devices by JAX's collectives and lax.ppermute only.
A program may use at most 128 MiB of HBM per device.

```python
import math
import jax
import jax.numpy as jnp

NZ = 128
BURNERS = 16
MOUTH = 8
SWEEPS = 4
SUBSTEPS = 8
NT = 1024
NR = 64


def draw_mouth_azimuth(key, part):
    top = NT // BURNERS - MOUTH
    values = jax.random.randint(jax.random.fold_in(key, 11), (BURNERS,), 0, top + 1)
    chosen = jax.random.randint(jax.random.fold_in(key, 12), (), 0, BURNERS)
    values = values.at[chosen].set(top)
    values = values.at[(chosen + 1) % BURNERS].set(0)
    return values.astype(jnp.int32)


def draw_mouth_radius(key, part):
    top = NR - MOUTH
    values = jax.random.randint(jax.random.fold_in(key, 21), (BURNERS,), 0, top + 1)
    chosen = jax.random.randint(jax.random.fold_in(key, 22), (), 0, BURNERS)
    values = values.at[chosen].set(top)
    values = values.at[(chosen + 1) % BURNERS].set(0)
    return values.astype(jnp.int32)


def shard_levels(key, extent, pieces, least, high):
    factor_of, own = 1.0, jax.random.fold_in(key, 6)
    for axis_at, parts in pieces:
        heights = jnp.exp(jax.random.uniform(jax.random.fold_in(own, axis_at), (parts,), jnp.float32, least / len(pieces), high / len(pieces)))
        factor_of = factor_of * jnp.repeat(heights, extent[axis_at] // parts).reshape([-1 if axis == axis_at else 1 for axis in range(len(extent))])
    return factor_of


def bell_draw(own_key, dims, width, bound, pieces=(), kind=jnp.bfloat16):
    factor_of = shard_levels(own_key, dims, pieces, -0.22, 0.18) if pieces else 1.0
    entries = jax.random.normal(own_key, dims, jnp.float32) * width * factor_of
    return jnp.minimum(jnp.maximum(entries, -bound), bound).astype(kind)


def setup_inputs(seed: int = 0) -> dict:
    seeds = jax.random.split(jax.random.key(seed), 8)
    density = jnp.clip(0.4 + 0.800000042 * jax.random.uniform(seeds[0], (NT, NR, NZ), jnp.float32) ** shard_levels(seeds[0], (NT, NR, NZ), ((0, 8), (1, 4)), -0.2, 0.2), 0.4, 1.2)
    swirl = bell_draw(seeds[1], (NT, NR, NZ), 1.0, 4.0, ((0, 8), (1, 4)), jnp.float32)
    heat_rate = jnp.clip(jnp.exp(math.log(3.0) - 3.4011974 * jax.random.uniform(seeds[2], (NT, NR, NZ), jnp.float32) ** shard_levels(seeds[2], (NT, NR, NZ), ((0, 8), (1, 4)), -0.2, 0.2)), 0.1, 3.0)
    acoustic = bell_draw(seeds[3], (3, NT, NZ), 1.0, 5.0, ((1, 8),), jnp.float32)
    mode_impedance = jnp.clip(jnp.exp(jax.random.uniform(seeds[4], (NT // 2 + 1,), jnp.float32, math.log(0.05), math.log(8.0))), 0.05, 8.0)
    mouth_azimuth = draw_mouth_azimuth(jax.random.fold_in(seeds[7], 71), 0)
    mouth_radius = draw_mouth_radius(jax.random.fold_in(seeds[7], 71), 0)
    return dict(density=density, swirl=swirl, heat_rate=heat_rate, acoustic=acoustic, mode_impedance=mode_impedance, mouth_azimuth=mouth_azimuth, mouth_radius=mouth_radius)


time_step = 0.2
diffusion = 0.05
inflow_rate = 0.5
wave_speed = 0.5
heat_coupling = 0.5
feedback = 0.5


def axial_pair(field):
    zeros = jnp.zeros_like(field[:, :, :1])
    return jnp.concatenate([field[:, :, 1:], zeros], 2) + jnp.concatenate([zeros, field[:, :, :-1]], 2)


def jacobi(forcing, diagonal):
    solution = forcing / diagonal
    for sweep in range(SWEEPS - 1):
        padded = jnp.pad(solution, ((0, 0), (1, 1), (0, 0)))
        solution = (forcing + (padded[:, 2:] + padded[:, :-2]) + axial_pair(solution)) / diagonal
    return solution


def reference(density, swirl, heat_rate, acoustic, mode_impedance, mouth_azimuth, mouth_radius):
    theta = jnp.arange(NT, dtype=jnp.int32)
    radius = jnp.arange(NR, dtype=jnp.int32)
    theta_start = jnp.arange(BURNERS, dtype=jnp.int32) * (NT // BURNERS) + mouth_azimuth
    inside_theta = ((theta[None, :] >= theta_start[:, None]) & (theta[None, :] < theta_start[:, None] + MOUTH)).astype(jnp.float32)
    inside_radius = ((radius[None, :] >= mouth_radius[:, None]) & (radius[None, :] < mouth_radius[:, None] + MOUTH)).astype(jnp.float32)
    mouth_mask = jnp.dot(inside_theta.T, inside_radius, preferred_element_type=jnp.float32)

    heat_field = heat_rate * density * density
    source = jnp.sum(heat_field, axis=1) / NR

    wave_press, wave_along, wave_axial = acoustic[0], acoustic[1], acoustic[2]
    zeros = jnp.zeros_like(wave_press[:, :1])
    for substep in range(SUBSTEPS):
        press_up = jnp.roll(wave_press, -1, axis=0)
        press_axial = jnp.concatenate([wave_press[:, 1:], zeros], 1)
        wave_along = wave_along - wave_speed * (press_up - wave_press)
        wave_axial = wave_axial - wave_speed * (press_axial - wave_press)
        along_down = jnp.roll(wave_along, 1, axis=0)
        axial_down = jnp.concatenate([zeros, wave_axial[:, :-1]], 1)
        wave_press = wave_press - wave_speed * ((wave_along - along_down) + (wave_axial - axial_down)) + heat_coupling * source
    acoustic_next = jnp.stack([wave_press, wave_along, wave_axial])

    flux = swirl * density
    twice = 2.0 * density
    radial_pad = jnp.pad(density, ((0, 0), (1, 1), (0, 0)))
    laplace = (jnp.roll(density, -1, axis=0) + jnp.roll(density, 1, axis=0) - twice) + (radial_pad[:, 2:] + radial_pad[:, :-2] - twice) + (axial_pair(density) - twice)
    advection = -0.5 * (jnp.roll(flux, -1, axis=0) - jnp.roll(flux, 1, axis=0))
    density_next = density + time_step * (advection + diffusion * laplace) + inflow_rate * mouth_mask[:, :, None] * (1.0 - density)
    forcing = (density_next - density) / time_step + feedback * wave_press[:, None, :]

    spectrum = jnp.fft.rfft(forcing, axis=0)
    order = jnp.arange(NT // 2 + 1, dtype=jnp.int32)
    shifted = 2.0 - 2.0 * jnp.cos(order.astype(jnp.float32) * (2.0 * math.pi / NT))
    diagonal = (4.0 + shifted + mode_impedance)[:, None, None]
    cosine = jacobi(jnp.real(spectrum).astype(jnp.float32), diagonal)
    sine = jacobi((-jnp.imag(spectrum)).astype(jnp.float32), diagonal)
    pressure = jnp.fft.irfft(cosine - 1j * sine, n=NT, axis=0).astype(jnp.float32)
    return density_next, pressure, acoustic_next
```

```python
import math

import jax
import jax.numpy as jnp
import numpy as np
from jax import lax
from jax.experimental import pallas as pl
from jax.experimental.pallas import tpu as pltpu
from jax.sharding import PartitionSpec as P

BURNERS = 16
MOUTH = 8
SWEEPS = 4
SUBSTEPS = 8

time_step = 0.2
diffusion = 0.05
inflow_rate = 0.5
wave_speed = 0.5
heat_coupling = 0.5
feedback = 0.5

F32 = jnp.float32
BF16 = jnp.bfloat16
HALO = SWEEPS - 1
EDGE = 8
VMEM = pl.BlockSpec(memory_space=pltpu.VMEM)
SMEM = pl.BlockSpec(memory_space=pltpu.SMEM)
ANY = pl.BlockSpec(memory_space=pl.ANY)


def halves(table):
    high = table.astype(BF16)
    low = (table - high.astype(np.float64)).astype(BF16)
    return high, low


def axial_tables(cells):
    index = np.arange(1, cells + 1, dtype=np.float64)
    basis = math.sqrt(2.0 / (cells + 1)) * np.sin(
        np.pi * ((index[:, None] * index[None, :]) % (2 * (cells + 1))) / (cells + 1)
    )
    return basis, 2.0 * np.cos(np.pi * index / (cells + 1))


def mode_classes(n_theta):
    half = n_theta // 2
    multiples = np.arange(0, half, 4)
    first = (
        np.concatenate([multiples, [half], multiples[1:]]),
        np.concatenate([np.zeros(len(multiples) + 1), np.ones(len(multiples) - 1)]),
    )
    twos = np.arange(2, half, 4)
    second = (np.concatenate([twos, twos]), np.repeat([0, 1], len(twos)))
    ones, threes = np.arange(1, half, 4), np.arange(3, half, 4)
    third = (np.concatenate([ones, threes, ones, threes]), np.repeat([0, 1], half // 2))
    return first, second, third


def azimuth_tables(n_theta):
    bases = []
    for (order, odd), rows in zip(mode_classes(n_theta), (n_theta // 4, n_theta // 4, n_theta // 2)):
        phase = (np.arange(rows)[:, None] * order[None, :].astype(np.int64)) % n_theta
        angle = phase * (2.0 * np.pi / n_theta)
        bases.append(np.where(odd[None, :] == 0, np.cos(angle), np.sin(angle)))
    return bases


def diagonal_tables(n_theta):
    half = n_theta // 2
    order = np.concatenate([part[0] for part in mode_classes(n_theta)])
    shifted = 2.0 - 2.0 * np.cos(order * (2.0 * np.pi / n_theta))
    weight = np.where((order == 0) | (order == half), 1.0, 2.0) / n_theta
    return (4.0 + shifted).astype(np.float32), weight.astype(np.float32)


def mode_rows(impedance):
    half = impedance.shape[0] - 1
    by_four = impedance[:half].reshape(half // 4, 4).T
    q0, q1, q2, q3 = by_four[0], by_four[1], by_four[2], by_four[3]
    first = jnp.concatenate([impedance[half:], q0[1:]])
    return jnp.concatenate([q0, first, q2, q2, q1, q3, q1, q3])


def split(value):
    high = value.astype(BF16)
    return high, (value - high.astype(F32)).astype(BF16)


def product(left, right, dims):
    def one(a, b):
        return lax.dot_general(a, b, (dims, ((), ())), preferred_element_type=F32)

    return one(left[0], right[0]) + (one(left[1], right[0]) + one(left[0], right[1]))


NN = ((1,), (0,))
NT = ((1,), (1,))


def edges_kernel(density, swirl, heat_rate, acoustic, heat, first, last, head, tail):
    cells_theta, cells_radius, _ = density.shape
    total = None
    for r in range(cells_radius):
        rho = density[:, r, :]
        term = heat_rate[:, r, :] * rho * rho
        total = term if total is None else total + term
    heat[...] = total
    first[...] = density[:, 0, :]
    last[...] = density[:, cells_radius - 1, :]
    for out, row, begin in ((head, 0, 0), (tail, cells_theta - 1, cells_theta - EDGE)):
        rho = density[row]
        out[0:cells_radius] = rho
        out[cells_radius : 2 * cells_radius] = rho * swirl[row]
        for k in range(3):
            at = 2 * cells_radius + k * EDGE
            out[at : at + EDGE] = acoustic[k, begin : begin + EDGE]


def flow_kernel(
    chunks, n_theta, mouth_azimuth, mouth_radius, density, swirl, above, below, inner, outer,
    basis_high, basis_low, density_next, *rest
):
    sends, forcing = rest[:chunks], rest[chunks]
    sectors = lax.axis_size("sector")
    radials = lax.axis_size("radial")
    sector = lax.axis_index("sector")
    radial = lax.axis_index("radial")
    cells_theta, cells_radius, cells_axial = density.shape
    shape = (cells_radius, cells_axial)
    rows = lax.broadcasted_iota(jnp.int32, shape, 0)
    lanes = lax.broadcasted_iota(jnp.int32, shape, 1)
    has_inner = (radial > 0).astype(F32)
    has_outer = (radial < radials - 1).astype(F32)
    segment = n_theta // BURNERS
    part = min(segment, cells_theta)

    row_above = above[0:cells_radius], above[cells_radius : 2 * cells_radius]
    row_below = below[0:cells_radius], below[cells_radius : 2 * cells_radius]

    def at(t):
        if t < 0:
            return row_below
        if t >= cells_theta:
            return row_above
        rho = density[t]
        return rho, rho * swirl[t]

    window = [at(-1), at(0)]
    for t in range(cells_theta):
        window.append(at(t + 1))
        (rho_down, flux_down), (rho, _), (rho_up, flux_up) = window
        window = window[1:]
        if t % part == 0:
            burner = (sector * cells_theta + t) // segment
            start = burner * segment + mouth_azimuth[burner] - sector * cells_theta
            radius = mouth_radius[burner] - radial * cells_radius
            mouth = ((rows >= radius) & (rows < radius + MOUTH)).astype(F32) * inflow_rate
        open_here = ((start <= t) & (t < start + MOUTH)).astype(F32)
        gain = mouth * open_here
        r_up = jnp.where(
            rows == cells_radius - 1,
            jnp.broadcast_to(outer[t : t + 1, :] * has_outer, shape),
            pltpu.roll(rho, cells_radius - 1, 0),
        )
        r_down = jnp.where(
            rows == 0,
            jnp.broadcast_to(inner[t : t + 1, :] * has_inner, shape),
            pltpu.roll(rho, 1, 0),
        )
        z_up = jnp.where(lanes == cells_axial - 1, 0.0, pltpu.roll(rho, cells_axial - 1, 1))
        z_down = jnp.where(lanes == 0, 0.0, pltpu.roll(rho, 1, 1))
        twice = 2.0 * rho
        laplace = (rho_up + rho_down - twice) + (r_up + r_down - twice) + (z_up + z_down - twice)
        advection = -0.5 * (flux_up - flux_down)
        flow = advection + diffusion * laplace
        inflow = gain * (1.0 - rho)
        density_next[t] = rho + time_step * flow + inflow
        forcing[t] = flow + inflow * (1.0 / time_step)

    basis = basis_high[...], basis_low[...]
    own = cells_axial // sectors
    each = own // chunks
    for r in range(cells_radius):
        modes = product(basis, split(forcing[:, r, :]), NT)
        for d in range(sectors):
            for c in range(chunks):
                begin = d * own + c * each
                sends[c][d, r * each : (r + 1) * each, :] = modes[begin : begin + each]


def acoustic_kernel(
    n_radius, columns, acoustic, above, below, source, source_above, source_below, basis_high,
    basis_low, send_in, acoustic_next, send, staged, sem
):
    cells_theta, cells_axial = source.shape
    skip = above.shape[0] - 3 * EDGE

    def extended(k):
        begin = skip + k * EDGE
        return jnp.concatenate(
            [below[begin : begin + EDGE], acoustic[k], above[begin : begin + EDGE]], 0
        )

    press, along, axial = extended(0), extended(1), extended(2)
    heat = jnp.concatenate([source_below[...], source[...], source_above[...]], 0)
    heat = heat * (heat_coupling / n_radius)
    count = press.shape[0]
    lanes = lax.broadcasted_iota(jnp.int32, press.shape, 1)
    for _ in range(SUBSTEPS):
        press_up = pltpu.roll(press, count - 1, 0)
        press_axial = jnp.where(lanes == cells_axial - 1, 0.0, pltpu.roll(press, cells_axial - 1, 1))
        along = along - wave_speed * (press_up - press)
        axial = axial - wave_speed * (press_axial - press)
        along_down = pltpu.roll(along, 1, 0)
        axial_down = jnp.where(lanes == 0, 0.0, pltpu.roll(axial, 1, 1))
        press = press - wave_speed * ((along - along_down) + (axial - axial_down)) + heat
    own = slice(EDGE, EDGE + cells_theta)
    acoustic_next[0] = press[own]
    acoustic_next[1] = along[own]
    acoustic_next[2] = axial[own]
    modes = product((basis_high[...], basis_low[...]), split(feedback * press[own]), NT)
    staged[...] = modes.reshape(staged.shape)
    copy = pltpu.make_async_copy(
        staged, send.at[:, pl.ds(columns, staged.shape[1]), :], sem
    )
    copy.start()
    copy.wait()


def forward_kernel(edge, columns, received, w0h, w0l, w1h, w1l, w2h, w2l, modes, first, last):
    blocks = received.shape[0]
    quarter = blocks // 4

    def joined(parts):
        return jnp.concatenate(parts, 1) if len(parts) > 1 else parts[0]

    pieces = [received[s] for s in range(blocks)]
    half = blocks // 2
    even = [pieces[s] + pieces[s + half] for s in range(half)]
    odd = [pieces[s] - pieces[s + half] for s in range(half)]
    both = [even[s] + even[s + quarter] for s in range(quarter)]
    apart = [even[s] - even[s + quarter] for s in range(quarter)]
    at = 0
    for parts, wh, wl in ((both, w0h, w0l), (apart, w1h, w1l), (odd, w2h, w2l)):
        width = wh.shape[1]
        out = product(split(joined(parts)), (wh[...], wl[...]), NN)
        modes[:, at : at + width] = out
        first[:, at : at + width] = out[:edge]
        last[:, at : at + width] = out[columns - edge : columns]
        at += width


def solve_kernel(
    chunk, chunks, modes, inner, outer, wave, inverse, scaled, axial, w0h, w0l, w1h, w1l, w2h,
    w2l, send, solved
):
    radials = lax.axis_size("radial")
    radial = lax.axis_index("radial")
    sector = lax.axis_index("sector")
    n_theta = modes.shape[1]
    each = axial.shape[1] // chunks
    cells_radius = inner.shape[0] // each // HALO
    cells_radius = send.shape[1] // each
    has_inner = (radial > 0).astype(F32)
    has_outer = (radial < radials - 1).astype(F32)
    eigen = axial[sector][chunk * each : (chunk + 1) * each, :]
    step = eigen.shape[1]
    total = cells_radius + 2 * HALO
    for block in range(n_theta // step):
        lane = slice(block * step, (block + 1) * step)
        inv = jnp.broadcast_to(inverse[:, lane], (each, step))
        inv_inner, inv_outer = inv * has_inner, inv * has_outer
        last_scale = jnp.broadcast_to(scaled[:, lane], (each, step))
        add = wave[chunk * each : (chunk + 1) * each, lane]

        def row_of(i):
            if i < HALO:
                return inner[i * each : (i + 1) * each, lane]
            i -= HALO
            if i < cells_radius:
                return modes[i * each : (i + 1) * each, lane]
            i -= cells_radius
            return outer[i * each : (i + 1) * each, lane]

        def scale_of(i):
            if i < HALO:
                return inv_inner
            return inv if i < HALO + cells_radius else inv_outer

        right = [row_of(i) + add for i in range(total)]
        x = [right[i] * scale_of(i) for i in range(total)]
        for sweep in range(1, SWEEPS):
            fresh = [None] * total
            for i in range(sweep, total - sweep):
                scale = last_scale if sweep == SWEEPS - 1 else scale_of(i)
                fresh[i] = (right[i] + (x[i + 1] + x[i - 1]) + eigen * x[i]) * scale
            x = fresh
        for i in range(cells_radius):
            solved[i * each : (i + 1) * each, lane] = x[i + HALO]

    sectors = send.shape[0]
    width = send.shape[2]
    n0, n1 = w0h.shape[1], w1h.shape[1]
    value = split(solved[:, :n0])
    both = product(value, (w0h[...], w0l[...]), NT)
    value = split(solved[:, n0 : n0 + n1])
    apart = product(value, (w1h[...], w1l[...]), NT)
    value = split(solved[:, n0 + n1 :])
    odd = product(value, (w2h[...], w2l[...]), NT)
    even = jnp.concatenate([both + apart, both - apart], 1)
    for s in range(sectors // 2):
        lane = slice(s * width, (s + 1) * width)
        send[s] = even[:, lane] + odd[:, lane]
        send[s + sectors // 2] = even[:, lane] - odd[:, lane]


def pressure_kernel(chunks, *refs):
    received, (basis_high, basis_low, pressure) = refs[:chunks], refs[chunks:]
    cells_radius = pressure.shape[1]
    sectors = received[0].shape[0]
    each = received[0].shape[1] // cells_radius
    basis = basis_high[...], basis_low[...]
    for r in range(cells_radius):
        rows = [
            received[c][d, r * each : (r + 1) * each, :]
            for d in range(sectors)
            for c in range(chunks)
        ]
        modes = jnp.concatenate(rows, 0)
        pressure[:, r, :] = product(split(modes.T), basis, NN)


def call(kernel, outs, ins, scratch=(), **more):
    flops = more.pop("flops", 0)
    moved = sum(math.prod(o.shape) * 4 for o in outs)
    return pl.pallas_call(
        kernel,
        out_shape=outs,
        in_specs=ins,
        out_specs=more.pop("out_specs", [VMEM] * len(outs)),
        scratch_shapes=list(scratch),
        cost_estimate=pl.CostEstimate(flops=flops, bytes_accessed=3 * moved, transcendentals=0),
        compiler_params=pltpu.CompilerParams(vmem_limit_bytes=40 * 1024 * 1024),
        **more,
    )


def shape(*dims):
    return jax.ShapeDtypeStruct(dims, F32)


def shifted(value, axis, steps):
    count = lax.axis_size(axis)
    return lax.ppermute(value, axis, [(i, (i + steps) % count) for i in range(count)])


def exchanged(value):
    return lax.all_to_all(value, "sector", split_axis=0, concat_axis=0, tiled=True)


def shards(density, swirl, heat_rate, acoustic, mode_impedance, mouth_azimuth, mouth_radius):
    sectors = lax.axis_size("sector")
    radials = lax.axis_size("radial")
    cells_theta, cells_radius, cells_axial = density.shape
    n_theta = cells_theta * sectors
    n_radius = cells_radius * radials
    own = cells_axial // sectors
    chunks = max(1, min(2, own // 8))
    each = own // chunks
    columns = cells_radius * each
    edge = HALO * each

    basis, eigen = axial_tables(cells_axial)
    basis_high, basis_low = (jnp.asarray(t) for t in halves(basis))
    eigen = jnp.asarray(
        np.broadcast_to(eigen.reshape(sectors, own, 1), (sectors, own, 128)).astype(np.float32)
    )
    tables = []
    for table in azimuth_tables(n_theta):
        tables += [jnp.asarray(t) for t in halves(table)]
    fixed, weight = diagonal_tables(n_theta)
    inverse = (1.0 / (jnp.asarray(fixed) + mode_rows(mode_impedance)))[None, :]
    scaled = inverse * jnp.asarray(weight)[None, :]

    packed = 2 * cells_radius + 3 * EDGE
    row_block = shape(cells_theta, cells_axial)
    heat, first, last, head, tail = call(
        edges_kernel,
        [row_block] * 3 + [shape(packed, cells_axial)] * 2,
        [VMEM] * 4,
    )(density, swirl, heat_rate, acoustic)
    above = shifted(head, "sector", -1)
    below = shifted(tail, "sector", 1)
    outer = shifted(first, "radial", -1)
    inner = shifted(last, "radial", 1)

    step = 1
    while step < radials:
        heat = heat + lax.ppermute(heat, "radial", [(i, i ^ step) for i in range(radials)])
        step *= 2
    source_above = shifted(heat[:EDGE], "sector", -1)
    source_below = shifted(heat[-EDGE:], "sector", 1)

    sent = [shape(sectors, columns, cells_theta)] * (chunks - 1)
    sent.append(shape(sectors, columns + own, cells_theta))
    density_next, *sends = call(
        lambda *refs: flow_kernel(chunks, n_theta, *refs),
        [shape(*density.shape)] + sent,
        [SMEM] * 2 + [VMEM] * 8,
        [pltpu.VMEM(density.shape, F32)],
    )(mouth_azimuth, mouth_radius, density, swirl, above, below, inner, outer, basis_high, basis_low)

    acoustic_next, sends[-1] = call(
        lambda *refs: acoustic_kernel(n_radius, columns, *refs),
        [shape(*acoustic.shape), sent[-1]],
        [VMEM] * 8 + [ANY],
        [pltpu.VMEM((sectors, own, cells_theta), F32), pltpu.SemaphoreType.DMA],
        out_specs=[VMEM, ANY],
        input_output_aliases={8: 1},
    )(acoustic, above, below, heat, source_above, source_below, basis_high, basis_low, sends[-1])

    received = [exchanged(value) for value in sends]
    modes = []
    for c in range(chunks):
        count = received[c].shape[1]
        c_modes, c_first, c_last = call(
            lambda *refs: forward_kernel(edge, columns, *refs),
            [shape(count, n_theta), shape(edge, n_theta), shape(edge, n_theta)],
            [VMEM] * 7,
        )(received[c], *tables)
        modes.append((c_modes, shifted(c_last, "radial", 1), shifted(c_first, "radial", -1)))
    wave = modes[-1][0][columns:]

    results = []
    for c in range(chunks):
        (send,) = call(
            lambda *refs: solve_kernel(c, chunks, *refs),
            [shape(sectors, columns, cells_theta)],
            [VMEM] * 13,
            [pltpu.VMEM((columns, n_theta), F32)],
        )(*modes[c], wave, inverse, scaled, eigen, *tables)
        results.append(exchanged(send))

    (pressure,) = call(
        lambda *refs: pressure_kernel(chunks, *refs),
        [shape(*density.shape)],
        [VMEM] * (chunks + 2),
    )(*results, basis_high, basis_low)
    return density_next, pressure, acoustic_next


def solution(mesh):
    return jax.shard_map(
        shards,
        mesh=mesh,
        in_specs=(
            P("sector", "radial", None),
            P("sector", "radial", None),
            P("sector", "radial", None),
            P(None, "sector", None),
            P(),
            P(),
            P(),
        ),
        out_specs=(
            P("sector", "radial", None),
            P("sector", "radial", None),
            P(None, "sector", None),
        ),
        check_vma=False,
    )
```

```python
import math

import jax
import jax.numpy as jnp
import numpy as np
from jax import lax
from jax.experimental import pallas as pl
from jax.experimental.pallas import tpu as pltpu
from jax.sharding import PartitionSpec as P

BURNERS = 16
MOUTH = 8
SWEEPS = 4
SUBSTEPS = 8

time_step = 0.2
diffusion = 0.05
inflow_rate = 0.5
wave_speed = 0.5
heat_coupling = 0.5
feedback = 0.5

F32 = jnp.float32
BF16 = jnp.bfloat16
HALO = SWEEPS - 1
EDGE = 8
VMEM = pl.BlockSpec(memory_space=pltpu.VMEM)
SMEM = pl.BlockSpec(memory_space=pltpu.SMEM)
HBM = pl.BlockSpec(memory_space=pltpu.HBM)


def halves(table):
    high = table.astype(BF16)
    low = (table - high.astype(np.float64)).astype(BF16)
    return high, low


def axial_tables(cells):
    index = np.arange(1, cells + 1, dtype=np.float64)
    basis = math.sqrt(2.0 / (cells + 1)) * np.sin(
        np.pi * ((index[:, None] * index[None, :]) % (2 * (cells + 1))) / (cells + 1)
    )
    return basis, 2.0 * np.cos(np.pi * index / (cells + 1))


def mode_classes(n_theta):
    half = n_theta // 2
    multiples = np.arange(0, half, 4)
    first = (
        np.concatenate([multiples, [half], multiples[1:]]),
        np.concatenate([np.zeros(len(multiples) + 1), np.ones(len(multiples) - 1)]),
    )
    twos = np.arange(2, half, 4)
    second = (np.concatenate([twos, twos]), np.repeat([0, 1], len(twos)))
    ones, threes = np.arange(1, half, 4), np.arange(3, half, 4)
    third = (np.concatenate([ones, threes, ones, threes]), np.repeat([0, 1], half // 2))
    return first, second, third


def azimuth_tables(n_theta):
    bases = []
    for (order, odd), rows in zip(mode_classes(n_theta), (n_theta // 4, n_theta // 4, n_theta // 2)):
        phase = (np.arange(rows)[:, None] * order[None, :].astype(np.int64)) % n_theta
        angle = phase * (2.0 * np.pi / n_theta)
        bases.append(np.where(odd[None, :] == 0, np.cos(angle), np.sin(angle)))
    return bases


def diagonal_tables(n_theta):
    half = n_theta // 2
    order = np.concatenate([part[0] for part in mode_classes(n_theta)])
    shifted = 2.0 - 2.0 * np.cos(order * (2.0 * np.pi / n_theta))
    weight = np.where((order == 0) | (order == half), 1.0, 2.0) / n_theta
    return (4.0 + shifted).astype(np.float32), weight.astype(np.float32)


def mode_rows(impedance):
    half = impedance.shape[0] - 1
    by_four = impedance[:half].reshape(half // 4, 4).T
    q0, q1, q2, q3 = by_four[0], by_four[1], by_four[2], by_four[3]
    first = jnp.concatenate([impedance[half:], q0[1:]])
    return jnp.concatenate([q0, first, q2, q2, q1, q3, q1, q3])


def split(value):
    high = value.astype(BF16)
    return high, (value - high.astype(F32)).astype(BF16)


def product(left, right, dims):
    def one(a, b):
        return lax.dot_general(a, b, (dims, ((), ())), preferred_element_type=F32)

    return one(left[0], right[0]) + (one(left[1], right[0]) + one(left[0], right[1]))


NN = ((1,), (0,))
NT = ((1,), (1,))


def edges_kernel(
    density, swirl, heat_rate, acoustic, first, last, head, tail, rho, rate, spin, wave, sems
):
    cells_theta, cells_radius, _ = density.shape
    copies = []

    def fetch(source, target):
        copy = pltpu.make_async_copy(source, target, sems.at[len(copies)])
        copy.start()
        copies.append(copy)

    for side, begin, row in ((0, 0, 0), (1, cells_theta - EDGE, cells_theta - 1)):
        fetch(density.at[pl.ds(begin, EDGE)], rho.at[side])
        fetch(heat_rate.at[pl.ds(begin, EDGE)], rate.at[side])
        fetch(swirl.at[pl.ds(row, 1)], spin.at[side])
        fetch(acoustic.at[:, pl.ds(begin, EDGE)], wave.at[side])
    fetch(density.at[:, 0, :], first)
    fetch(density.at[:, cells_radius - 1, :], last)
    for copy in copies:
        copy.wait()
    for side, out, row in ((0, head, 0), (1, tail, EDGE - 1)):
        edge = rho[side, row]
        out[0:cells_radius] = edge
        out[cells_radius : 2 * cells_radius] = edge * spin[side, 0]
        at = 2 * cells_radius
        for k in range(3):
            out[at : at + EDGE] = wave[side, k]
            at += EDGE
        heat = jnp.sum(rate[side] * rho[side] * rho[side], axis=1)
        out[at : at + EDGE] = heat


def flow_kernel(n_theta, mouth_azimuth, mouth_radius, density, swirl, heat_rate, forcing, heat):
    sector = lax.axis_index("sector")
    radial = lax.axis_index("radial")
    cells_theta, cells_radius, cells_axial = density.shape
    shape = (cells_radius, cells_axial)
    rows = lax.broadcasted_iota(jnp.int32, shape, 0)
    lanes = lax.broadcasted_iota(jnp.int32, shape, 1)
    segment = n_theta // BURNERS
    part = min(segment, cells_theta)
    zero = jnp.zeros(shape, F32)

    def at(t):
        if t < 0 or t >= cells_theta:
            return zero, zero
        rho = density[t]
        return rho, rho * swirl[t]

    window = [at(-1), at(0)]
    for t in range(cells_theta):
        window.append(at(t + 1))
        (rho_down, flux_down), (rho, _), (rho_up, flux_up) = window
        window = window[1:]
        if t % part == 0:
            burner = (sector * cells_theta + t) // segment
            start = burner * segment + mouth_azimuth[burner] - sector * cells_theta
            radius = mouth_radius[burner] - radial * cells_radius
            mouth = ((rows >= radius) & (rows < radius + MOUTH)).astype(F32)
            mouth = mouth * (inflow_rate / time_step)
        gain = mouth * ((start <= t) & (t < start + MOUTH)).astype(F32)
        r_up = jnp.where(rows == cells_radius - 1, 0.0, pltpu.roll(rho, cells_radius - 1, 0))
        r_down = jnp.where(rows == 0, 0.0, pltpu.roll(rho, 1, 0))
        z_up = jnp.where(lanes == cells_axial - 1, 0.0, pltpu.roll(rho, cells_axial - 1, 1))
        z_down = jnp.where(lanes == 0, 0.0, pltpu.roll(rho, 1, 1))
        twice = 2.0 * rho
        laplace = (rho_up + rho_down - twice) + (r_up + r_down - twice) + (z_up + z_down - twice)
        forcing[t] = -0.5 * (flux_up - flux_down) + diffusion * laplace + gain * (1.0 - rho)

    total = None
    for r in range(cells_radius):
        rho = density[:, r, :]
        term = heat_rate[:, r, :] * rho * rho
        total = term if total is None else total + term
    heat[...] = total


def own_basis(basis, own, begin, each):
    sectors = lax.axis_size("sector")
    sector = lax.axis_index("sector")
    rows = [
        basis[pl.ds(pl.multiple_of((sector ^ k) * own + begin, 8), each), :]
        for k in range(sectors)
    ]
    return jnp.concatenate(rows, 0)


def sine_modes(basis, fields):
    high, low = split(basis)
    count = high.shape[0]
    left = jnp.concatenate(
        [jnp.concatenate([high, high], 1), jnp.concatenate([low, jnp.zeros_like(low)], 1)], 0
    )
    right = jnp.concatenate([jnp.concatenate(split(field), 1) for field in fields], 0)
    out = lax.dot_general(left, right, (NT, ((), ())), preferred_element_type=F32)
    return out[:count] + out[count:]


def spread(slots, forcing, basis, own, begin, each):
    cells_theta, cells_radius, _ = forcing.shape
    mine = own_basis(basis, own, begin, each)
    for r in range(0, cells_radius, 2):
        modes = sine_modes(mine, [forcing[:, r + i, :] for i in range(2)])
        for i in range(2):
            lane = slice(i * cells_theta, (i + 1) * cells_theta)
            for k, slot in enumerate(slots):
                slot[(r + i) * each : (r + i + 1) * each, :] = modes[
                    k * each : (k + 1) * each, lane
                ]


def first_kernel(
    each, n_radius, partial, heat, acoustic, above, below, inner, outer, basis, forcing, state,
    *slots
):
    radials = lax.axis_size("radial")
    radial = lax.axis_index("radial")
    cells_theta, cells_radius, cells_axial = partial.shape
    shape = (cells_radius, cells_axial)
    sectors = len(slots)
    own = cells_axial // sectors
    columns = cells_radius * each
    forcing[...] = partial[...]
    rho, flux = slice(0, cells_radius), slice(cells_radius, 2 * cells_radius)
    forcing[0] = forcing[0] + (0.5 * below[flux] + diffusion * below[rho])
    forcing[cells_theta - 1] = forcing[cells_theta - 1] + (
        diffusion * above[rho] - 0.5 * above[flux]
    )
    inside = diffusion * (radial > 0).astype(F32)
    outside = diffusion * (radial < radials - 1).astype(F32)
    forcing[:, 0, :] = forcing[:, 0, :] + inside * inner[...]
    forcing[:, cells_radius - 1, :] = forcing[:, cells_radius - 1, :] + outside * outer[...]
    spread(slots, forcing, basis, own, 0, each)

    skip = 2 * cells_radius
    share = (radial == 0).astype(F32)

    def extended(k):
        rows = slice(skip + k * EDGE, skip + (k + 1) * EDGE)
        middle = acoustic[k] if k < 3 else heat[...]
        return jnp.concatenate([below[rows], middle, above[rows]], 0)

    press, along, axial = extended(0) * share, extended(1) * share, extended(2) * share
    warm = extended(3) * (heat_coupling / n_radius)
    count = press.shape[0]
    lanes = lax.broadcasted_iota(jnp.int32, press.shape, 1)
    for _ in range(SUBSTEPS):
        press_up = pltpu.roll(press, count - 1, 0)
        press_axial = jnp.where(lanes == cells_axial - 1, 0.0, pltpu.roll(press, cells_axial - 1, 1))
        along = along - wave_speed * (press_up - press)
        axial = axial - wave_speed * (press_axial - press)
        along_down = pltpu.roll(along, 1, 0)
        axial_down = jnp.where(lanes == 0, 0.0, pltpu.roll(axial, 1, 1))
        press = press - wave_speed * ((along - along_down) + (axial - axial_down)) + warm
    middle = slice(EDGE, EDGE + cells_theta)
    state[0] = press[middle]
    state[1] = along[middle]
    state[2] = axial[middle]
    modes = sine_modes(own_basis(basis, own, 0, own), [feedback * press[middle]])
    for k, slot in enumerate(slots):
        slot[columns : columns + own, :] = modes[k * own : (k + 1) * own]


def next_kernel(chunk, each, forcing, basis, *slots):
    own = forcing.shape[2] // len(slots)
    spread(slots, forcing, basis, own, chunk * each, each)


def forward_kernel(edge, columns, sectors, *refs):
    received, refs = refs[:sectors], refs[sectors:]
    tables, refs = refs[:6], refs[6:]
    outs, pieces = refs[:-1], refs[-1]
    modes, first, last = outs[:3]
    sector = lax.axis_index("sector")
    for k in range(sectors):
        pieces[sector ^ k] = received[k][...]
    quarter, half = sectors // 4, sectors // 2

    def joined(parts):
        return jnp.concatenate(parts, 1) if len(parts) > 1 else parts[0]

    values = [pieces[s] for s in range(sectors)]
    even = [values[s] + values[s + half] for s in range(half)]
    odd = [values[s] - values[s + half] for s in range(half)]
    both = [even[s] + even[s + quarter] for s in range(quarter)]
    apart = [even[s] - even[s + quarter] for s in range(quarter)]
    at = 0
    for i, parts in enumerate((both, apart, odd)):
        wh, wl = tables[2 * i : 2 * i + 2]
        lane = slice(at, at + wh.shape[1])
        out = product(split(joined(parts)), (wh[...], wl[...]), NN)
        modes[:, lane] = out[:columns]
        first[:, lane] = out[:edge]
        last[:, lane] = out[columns - edge : columns]
        if len(outs) > 3:
            outs[3][:, lane] = out[columns:]
        at += wh.shape[1]


def solve_kernel(
    chunk, each, modes, inner, outer, wave, inverse, scaled, axial, w0h, w0l, w1h, w1l, w2h,
    w2l, *refs
):
    slots, solved, pieces = refs[:-2], refs[-2], refs[-1]
    radials = lax.axis_size("radial")
    radial = lax.axis_index("radial")
    sector = lax.axis_index("sector")
    columns, n_theta = modes.shape
    cells_radius = columns // each
    has_inner = (radial > 0).astype(F32)
    has_outer = (radial < radials - 1).astype(F32)
    eigen = axial[sector][chunk * each : (chunk + 1) * each, :]
    step = eigen.shape[1]
    total = cells_radius + 2 * HALO
    for block in range(n_theta // step):
        lane = slice(block * step, (block + 1) * step)
        inv = jnp.broadcast_to(inverse[:, lane], (each, step))
        inv_inner, inv_outer = inv * has_inner, inv * has_outer
        last_scale = jnp.broadcast_to(scaled[:, lane], (each, step))
        add = wave[chunk * each : (chunk + 1) * each, lane]

        def row_of(i):
            if i < HALO:
                return inner[i * each : (i + 1) * each, lane]
            i -= HALO
            if i < cells_radius:
                return modes[i * each : (i + 1) * each, lane]
            i -= cells_radius
            return outer[i * each : (i + 1) * each, lane]

        def scale_of(i):
            if i < HALO:
                return inv_inner
            return inv if i < HALO + cells_radius else inv_outer

        right = [row_of(i) + add for i in range(total)]
        x = [right[i] * scale_of(i) for i in range(total)]
        for sweep in range(1, SWEEPS):
            fresh = [None] * total
            for i in range(sweep, total - sweep):
                scale = last_scale if sweep == SWEEPS - 1 else scale_of(i)
                fresh[i] = (right[i] + (x[i + 1] + x[i - 1]) + eigen * x[i]) * scale
            x = fresh
        for i in range(cells_radius):
            solved[i * each : (i + 1) * each, lane] = x[i + HALO]

    sectors = len(slots)
    width = pieces.shape[2]
    n0, n1 = w0h.shape[1], w1h.shape[1]
    both = product(split(solved[:, :n0]), (w0h[...], w0l[...]), NT)
    apart = product(split(solved[:, n0 : n0 + n1]), (w1h[...], w1l[...]), NT)
    odd = product(split(solved[:, n0 + n1 :]), (w2h[...], w2l[...]), NT)
    even = jnp.concatenate([both + apart, both - apart], 1)
    for s in range(sectors // 2):
        lane = slice(s * width, (s + 1) * width)
        pieces[s] = even[:, lane] + odd[:, lane]
        pieces[s + sectors // 2] = even[:, lane] - odd[:, lane]
    for k, slot in enumerate(slots):
        slot[...] = pieces[sector ^ k]


def pressure_kernel(chunks, *refs):
    received, (basis, pressure) = refs[:-2], refs[-2:]
    sectors = len(received) // chunks
    cells_radius = pressure.shape[1]
    each = received[0].shape[0] // cells_radius
    high, low = split(own_basis(basis, each * chunks, 0, each * chunks))
    right = jnp.concatenate(
        [jnp.concatenate([high, low], 1), jnp.concatenate([high, jnp.zeros_like(low)], 1)], 0
    )
    cells_axial = high.shape[1]
    for r in range(cells_radius):
        rows = [
            received[c * sectors + k][r * each : (r + 1) * each, :]
            for k in range(sectors)
            for c in range(chunks)
        ]
        modes = jnp.concatenate(rows, 0)
        left = jnp.concatenate(split(modes.T), 1)
        out = lax.dot_general(left, right, (NN, ((), ())), preferred_element_type=F32)
        pressure[:, r, :] = out[:, :cells_axial] + out[:, cells_axial:]


def call(kernel, outs, ins, scratch=(), **more):
    moved = sum(math.prod(o.shape) * 4 for o in outs)
    return pl.pallas_call(
        kernel,
        out_shape=outs,
        in_specs=ins,
        out_specs=[VMEM] * len(outs),
        scratch_shapes=list(scratch),
        cost_estimate=pl.CostEstimate(flops=0, bytes_accessed=3 * moved, transcendentals=0),
        compiler_params=pltpu.CompilerParams(vmem_limit_bytes=24 * 1024 * 1024),
        **more,
    )


def shape(*dims):
    return jax.ShapeDtypeStruct(dims, F32)


def shifted(value, axis, steps):
    count = lax.axis_size(axis)
    return lax.ppermute(value, axis, [(i, (i + steps) % count) for i in range(count)])


def swapped(value, axis, bits):
    return lax.ppermute(value, axis, [(i, i ^ bits) for i in range(lax.axis_size(axis))])


def summed(value, axis):
    step = 1
    while step < lax.axis_size(axis):
        value = value + swapped(value, axis, step)
        step *= 2
    return value


def exchanged(slots):
    return [slots[0]] + [swapped(slots[k], "sector", k) for k in range(1, len(slots))]


def shards(density, swirl, heat_rate, acoustic, mode_impedance, mouth_azimuth, mouth_radius):
    sectors = lax.axis_size("sector")
    radials = lax.axis_size("radial")
    cells_theta, cells_radius, cells_axial = density.shape
    n_theta = cells_theta * sectors
    n_radius = cells_radius * radials
    own = cells_axial // sectors
    chunks = max(1, min(2, own // 8))
    each = own // chunks
    columns = cells_radius * each
    edge = HALO * each

    basis, eigen = axial_tables(cells_axial)
    basis = jnp.asarray(basis.astype(np.float32))
    eigen = jnp.asarray(
        np.broadcast_to(eigen.reshape(sectors, own, 1), (sectors, own, 128)).astype(np.float32)
    )
    tables = []
    for table in azimuth_tables(n_theta):
        tables += [jnp.asarray(t) for t in halves(table)]
    fixed, weight = diagonal_tables(n_theta)
    inverse = (1.0 / (jnp.asarray(fixed) + mode_rows(mode_impedance)))[None, :]
    scaled = inverse * jnp.asarray(weight)[None, :]

    packed = 2 * cells_radius + 4 * EDGE
    row_block = shape(cells_theta, cells_axial)
    first, last, head, tail = call(
        edges_kernel,
        [row_block] * 2 + [shape(packed, cells_axial)] * 2,
        [HBM] * 4,
        [
            pltpu.VMEM((2, EDGE, cells_radius, cells_axial), F32),
            pltpu.VMEM((2, EDGE, cells_radius, cells_axial), F32),
            pltpu.VMEM((2, 1, cells_radius, cells_axial), F32),
            pltpu.VMEM((2, 3, EDGE, cells_axial), F32),
            pltpu.SemaphoreType.DMA((10,)),
        ],
    )(density, swirl, heat_rate, acoustic)
    above = shifted(head, "sector", -1)
    below = shifted(tail, "sector", 1)
    outer = shifted(first, "radial", -1)
    inner = shifted(last, "radial", 1)

    partial, heat = call(
        lambda *refs: flow_kernel(n_theta, *refs),
        [shape(*density.shape), row_block],
        [SMEM] * 2 + [VMEM] * 3,
    )(mouth_azimuth, mouth_radius, density, swirl, heat_rate)

    forcing, state, *slots = call(
        lambda *refs: first_kernel(each, n_radius, *refs),
        [shape(*density.shape), shape(*acoustic.shape)]
        + [shape(columns + own, cells_theta)] * sectors,
        [VMEM] * 8,
    )(partial, heat, acoustic, above, below, inner, outer, basis)
    received = [exchanged(slots)]
    for c in range(1, chunks):
        slots = call(
            lambda *refs: next_kernel(c, each, *refs),
            [shape(columns, cells_theta)] * sectors,
            [VMEM] * 2,
        )(forcing, basis)
        received.append(exchanged(slots))
    density_next = density + time_step * forcing

    modes, wave = [], None
    for c in range(chunks):
        count = received[c][0].shape[0]
        outs = [shape(columns, n_theta), shape(edge, n_theta), shape(edge, n_theta)]
        if c == 0:
            outs.append(shape(own, n_theta))
        c_modes, c_first, c_last, *waves = call(
            lambda *refs: forward_kernel(edge, columns, sectors, *refs),
            outs,
            [VMEM] * (sectors + 6),
            [pltpu.VMEM((sectors, count, cells_theta), F32)],
        )(*received[c], *tables)
        if c == 0:
            wave = summed(waves[0], "radial")
        modes.append((c_modes, shifted(c_last, "radial", 1), shifted(c_first, "radial", -1)))

    results = []
    for c in range(chunks):
        slots = call(
            lambda *refs: solve_kernel(c, each, *refs),
            [shape(columns, cells_theta)] * sectors,
            [VMEM] * 13,
            [pltpu.VMEM((columns, n_theta), F32), pltpu.VMEM((sectors, columns, cells_theta), F32)],
        )(*modes[c], wave, inverse, scaled, eigen, *tables)
        results += exchanged(slots)
    acoustic_next = summed(state, "radial")

    (pressure,) = call(
        lambda *refs: pressure_kernel(chunks, *refs),
        [shape(*density.shape)],
        [VMEM] * (chunks * sectors + 1),
    )(*results, basis)
    return density_next, pressure, acoustic_next


def solution(mesh):
    return jax.shard_map(
        shards,
        mesh=mesh,
        in_specs=(
            P("sector", "radial", None),
            P("sector", "radial", None),
            P("sector", "radial", None),
            P(None, "sector", None),
            P(),
            P(),
            P(),
        ),
        out_specs=(
            P("sector", "radial", None),
            P("sector", "radial", None),
            P(None, "sector", None),
        ),
        check_vma=False,
    )
```

```python
import math

import jax
import jax.numpy as jnp
import numpy as np
from jax import lax
from jax.experimental import pallas as pl
from jax.experimental.pallas import tpu as pltpu
from jax.sharding import PartitionSpec as P

BURNERS = 16
MOUTH = 8
SWEEPS = 4
SUBSTEPS = 8

time_step = 0.2
diffusion = 0.05
inflow_rate = 0.5
wave_speed = 0.5
heat_coupling = 0.5
feedback = 0.5

F32 = jnp.float32
BF16 = jnp.bfloat16
HALO = SWEEPS - 1
EDGE = 8
VMEM = pl.BlockSpec(memory_space=pltpu.VMEM)
SMEM = pl.BlockSpec(memory_space=pltpu.SMEM)
HBM = pl.BlockSpec(memory_space=pltpu.HBM)


def halves(table):
    high = table.astype(BF16)
    low = (table - high.astype(np.float64)).astype(BF16)
    return high, low


def axial_tables(cells):
    index = np.arange(1, cells + 1, dtype=np.float64)
    basis = math.sqrt(2.0 / (cells + 1)) * np.sin(
        np.pi * ((index[:, None] * index[None, :]) % (2 * (cells + 1))) / (cells + 1)
    )
    return basis, 2.0 * np.cos(np.pi * index / (cells + 1))


def mode_classes(n_theta):
    half = n_theta // 2
    multiples = np.arange(0, half, 4)
    first = (
        np.concatenate([multiples, [half], multiples[1:]]),
        np.concatenate([np.zeros(len(multiples) + 1), np.ones(len(multiples) - 1)]),
    )
    twos = np.arange(2, half, 4)
    second = (np.concatenate([twos, twos]), np.repeat([0, 1], len(twos)))
    ones, threes = np.arange(1, half, 4), np.arange(3, half, 4)
    third = (np.concatenate([ones, threes, ones, threes]), np.repeat([0, 1], half // 2))
    return first, second, third


def azimuth_tables(n_theta):
    bases = []
    for (order, odd), rows in zip(mode_classes(n_theta), (n_theta // 4, n_theta // 4, n_theta // 2)):
        phase = (np.arange(rows)[:, None] * order[None, :].astype(np.int64)) % n_theta
        angle = phase * (2.0 * np.pi / n_theta)
        bases.append(np.where(odd[None, :] == 0, np.cos(angle), np.sin(angle)))
    return bases


def diagonal_tables(n_theta):
    half = n_theta // 2
    order = np.concatenate([part[0] for part in mode_classes(n_theta)])
    shifted = 2.0 - 2.0 * np.cos(order * (2.0 * np.pi / n_theta))
    weight = np.where((order == 0) | (order == half), 1.0, 2.0) / n_theta
    return (4.0 + shifted).astype(np.float32), weight.astype(np.float32)


def mode_rows(impedance):
    half = impedance.shape[0] - 1
    by_four = impedance[:half].reshape(half // 4, 4).T
    q0, q1, q2, q3 = by_four[0], by_four[1], by_four[2], by_four[3]
    first = jnp.concatenate([impedance[half:], q0[1:]])
    return jnp.concatenate([q0, first, q2, q2, q1, q3, q1, q3])


def split(value):
    high = value.astype(BF16)
    return high, (value - high.astype(F32)).astype(BF16)


def product(left, right, dims):
    def one(a, b):
        return lax.dot_general(a, b, (dims, ((), ())), preferred_element_type=F32)

    return one(left[0], right[0]) + (one(left[1], right[0]) + one(left[0], right[1]))


NN = ((1,), (0,))
NT = ((1,), (1,))


def edges_kernel(
    density, swirl, heat_rate, acoustic, radial_pair, radial_link, sector_pair, sector_link, rho,
    rate, spin, wave, rim, sems
):
    cells_theta, cells_radius, _ = density.shape
    radial_odd = lax.axis_index("radial") % 2
    sector_odd = lax.axis_index("sector") % 2
    copies = []

    def fetch(source, target):
        copy = pltpu.make_async_copy(source, target, sems.at[len(copies)])
        copy.start()
        copies.append(copy)

    for side, begin, row in ((0, 0, 0), (1, cells_theta - EDGE, cells_theta - 1)):
        fetch(density.at[pl.ds(begin, EDGE)], rho.at[side])
        fetch(heat_rate.at[pl.ds(begin, EDGE)], rate.at[side])
        fetch(swirl.at[pl.ds(row, 1)], spin.at[side])
        fetch(acoustic.at[:, pl.ds(begin, EDGE)], wave.at[side])
    fetch(density.at[:, 0, :], rim.at[0])
    fetch(density.at[:, cells_radius - 1, :], rim.at[1])
    for copy in copies:
        copy.wait()
    radial_pair[...] = rim[1 - radial_odd]
    radial_link[...] = rim[radial_odd]
    for out, side in ((sector_pair, 1 - sector_odd), (sector_link, sector_odd)):
        edge = jnp.where(side == 0, rho[0, 0], rho[1, EDGE - 1])
        out[0:cells_radius] = edge
        out[cells_radius : 2 * cells_radius] = edge * spin[side, 0]
        at = 2 * cells_radius
        for k in range(3):
            out[at : at + EDGE] = wave[side, k]
            at += EDGE
        heat = jnp.sum(rate[side] * rho[side] * rho[side], axis=1)
        out[at : at + EDGE] = heat


PIECES = 4


def flow_kernel(
    n_theta, mouth_azimuth, mouth_radius, density_in, swirl_in, heat_rate_in, forcing, heat,
    density, swirl, heat_rate, sems
):
    sector = lax.axis_index("sector")
    radial = lax.axis_index("radial")
    cells_theta, cells_radius, cells_axial = density.shape
    shape = (cells_radius, cells_axial)
    rows = lax.broadcasted_iota(jnp.int32, shape, 0)
    lanes = lax.broadcasted_iota(jnp.int32, shape, 1)
    segment = n_theta // BURNERS
    part = min(segment, cells_theta)
    zero = jnp.zeros(shape, F32)
    piece = cells_theta // PIECES
    copies = {}
    for i in range(PIECES):
        rows_here = pl.ds(i * piece, piece)
        for k, (source, target) in enumerate(
            ((density_in, density), (swirl_in, swirl), (heat_rate_in, heat_rate))
        ):
            copies[k, i] = pltpu.make_async_copy(
                source.at[rows_here], target.at[rows_here], sems.at[k, i]
            )
            copies[k, i].start()

    def at(t):
        if t < 0 or t >= cells_theta:
            return zero, zero
        if t % piece == 0:
            copies[0, t // piece].wait()
            copies[1, t // piece].wait()
        rho = density[t]
        return rho, rho * swirl[t]

    window = [at(-1), at(0)]
    for t in range(cells_theta):
        window.append(at(t + 1))
        (rho_down, flux_down), (rho, _), (rho_up, flux_up) = window
        window = window[1:]
        if t % part == 0:
            burner = (sector * cells_theta + t) // segment
            start = burner * segment + mouth_azimuth[burner] - sector * cells_theta
            radius = mouth_radius[burner] - radial * cells_radius
            mouth = ((rows >= radius) & (rows < radius + MOUTH)).astype(F32)
            mouth = mouth * (inflow_rate / time_step)
        gain = mouth * ((start <= t) & (t < start + MOUTH)).astype(F32)
        r_up = jnp.where(rows == cells_radius - 1, 0.0, pltpu.roll(rho, cells_radius - 1, 0))
        r_down = jnp.where(rows == 0, 0.0, pltpu.roll(rho, 1, 0))
        z_up = jnp.where(lanes == cells_axial - 1, 0.0, pltpu.roll(rho, cells_axial - 1, 1))
        z_down = jnp.where(lanes == 0, 0.0, pltpu.roll(rho, 1, 1))
        twice = 2.0 * rho
        laplace = (rho_up + rho_down - twice) + (r_up + r_down - twice) + (z_up + z_down - twice)
        forcing[t] = -0.5 * (flux_up - flux_down) + diffusion * laplace + gain * (1.0 - rho)

    for i in range(PIECES):
        copies[2, i].wait()
    total = None
    for r in range(cells_radius):
        rho = density[:, r, :]
        term = heat_rate[:, r, :] * rho * rho
        total = term if total is None else total + term
    heat[...] = total


def sine_modes(basis, fields):
    high, low = split(basis)
    count = high.shape[0]
    left = jnp.concatenate(
        [jnp.concatenate([high, high], 1), jnp.concatenate([low, jnp.zeros_like(low)], 1)], 0
    )
    right = jnp.concatenate([jnp.concatenate(split(field), 1) for field in fields], 0)
    out = lax.dot_general(left, right, (NT, ((), ())), preferred_element_type=F32)
    return out[:count] + out[count:]


def spread(send, forcing, basis, own, begin, each):
    cells_theta, cells_radius, _ = forcing.shape
    sectors = send.shape[0]
    mine = [basis[d * own + begin : d * own + begin + each, :] for d in range(sectors)]
    mine = jnp.concatenate(mine, 0)
    for r in range(0, cells_radius, 2):
        modes = sine_modes(mine, [forcing[:, r + i, :] for i in range(2)])
        for i in range(2):
            lane = slice(i * cells_theta, (i + 1) * cells_theta)
            for d in range(sectors):
                send[d, (r + i) * each : (r + i + 1) * each, :] = modes[
                    d * each : (d + 1) * each, lane
                ]


def first_kernel(
    each, n_radius, partial, heat, acoustic, radial_pair, radial_link, sector_pair, sector_link,
    basis, forcing, state, send
):
    radials = lax.axis_size("radial")
    radial = lax.axis_index("radial")
    cells_theta, cells_radius, cells_axial = partial.shape
    shape = (cells_radius, cells_axial)
    sectors = send.shape[0]
    own = cells_axial // sectors
    columns = cells_radius * each
    sector_odd = lax.axis_index("sector") % 2 == 1
    radial_odd = radial % 2 == 1
    above = jnp.where(sector_odd, sector_link[...], sector_pair[...])
    below = jnp.where(sector_odd, sector_pair[...], sector_link[...])
    outer = jnp.where(radial_odd, radial_link[...], radial_pair[...])
    inner = jnp.where(radial_odd, radial_pair[...], radial_link[...])
    forcing[...] = partial[...]
    rho, flux = slice(0, cells_radius), slice(cells_radius, 2 * cells_radius)
    forcing[0] = forcing[0] + (0.5 * below[flux] + diffusion * below[rho])
    forcing[cells_theta - 1] = forcing[cells_theta - 1] + (
        diffusion * above[rho] - 0.5 * above[flux]
    )
    inside = diffusion * (radial > 0).astype(F32)
    outside = diffusion * (radial < radials - 1).astype(F32)
    forcing[:, 0, :] = forcing[:, 0, :] + inside * inner
    forcing[:, cells_radius - 1, :] = forcing[:, cells_radius - 1, :] + outside * outer
    spread(send, forcing, basis, own, 0, each)

    skip = 2 * cells_radius
    share = (radial == 0).astype(F32)

    def extended(k):
        rows = slice(skip + k * EDGE, skip + (k + 1) * EDGE)
        middle = acoustic[k] if k < 3 else heat[...]
        return jnp.concatenate([below[rows], middle, above[rows]], 0)

    press, along, axial = extended(0) * share, extended(1) * share, extended(2) * share
    warm = extended(3) * (heat_coupling / n_radius)
    count = press.shape[0]
    lanes = lax.broadcasted_iota(jnp.int32, press.shape, 1)
    for _ in range(SUBSTEPS):
        press_up = pltpu.roll(press, count - 1, 0)
        press_axial = jnp.where(lanes == cells_axial - 1, 0.0, pltpu.roll(press, cells_axial - 1, 1))
        along = along - wave_speed * (press_up - press)
        axial = axial - wave_speed * (press_axial - press)
        along_down = pltpu.roll(along, 1, 0)
        axial_down = jnp.where(lanes == 0, 0.0, pltpu.roll(axial, 1, 1))
        press = press - wave_speed * ((along - along_down) + (axial - axial_down)) + warm
    middle = slice(EDGE, EDGE + cells_theta)
    state[0] = press[middle]
    state[1] = along[middle]
    state[2] = axial[middle]
    modes = sine_modes(basis[...], [feedback * press[middle]])
    for d in range(sectors):
        send[d, columns : columns + own, :] = modes[d * own : (d + 1) * own]


def next_kernel(chunk, each, forcing, basis, send):
    own = forcing.shape[2] // send.shape[0]
    spread(send, forcing, basis, own, chunk * each, each)


def forward_kernel(edge, columns, received, *refs):
    tables, outs = refs[:6], refs[6:]
    modes, pair, link = outs[:3]
    sectors = received.shape[0]
    radial_odd = lax.axis_index("radial") % 2 == 1
    quarter, half = sectors // 4, sectors // 2

    def joined(parts):
        return jnp.concatenate(parts, 1) if len(parts) > 1 else parts[0]

    values = [received[s] for s in range(sectors)]
    even = [values[s] + values[s + half] for s in range(half)]
    odd = [values[s] - values[s + half] for s in range(half)]
    both = [even[s] + even[s + quarter] for s in range(quarter)]
    apart = [even[s] - even[s + quarter] for s in range(quarter)]
    at = 0
    for i, parts in enumerate((both, apart, odd)):
        wh, wl = tables[2 * i : 2 * i + 2]
        lane = slice(at, at + wh.shape[1])
        out = product(split(joined(parts)), (wh[...], wl[...]), NN)
        modes[:, lane] = out[:columns]
        first, last = out[:edge], out[columns - edge : columns]
        pair[:, lane] = jnp.where(radial_odd, first, last)
        link[:, lane] = jnp.where(radial_odd, last, first)
        if len(outs) > 3:
            outs[3][:, lane] = out[columns:]
        at += wh.shape[1]


def solve_kernel(
    chunk, each, modes, pair, link, wave, inverse, scaled, axial, w0h, w0l, w1h, w1l, w2h, w2l,
    send, solved
):
    radials = lax.axis_size("radial")
    radial = lax.axis_index("radial")
    sector = lax.axis_index("sector")
    columns, n_theta = modes.shape
    cells_radius = columns // each
    has_inner = (radial > 0).astype(F32)
    has_outer = (radial < radials - 1).astype(F32)
    radial_odd = radial % 2 == 1
    eigen = axial[sector][chunk * each : (chunk + 1) * each, :]
    step = eigen.shape[1]
    total = cells_radius + 2 * HALO
    for block in range(n_theta // step):
        lane = slice(block * step, (block + 1) * step)
        inv = jnp.broadcast_to(inverse[:, lane], (each, step))
        inv_inner, inv_outer = inv * has_inner, inv * has_outer
        last_scale = jnp.broadcast_to(scaled[:, lane], (each, step))
        add = wave[chunk * each : (chunk + 1) * each, lane]

        def row_of(i):
            i -= HALO
            if 0 <= i < cells_radius:
                return modes[i * each : (i + 1) * each, lane]
            odd_one, even_one = (pair, link) if i < 0 else (link, pair)
            i = i + HALO if i < 0 else i - cells_radius
            rows = slice(i * each, (i + 1) * each)
            return jnp.where(radial_odd, odd_one[rows, lane], even_one[rows, lane])

        def scale_of(i):
            if i < HALO:
                return inv_inner
            return inv if i < HALO + cells_radius else inv_outer

        right = [row_of(i) + add for i in range(total)]
        x = [right[i] * scale_of(i) for i in range(total)]
        for sweep in range(1, SWEEPS):
            fresh = [None] * total
            for i in range(sweep, total - sweep):
                scale = last_scale if sweep == SWEEPS - 1 else scale_of(i)
                fresh[i] = (right[i] + (x[i + 1] + x[i - 1]) + eigen * x[i]) * scale
            x = fresh
        for i in range(cells_radius):
            solved[i * each : (i + 1) * each, lane] = x[i + HALO]

    sectors, _, width = send.shape
    n0, n1 = w0h.shape[1], w1h.shape[1]
    both = product(split(solved[:, :n0]), (w0h[...], w0l[...]), NT)
    apart = product(split(solved[:, n0 : n0 + n1]), (w1h[...], w1l[...]), NT)
    odd = product(split(solved[:, n0 + n1 :]), (w2h[...], w2l[...]), NT)
    even = jnp.concatenate([both + apart, both - apart], 1)
    for s in range(sectors // 2):
        lane = slice(s * width, (s + 1) * width)
        send[s] = even[:, lane] + odd[:, lane]
        send[s + sectors // 2] = even[:, lane] - odd[:, lane]


def pressure_kernel(chunks, *refs):
    received, (basis, pressure) = refs[:-2], refs[-2:]
    sectors = received[0].shape[0]
    cells_radius = pressure.shape[1]
    each = received[0].shape[1] // cells_radius
    high, low = split(basis[...])
    right = jnp.concatenate(
        [jnp.concatenate([high, low], 1), jnp.concatenate([high, jnp.zeros_like(low)], 1)], 0
    )
    cells_axial = high.shape[1]
    for r in range(cells_radius):
        rows = [
            received[c][d, r * each : (r + 1) * each, :]
            for d in range(sectors)
            for c in range(chunks)
        ]
        modes = jnp.concatenate(rows, 0)
        left = jnp.concatenate(split(modes.T), 1)
        out = lax.dot_general(left, right, (NN, ((), ())), preferred_element_type=F32)
        pressure[:, r, :] = out[:, :cells_axial] + out[:, cells_axial:]


def call(kernel, outs, ins, scratch=(), limit=24 * 1024 * 1024, **more):
    moved = sum(math.prod(o.shape) * 4 for o in outs)
    return pl.pallas_call(
        kernel,
        out_shape=outs,
        in_specs=ins,
        out_specs=[VMEM] * len(outs),
        scratch_shapes=list(scratch),
        cost_estimate=pl.CostEstimate(flops=0, bytes_accessed=3 * moved, transcendentals=0),
        compiler_params=pltpu.CompilerParams(vmem_limit_bytes=limit),
        **more,
    )


def shape(*dims):
    return jax.ShapeDtypeStruct(dims, F32)


def paired(pair, link, axis, closed):
    count = lax.axis_size(axis)
    first = [(i, i ^ 1) for i in range(count)]
    second = [(i, (i + 1) % count) for i in range(1, count if closed else count - 1, 2)]
    second += [(j, i) for i, j in second]
    return lax.ppermute(pair, axis, first), lax.ppermute(link, axis, second)


def swapped(value, axis, bits):
    return lax.ppermute(value, axis, [(i, i ^ bits) for i in range(lax.axis_size(axis))])


def summed(value, axis):
    step = 1
    while step < lax.axis_size(axis):
        value = value + swapped(value, axis, step)
        step *= 2
    return value


def exchanged(value):
    return lax.all_to_all(value, "sector", split_axis=0, concat_axis=0, tiled=True)


def shards(density, swirl, heat_rate, acoustic, mode_impedance, mouth_azimuth, mouth_radius):
    sectors = lax.axis_size("sector")
    radials = lax.axis_size("radial")
    cells_theta, cells_radius, cells_axial = density.shape
    n_theta = cells_theta * sectors
    n_radius = cells_radius * radials
    own = cells_axial // sectors
    chunks = max(1, min(2, own // 8))
    each = own // chunks
    columns = cells_radius * each
    edge = HALO * each

    basis, eigen = axial_tables(cells_axial)
    basis = jnp.asarray(basis.astype(np.float32))
    eigen = jnp.asarray(
        np.broadcast_to(eigen.reshape(sectors, own, 1), (sectors, own, 128)).astype(np.float32)
    )
    tables = []
    for table in azimuth_tables(n_theta):
        tables += [jnp.asarray(t) for t in halves(table)]
    fixed, weight = diagonal_tables(n_theta)
    inverse = (1.0 / (jnp.asarray(fixed) + mode_rows(mode_impedance)))[None, :]
    scaled = inverse * jnp.asarray(weight)[None, :]

    packed = 2 * cells_radius + 4 * EDGE
    row_block = shape(cells_theta, cells_axial)
    edges = call(
        edges_kernel,
        [row_block] * 2 + [shape(packed, cells_axial)] * 2,
        [HBM] * 4,
        [
            pltpu.VMEM((2, EDGE, cells_radius, cells_axial), F32),
            pltpu.VMEM((2, EDGE, cells_radius, cells_axial), F32),
            pltpu.VMEM((2, 1, cells_radius, cells_axial), F32),
            pltpu.VMEM((2, 3, EDGE, cells_axial), F32),
            pltpu.VMEM((2, cells_theta, cells_axial), F32),
            pltpu.SemaphoreType.DMA((10,)),
        ],
        limit=None,
    )(density, swirl, heat_rate, acoustic)
    sector_halo = paired(edges[2], edges[3], "sector", True)
    radial_halo = paired(edges[0], edges[1], "radial", False)

    partial, heat = call(
        lambda *refs: flow_kernel(n_theta, *refs),
        [shape(*density.shape), row_block],
        [SMEM] * 2 + [HBM] * 3,
        [pltpu.VMEM(density.shape, F32)] * 3 + [pltpu.SemaphoreType.DMA((3, PIECES))],
        limit=None,
    )(mouth_azimuth, mouth_radius, density, swirl, heat_rate)

    forcing, state, send = call(
        lambda *refs: first_kernel(each, n_radius, *refs),
        [shape(*density.shape), shape(*acoustic.shape), shape(sectors, columns + own, cells_theta)],
        [VMEM] * 8,
    )(partial, heat, acoustic, *radial_halo, *sector_halo, basis)
    received = [exchanged(send)]
    for c in range(1, chunks):
        (send,) = call(
            lambda *refs: next_kernel(c, each, *refs),
            [shape(sectors, columns, cells_theta)],
            [VMEM] * 2,
        )(forcing, basis)
        received.append(exchanged(send))
    density_next = density + time_step * forcing

    modes, wave = [], None
    for c in range(chunks):
        outs = [shape(columns, n_theta), shape(edge, n_theta), shape(edge, n_theta)]
        if c == 0:
            outs.append(shape(own, n_theta))
        c_modes, pair, link, *waves = call(
            lambda *refs: forward_kernel(edge, columns, *refs), outs, [VMEM] * 7
        )(received[c], *tables)
        if c == 0:
            wave = summed(waves[0], "radial")
        modes.append((c_modes, *paired(pair, link, "radial", False)))

    results = []
    for c in range(chunks):
        (send,) = call(
            lambda *refs: solve_kernel(c, each, *refs),
            [shape(sectors, columns, cells_theta)],
            [VMEM] * 13,
            [pltpu.VMEM((columns, n_theta), F32)],
        )(*modes[c], wave, inverse, scaled, eigen, *tables)
        results.append(exchanged(send))
    acoustic_next = summed(state, "radial")

    (pressure,) = call(
        lambda *refs: pressure_kernel(chunks, *refs),
        [shape(*density.shape)],
        [VMEM] * (chunks + 1),
    )(*results, basis)
    return density_next, pressure, acoustic_next


def solution(mesh):
    return jax.shard_map(
        shards,
        mesh=mesh,
        in_specs=(
            P("sector", "radial", None),
            P("sector", "radial", None),
            P("sector", "radial", None),
            P(None, "sector", None),
            P(),
            P(),
            P(),
        ),
        out_specs=(
            P("sector", "radial", None),
            P("sector", "radial", None),
            P(None, "sector", None),
        ),
        check_vma=False,
    )
```

```python
import math

import jax
import jax.numpy as jnp
import numpy as np
from jax import lax
from jax.experimental import pallas as pl
from jax.experimental.pallas import tpu as pltpu
from jax.sharding import PartitionSpec as P

BURNERS = 16
MOUTH = 8
SWEEPS = 4
SUBSTEPS = 8

time_step = 0.2
diffusion = 0.05
inflow_rate = 0.5
wave_speed = 0.5
heat_coupling = 0.5
feedback = 0.5

F32 = jnp.float32
BF16 = jnp.bfloat16
HALO = SWEEPS - 1
EDGE = 8
VMEM = pl.BlockSpec(memory_space=pltpu.VMEM)
SMEM = pl.BlockSpec(memory_space=pltpu.SMEM)
HBM = pl.BlockSpec(memory_space=pltpu.HBM)


def halves(table):
    high = table.astype(BF16)
    low = (table - high.astype(np.float64)).astype(BF16)
    return high, low


def axial_tables(cells):
    index = np.arange(1, cells + 1, dtype=np.float64)
    basis = math.sqrt(2.0 / (cells + 1)) * np.sin(
        np.pi * ((index[:, None] * index[None, :]) % (2 * (cells + 1))) / (cells + 1)
    )
    return basis, 2.0 * np.cos(np.pi * index / (cells + 1))


def mode_classes(n_theta):
    half = n_theta // 2
    multiples = np.arange(0, half, 4)
    first = (
        np.concatenate([multiples, [half], multiples[1:]]),
        np.concatenate([np.zeros(len(multiples) + 1), np.ones(len(multiples) - 1)]),
    )
    twos = np.arange(2, half, 4)
    second = (np.concatenate([twos, twos]), np.repeat([0, 1], len(twos)))
    ones, threes = np.arange(1, half, 4), np.arange(3, half, 4)
    third = (np.concatenate([ones, threes, ones, threes]), np.repeat([0, 1], half // 2))
    return first, second, third


def azimuth_tables(n_theta):
    bases = []
    for (order, odd), rows in zip(mode_classes(n_theta), (n_theta // 4, n_theta // 4, n_theta // 2)):
        phase = (np.arange(rows)[:, None] * order[None, :].astype(np.int64)) % n_theta
        angle = phase * (2.0 * np.pi / n_theta)
        bases.append(np.where(odd[None, :] == 0, np.cos(angle), np.sin(angle)))
    return bases


def diagonal_tables(n_theta):
    half = n_theta // 2
    order = np.concatenate([part[0] for part in mode_classes(n_theta)])
    shifted = 2.0 - 2.0 * np.cos(order * (2.0 * np.pi / n_theta))
    weight = np.where((order == 0) | (order == half), 1.0, 2.0) / n_theta
    return (4.0 + shifted).astype(np.float32), weight.astype(np.float32)


def mode_rows(impedance):
    half = impedance.shape[0] - 1
    by_four = impedance[:half].reshape(half // 4, 4).T
    q0, q1, q2, q3 = by_four[0], by_four[1], by_four[2], by_four[3]
    first = jnp.concatenate([impedance[half:], q0[1:]])
    return jnp.concatenate([q0, first, q2, q2, q1, q3, q1, q3])


def split(value):
    high = value.astype(BF16)
    return high, (value - high.astype(F32)).astype(BF16)


def product(left, right, dims):
    def one(a, b):
        return lax.dot_general(a, b, (dims, ((), ())), preferred_element_type=F32)

    return one(left[0], right[0]) + (one(left[1], right[0]) + one(left[0], right[1]))


NN = ((1,), (0,))
NT = ((1,), (1,))


def rim_kernel(density, pair, link, rim, sems):
    cells_radius = density.shape[1]
    odd = lax.axis_index("radial") % 2
    copies = [
        pltpu.make_async_copy(density.at[:, row, :], rim.at[side], sems.at[side])
        for side, row in ((0, 0), (1, cells_radius - 1))
    ]
    for copy in copies:
        copy.start()
    for copy in copies:
        copy.wait()
    pair[...] = rim[1 - odd]
    link[...] = rim[odd]


def pack_kernel(density, swirl, acoustic, heat, pair, link, rho, spin, wave, sems):
    cells_theta, cells_radius, _ = density.shape
    odd = lax.axis_index("sector") % 2
    copies = []

    def fetch(source, target):
        copy = pltpu.make_async_copy(source, target, sems.at[len(copies)])
        copy.start()
        copies.append(copy)

    for side, begin, row in ((0, 0, 0), (1, cells_theta - EDGE, cells_theta - 1)):
        fetch(density.at[pl.ds(row, 1)], rho.at[side])
        fetch(swirl.at[pl.ds(row, 1)], spin.at[side])
        fetch(acoustic.at[:, pl.ds(begin, EDGE)], wave.at[side])
    for copy in copies:
        copy.wait()
    for out, side in ((pair, 1 - odd), (link, odd)):
        edge = rho[side, 0]
        out[0:cells_radius] = edge
        out[cells_radius : 2 * cells_radius] = edge * spin[side, 0]
        at = 2 * cells_radius
        for k in range(3):
            out[at : at + EDGE] = wave[side, k]
            at += EDGE
        out[at : at + EDGE] = jnp.where(side == 0, heat[:EDGE], heat[cells_theta - EDGE :])


def flow_kernel(n_theta, mouth_azimuth, mouth_radius, density, swirl, heat_rate, forcing, heat):
    sector = lax.axis_index("sector")
    radial = lax.axis_index("radial")
    cells_theta, cells_radius, cells_axial = density.shape
    shape = (cells_radius, cells_axial)
    rows = lax.broadcasted_iota(jnp.int32, shape, 0)
    lanes = lax.broadcasted_iota(jnp.int32, shape, 1)
    segment = n_theta // BURNERS
    part = min(segment, cells_theta)
    zero = jnp.zeros(shape, F32)

    def at(t):
        if t < 0 or t >= cells_theta:
            return zero, zero
        rho = density[t]
        return rho, rho * swirl[t]

    window = [at(-1), at(0)]
    for t in range(cells_theta):
        window.append(at(t + 1))
        (rho_down, flux_down), (rho, _), (rho_up, flux_up) = window
        window = window[1:]
        if t % part == 0:
            burner = (sector * cells_theta + t) // segment
            start = burner * segment + mouth_azimuth[burner] - sector * cells_theta
            radius = mouth_radius[burner] - radial * cells_radius
            mouth = ((rows >= radius) & (rows < radius + MOUTH)).astype(F32)
            mouth = mouth * (inflow_rate / time_step)
        gain = mouth * ((start <= t) & (t < start + MOUTH)).astype(F32)
        r_up = jnp.where(rows == cells_radius - 1, 0.0, pltpu.roll(rho, cells_radius - 1, 0))
        r_down = jnp.where(rows == 0, 0.0, pltpu.roll(rho, 1, 0))
        z_up = jnp.where(lanes == cells_axial - 1, 0.0, pltpu.roll(rho, cells_axial - 1, 1))
        z_down = jnp.where(lanes == 0, 0.0, pltpu.roll(rho, 1, 1))
        twice = 2.0 * rho
        laplace = (rho_up + rho_down - twice) + (r_up + r_down - twice) + (z_up + z_down - twice)
        forcing[t] = -0.5 * (flux_up - flux_down) + diffusion * laplace + gain * (1.0 - rho)

    total = None
    for r in range(cells_radius):
        rho = density[:, r, :]
        term = heat_rate[:, r, :] * rho * rho
        total = term if total is None else total + term
    heat[...] = total


def sine_modes(basis, fields):
    high, low = split(basis)
    count = high.shape[0]
    left = jnp.concatenate(
        [jnp.concatenate([high, high], 1), jnp.concatenate([low, jnp.zeros_like(low)], 1)], 0
    )
    right = jnp.concatenate([jnp.concatenate(split(field), 1) for field in fields], 0)
    out = lax.dot_general(left, right, (NT, ((), ())), preferred_element_type=F32)
    return out[:count] + out[count:]


def spread_kernel(partial, partial_heat, pair, link, basis, forcing, heat, send):
    radials = lax.axis_size("radial")
    radial = lax.axis_index("radial")
    cells_theta, cells_radius, cells_axial = partial.shape
    sectors = send.shape[0]
    own = cells_axial // sectors
    odd = radial % 2 == 1
    inner = jnp.where(odd, pair[...], link[...]) * (diffusion * (radial > 0).astype(F32))
    outer = jnp.where(odd, link[...], pair[...]) * (diffusion * (radial < radials - 1).astype(F32))
    forcing[...] = partial[...]
    forcing[:, 0, :] = forcing[:, 0, :] + inner
    forcing[:, cells_radius - 1, :] = forcing[:, cells_radius - 1, :] + outer
    heat[...] = partial_heat[...]
    mine = basis[...]
    for r in range(0, cells_radius, 2):
        modes = sine_modes(mine, [forcing[:, r + i, :] for i in range(2)])
        for i in range(2):
            lane = slice(i * cells_theta, (i + 1) * cells_theta)
            for d in range(sectors):
                send[d, (r + i) * own : (r + i + 1) * own, :] = modes[
                    d * own : (d + 1) * own, lane
                ]


def late_kernel(
    n_radius, density, forcing, heat, acoustic, pair, link, basis, density_next, acoustic_next,
    *slots
):
    sector = lax.axis_index("sector")
    cells_theta, cells_radius, cells_axial = density.shape
    sectors = len(slots)
    own = cells_axial // sectors
    odd = sector % 2 == 1
    above = jnp.where(odd, link[...], pair[...])
    below = jnp.where(odd, pair[...], link[...])
    rho, flux = slice(0, cells_radius), slice(cells_radius, 2 * cells_radius)
    first = 0.5 * below[flux] + diffusion * below[rho]
    last = diffusion * above[rho] - 0.5 * above[flux]
    density_next[...] = density[...] + time_step * forcing[...]
    density_next[0] = density[0] + time_step * (forcing[0] + first)
    end = cells_theta - 1
    density_next[end] = density[end] + time_step * (forcing[end] + last)

    skip = 2 * cells_radius

    def extended(k):
        rows = slice(skip + k * EDGE, skip + (k + 1) * EDGE)
        middle = acoustic[k] if k < 3 else heat[...]
        return jnp.concatenate([below[rows], middle, above[rows]], 0)

    press, along, axial = extended(0), extended(1), extended(2)
    warm = extended(3) * (heat_coupling / n_radius)
    count = press.shape[0]
    lanes = lax.broadcasted_iota(jnp.int32, press.shape, 1)
    for _ in range(SUBSTEPS):
        press_up = pltpu.roll(press, count - 1, 0)
        press_axial = jnp.where(lanes == cells_axial - 1, 0.0, pltpu.roll(press, cells_axial - 1, 1))
        along = along - wave_speed * (press_up - press)
        axial = axial - wave_speed * (press_axial - press)
        along_down = pltpu.roll(along, 1, 0)
        axial_down = jnp.where(lanes == 0, 0.0, pltpu.roll(axial, 1, 1))
        press = press - wave_speed * ((along - along_down) + (axial - axial_down)) + warm
    middle = slice(EDGE, EDGE + cells_theta)
    acoustic_next[0] = press[middle]
    acoustic_next[1] = along[middle]
    acoustic_next[2] = axial[middle]
    mine = jnp.concatenate(
        [basis[pl.ds(pl.multiple_of((sector ^ k) * own, 8), own), :] for k in range(sectors)], 0
    )
    blank = jnp.zeros((cells_theta - 2 * cells_radius, cells_axial), F32)
    edges = jnp.concatenate([first, last, blank], 0)
    modes = sine_modes(mine, [feedback * press[middle], edges])
    for k, slot in enumerate(slots):
        rows = slice(k * own, (k + 1) * own)
        slot[:own] = modes[rows, :cells_theta]
        slot[own:] = modes[rows, cells_theta:]


def forward_kernel(edge, received, *refs):
    sectors, columns, cells_theta = received.shape
    slots, refs = refs[:sectors], refs[sectors:]
    tables, (modes, pair, link, wave), late = refs[:6], refs[6:10], refs[10]
    own = wave.shape[0]
    cells_radius = columns // own
    sector = lax.axis_index("sector")
    radial_odd = lax.axis_index("radial") % 2 == 1
    for k in range(sectors):
        late[sector ^ k] = slots[k][...]
    lanes = lax.broadcasted_iota(jnp.int32, (own, cells_theta), 1)

    def value(s):
        extra = late[s, own:]
        rows = []
        for r in range(cells_radius):
            first = jnp.where(lanes == 0, extra[:, r : r + 1], 0.0)
            at = cells_radius + r
            both = jnp.where(lanes == cells_theta - 1, extra[:, at : at + 1], first)
            rows.append(received[s, r * own : (r + 1) * own, :] + both)
        return jnp.concatenate(rows + [late[s, :own]], 0)

    quarter, half = sectors // 4, sectors // 2

    def joined(parts):
        return jnp.concatenate(parts, 1) if len(parts) > 1 else parts[0]

    values = [value(s) for s in range(sectors)]
    even = [values[s] + values[s + half] for s in range(half)]
    odd = [values[s] - values[s + half] for s in range(half)]
    both = [even[s] + even[s + quarter] for s in range(quarter)]
    apart = [even[s] - even[s + quarter] for s in range(quarter)]
    at = 0
    for i, parts in enumerate((both, apart, odd)):
        wh, wl = tables[2 * i : 2 * i + 2]
        lane = slice(at, at + wh.shape[1])
        out = product(split(joined(parts)), (wh[...], wl[...]), NN)
        modes[:, lane] = out[:columns]
        first, last = out[:edge], out[columns - edge : columns]
        pair[:, lane] = jnp.where(radial_odd, first, last)
        link[:, lane] = jnp.where(radial_odd, last, first)
        wave[:, lane] = out[columns:]
        at += wh.shape[1]


def solve_kernel(
    modes, pair, link, wave, inverse, scaled, axial, w0h, w0l, w1h, w1l, w2h, w2l,
    send, solved
):
    radials = lax.axis_size("radial")
    radial = lax.axis_index("radial")
    sector = lax.axis_index("sector")
    columns, n_theta = modes.shape
    each = axial.shape[1]
    cells_radius = columns // each
    has_inner = (radial > 0).astype(F32)
    has_outer = (radial < radials - 1).astype(F32)
    radial_odd = radial % 2 == 1
    eigen = axial[sector]
    step = eigen.shape[1]
    total = cells_radius + 2 * HALO
    for block in range(n_theta // step):
        lane = slice(block * step, (block + 1) * step)
        inv = jnp.broadcast_to(inverse[:, lane], (each, step))
        inv_inner, inv_outer = inv * has_inner, inv * has_outer
        last_scale = jnp.broadcast_to(scaled[:, lane], (each, step))
        add = wave[:, lane]

        def row_of(i):
            i -= HALO
            if 0 <= i < cells_radius:
                return modes[i * each : (i + 1) * each, lane]
            odd_one, even_one = (pair, link) if i < 0 else (link, pair)
            i = i + HALO if i < 0 else i - cells_radius
            rows = slice(i * each, (i + 1) * each)
            return jnp.where(radial_odd, odd_one[rows, lane], even_one[rows, lane])

        def scale_of(i):
            if i < HALO:
                return inv_inner
            return inv if i < HALO + cells_radius else inv_outer

        right = [row_of(i) + add for i in range(total)]
        x = [right[i] * scale_of(i) for i in range(total)]
        for sweep in range(1, SWEEPS):
            fresh = [None] * total
            for i in range(sweep, total - sweep):
                scale = last_scale if sweep == SWEEPS - 1 else scale_of(i)
                fresh[i] = (right[i] + (x[i + 1] + x[i - 1]) + eigen * x[i]) * scale
            x = fresh
        for i in range(cells_radius):
            solved[i * each : (i + 1) * each, lane] = x[i + HALO]

    sectors, _, width = send.shape
    n0, n1 = w0h.shape[1], w1h.shape[1]
    both = product(split(solved[:, :n0]), (w0h[...], w0l[...]), NT)
    apart = product(split(solved[:, n0 : n0 + n1]), (w1h[...], w1l[...]), NT)
    odd = product(split(solved[:, n0 + n1 :]), (w2h[...], w2l[...]), NT)
    even = jnp.concatenate([both + apart, both - apart], 1)
    for s in range(sectors // 2):
        lane = slice(s * width, (s + 1) * width)
        send[s] = even[:, lane] + odd[:, lane]
        send[s + sectors // 2] = even[:, lane] - odd[:, lane]


def pressure_kernel(received, basis, pressure):
    sectors = received.shape[0]
    cells_radius = pressure.shape[1]
    own = received.shape[1] // cells_radius
    high, low = split(basis[...])
    right = jnp.concatenate(
        [jnp.concatenate([high, low], 1), jnp.concatenate([high, jnp.zeros_like(low)], 1)], 0
    )
    cells_axial = high.shape[1]
    for r in range(cells_radius):
        rows = [received[d, r * own : (r + 1) * own, :] for d in range(sectors)]
        modes = jnp.concatenate(rows, 0)
        left = jnp.concatenate(split(modes.T), 1)
        out = lax.dot_general(left, right, (NN, ((), ())), preferred_element_type=F32)
        pressure[:, r, :] = out[:, :cells_axial] + out[:, cells_axial:]


def call(kernel, outs, ins, scratch=(), limit=24 * 1024 * 1024, **more):
    moved = sum(math.prod(o.shape) * 4 for o in outs)
    return pl.pallas_call(
        kernel,
        out_shape=outs,
        in_specs=ins,
        out_specs=[VMEM] * len(outs),
        scratch_shapes=list(scratch),
        cost_estimate=pl.CostEstimate(flops=0, bytes_accessed=3 * moved, transcendentals=0),
        compiler_params=pltpu.CompilerParams(vmem_limit_bytes=limit),
        **more,
    )


def shape(*dims):
    return jax.ShapeDtypeStruct(dims, F32)


def paired(pair, link, axis, closed):
    count = lax.axis_size(axis)
    first = [(i, i ^ 1) for i in range(count)]
    second = [(i, (i + 1) % count) for i in range(1, count if closed else count - 1, 2)]
    second += [(j, i) for i, j in second]
    return lax.ppermute(pair, axis, first), lax.ppermute(link, axis, second)


def swapped(value, axis, bits):
    return lax.ppermute(value, axis, [(i, i ^ bits) for i in range(lax.axis_size(axis))])


def summed(value, axis):
    step = 1
    while step < lax.axis_size(axis):
        value = value + swapped(value, axis, step)
        step *= 2
    return value


def exchanged(value):
    return lax.all_to_all(value, "sector", split_axis=0, concat_axis=0, tiled=True)


def shards(density, swirl, heat_rate, acoustic, mode_impedance, mouth_azimuth, mouth_radius):
    sectors = lax.axis_size("sector")
    radials = lax.axis_size("radial")
    cells_theta, cells_radius, cells_axial = density.shape
    n_theta = cells_theta * sectors
    n_radius = cells_radius * radials
    own = cells_axial // sectors
    columns = cells_radius * own
    edge = HALO * own

    basis, eigen = axial_tables(cells_axial)
    basis = jnp.asarray(basis.astype(np.float32))
    eigen = jnp.asarray(
        np.broadcast_to(eigen.reshape(sectors, own, 1), (sectors, own, 128)).astype(np.float32)
    )
    tables = []
    for table in azimuth_tables(n_theta):
        tables += [jnp.asarray(t) for t in halves(table)]
    fixed, weight = diagonal_tables(n_theta)
    inverse = (1.0 / (jnp.asarray(fixed) + mode_rows(mode_impedance)))[None, :]
    scaled = inverse * jnp.asarray(weight)[None, :]

    packed = 2 * cells_radius + 4 * EDGE
    row_block = shape(cells_theta, cells_axial)
    pair, link = call(
        rim_kernel,
        [row_block] * 2,
        [HBM],
        [pltpu.VMEM((2, cells_theta, cells_axial), F32), pltpu.SemaphoreType.DMA((2,))],
        limit=None,
    )(density)
    radial_halo = paired(pair, link, "radial", False)

    partial, heat = call(
        lambda *refs: flow_kernel(n_theta, *refs),
        [shape(*density.shape), row_block],
        [SMEM] * 2 + [VMEM] * 3,
    )(mouth_azimuth, mouth_radius, density, swirl, heat_rate)
    forcing, heat, send = call(
        spread_kernel,
        [shape(*density.shape), row_block, shape(sectors, columns, cells_theta)],
        [VMEM] * 5,
    )(partial, heat, *radial_halo, basis)
    received = exchanged(send)

    heat = summed(heat, "radial")
    pair, link = call(
        pack_kernel,
        [shape(packed, cells_axial)] * 2,
        [HBM] * 3 + [VMEM],
        [
            pltpu.VMEM((2, 1, cells_radius, cells_axial), F32),
            pltpu.VMEM((2, 1, cells_radius, cells_axial), F32),
            pltpu.VMEM((2, 3, EDGE, cells_axial), F32),
            pltpu.SemaphoreType.DMA((6,)),
        ],
    )(density, swirl, acoustic, heat)
    density_next, acoustic_next, *slots = call(
        lambda *refs: late_kernel(n_radius, *refs),
        [shape(*density.shape), shape(*acoustic.shape)] + [shape(2 * own, cells_theta)] * sectors,
        [VMEM] * 7,
    )(density, forcing, heat, acoustic, *paired(pair, link, "sector", True), basis)
    slots = [slots[0]] + [swapped(slots[k], "sector", k) for k in range(1, sectors)]

    modes, pair, link, wave = call(
        lambda *refs: forward_kernel(edge, *refs),
        [shape(columns, n_theta)] + [shape(edge, n_theta)] * 2 + [shape(own, n_theta)],
        [VMEM] * (sectors + 7),
        [pltpu.VMEM((sectors, 2 * own, cells_theta), F32)],
    )(received, *slots, *tables)
    (send,) = call(
        solve_kernel,
        [shape(sectors, columns, cells_theta)],
        [VMEM] * 13,
        [pltpu.VMEM((columns, n_theta), F32)],
    )(modes, *paired(pair, link, "radial", False), wave, inverse, scaled, eigen, *tables)

    (pressure,) = call(pressure_kernel, [shape(*density.shape)], [VMEM] * 2)(exchanged(send), basis)
    return density_next, pressure, acoustic_next


def solution(mesh):
    return jax.shard_map(
        shards,
        mesh=mesh,
        in_specs=(
            P("sector", "radial", None),
            P("sector", "radial", None),
            P("sector", "radial", None),
            P(None, "sector", None),
            P(),
            P(),
            P(),
        ),
        out_specs=(
            P("sector", "radial", None),
            P("sector", "radial", None),
            P(None, "sector", None),
        ),
        check_vma=False,
    )
```

```python
import math

import jax
import jax.numpy as jnp
import numpy as np
from jax import lax
from jax.experimental import pallas as pl
from jax.experimental.pallas import tpu as pltpu
from jax.sharding import PartitionSpec as P

BURNERS = 16
MOUTH = 8
SWEEPS = 4
SUBSTEPS = 8

time_step = 0.2
diffusion = 0.05
inflow_rate = 0.5
wave_speed = 0.5
heat_coupling = 0.5
feedback = 0.5

F32 = jnp.float32
BF16 = jnp.bfloat16
HALO = SWEEPS - 1
EDGE = 8
VMEM = pl.BlockSpec(memory_space=pltpu.VMEM)
SMEM = pl.BlockSpec(memory_space=pltpu.SMEM)
HBM = pl.BlockSpec(memory_space=pltpu.HBM)


def halves(table):
    high = table.astype(BF16)
    low = (table - high.astype(np.float64)).astype(BF16)
    return high, low


def axial_tables(cells):
    index = np.arange(1, cells + 1, dtype=np.float64)
    basis = math.sqrt(2.0 / (cells + 1)) * np.sin(
        np.pi * ((index[:, None] * index[None, :]) % (2 * (cells + 1))) / (cells + 1)
    )
    return basis, 2.0 * np.cos(np.pi * index / (cells + 1))


def mode_classes(n_theta):
    half = n_theta // 2
    multiples = np.arange(0, half, 4)
    first = (
        np.concatenate([multiples, [half], multiples[1:]]),
        np.concatenate([np.zeros(len(multiples) + 1), np.ones(len(multiples) - 1)]),
    )
    twos = np.arange(2, half, 4)
    second = (np.concatenate([twos, twos]), np.repeat([0, 1], len(twos)))
    ones, threes = np.arange(1, half, 4), np.arange(3, half, 4)
    third = (np.concatenate([ones, threes, ones, threes]), np.repeat([0, 1], half // 2))
    return first, second, third


def azimuth_tables(n_theta):
    bases = []
    for (order, odd), rows in zip(mode_classes(n_theta), (n_theta // 4, n_theta // 4, n_theta // 2)):
        phase = (np.arange(rows)[:, None] * order[None, :].astype(np.int64)) % n_theta
        angle = phase * (2.0 * np.pi / n_theta)
        bases.append(np.where(odd[None, :] == 0, np.cos(angle), np.sin(angle)))
    return bases


def diagonal_tables(n_theta):
    half = n_theta // 2
    order = np.concatenate([part[0] for part in mode_classes(n_theta)])
    shifted = 2.0 - 2.0 * np.cos(order * (2.0 * np.pi / n_theta))
    weight = np.where((order == 0) | (order == half), 1.0, 2.0) / n_theta
    return (4.0 + shifted).astype(np.float32), weight.astype(np.float32)


def mode_rows(impedance):
    half = impedance.shape[0] - 1
    by_four = impedance[:half].reshape(half // 4, 4).T
    q0, q1, q2, q3 = by_four[0], by_four[1], by_four[2], by_four[3]
    first = jnp.concatenate([impedance[half:], q0[1:]])
    return jnp.concatenate([q0, first, q2, q2, q1, q3, q1, q3])


def split(value):
    high = value.astype(BF16)
    return high, (value - high.astype(F32)).astype(BF16)


def product(left, right, dims):
    def one(a, b):
        return lax.dot_general(a, b, (dims, ((), ())), preferred_element_type=F32)

    return one(left[0], right[0]) + (one(left[1], right[0]) + one(left[0], right[1]))


NN = ((1,), (0,))
NT = ((1,), (1,))


def edges_kernel(
    density, swirl, heat_rate, acoustic, radial_pair, radial_link, sector_pair, sector_link, rho,
    rate, spin, wave, rim, sems
):
    cells_theta, cells_radius, _ = density.shape
    radial_odd = lax.axis_index("radial") % 2
    sector_odd = lax.axis_index("sector") % 2
    copies = []

    def fetch(source, target):
        copy = pltpu.make_async_copy(source, target, sems.at[len(copies)])
        copy.start()
        copies.append(copy)

    for side, begin, row in ((0, 0, 0), (1, cells_theta - EDGE, cells_theta - 1)):
        fetch(density.at[pl.ds(begin, EDGE)], rho.at[side])
        fetch(heat_rate.at[pl.ds(begin, EDGE)], rate.at[side])
        fetch(swirl.at[pl.ds(row, 1)], spin.at[side])
        fetch(acoustic.at[:, pl.ds(begin, EDGE)], wave.at[side])
    fetch(density.at[:, 0, :], rim.at[0])
    fetch(density.at[:, cells_radius - 1, :], rim.at[1])
    for copy in copies:
        copy.wait()
    radial_pair[...] = rim[1 - radial_odd]
    radial_link[...] = rim[radial_odd]
    for out, side in ((sector_pair, 1 - sector_odd), (sector_link, sector_odd)):
        edge = jnp.where(side == 0, rho[0, 0], rho[1, EDGE - 1])
        out[0:cells_radius] = edge
        out[cells_radius : 2 * cells_radius] = edge * spin[side, 0]
        at = 2 * cells_radius
        for k in range(3):
            out[at : at + EDGE] = wave[side, k]
            at += EDGE
        heat = jnp.sum(rate[side] * rho[side] * rho[side], axis=1)
        out[at : at + EDGE] = heat


def flow_kernel(n_theta, mouth_azimuth, mouth_radius, density, swirl, forcing):
    sector = lax.axis_index("sector")
    radial = lax.axis_index("radial")
    cells_theta, cells_radius, cells_axial = density.shape
    shape = (cells_radius, cells_axial)
    rows = lax.broadcasted_iota(jnp.int32, shape, 0)
    lanes = lax.broadcasted_iota(jnp.int32, shape, 1)
    segment = n_theta // BURNERS
    part = min(segment, cells_theta)
    zero = jnp.zeros(shape, F32)

    def at(t):
        if t < 0 or t >= cells_theta:
            return zero, zero
        rho = density[t]
        return rho, rho * swirl[t]

    window = [at(-1), at(0)]
    for t in range(cells_theta):
        window.append(at(t + 1))
        (rho_down, flux_down), (rho, _), (rho_up, flux_up) = window
        window = window[1:]
        if t % part == 0:
            burner = (sector * cells_theta + t) // segment
            start = burner * segment + mouth_azimuth[burner] - sector * cells_theta
            radius = mouth_radius[burner] - radial * cells_radius
            mouth = ((rows >= radius) & (rows < radius + MOUTH)).astype(F32)
            mouth = mouth * (inflow_rate / time_step)
        gain = mouth * ((start <= t) & (t < start + MOUTH)).astype(F32)
        r_up = jnp.where(rows == cells_radius - 1, 0.0, pltpu.roll(rho, cells_radius - 1, 0))
        r_down = jnp.where(rows == 0, 0.0, pltpu.roll(rho, 1, 0))
        z_up = jnp.where(lanes == cells_axial - 1, 0.0, pltpu.roll(rho, cells_axial - 1, 1))
        z_down = jnp.where(lanes == 0, 0.0, pltpu.roll(rho, 1, 1))
        twice = 2.0 * rho
        laplace = (rho_up + rho_down - twice) + (r_up + r_down - twice) + (z_up + z_down - twice)
        forcing[t] = -0.5 * (flux_up - flux_down) + diffusion * laplace + gain * (1.0 - rho)


def sine_modes(basis, fields):
    high, low = split(basis)
    count = high.shape[0]
    left = jnp.concatenate(
        [jnp.concatenate([high, high], 1), jnp.concatenate([low, jnp.zeros_like(low)], 1)], 0
    )
    right = jnp.concatenate([jnp.concatenate(split(field), 1) for field in fields], 0)
    out = lax.dot_general(left, right, (NT, ((), ())), preferred_element_type=F32)
    return out[:count] + out[count:]


GROUP = 4


def spread_kernel(
    partial, density, radial_pair, radial_link, sector_pair, sector_link, basis, density_next, send,
    forcing, following, staged, sems
):
    radials = lax.axis_size("radial")
    radial = lax.axis_index("radial")
    cells_theta, cells_radius, cells_axial = partial.shape
    sectors = send.shape[0]
    own = cells_axial // sectors
    odd = lax.axis_index("sector") % 2 == 1
    above = jnp.where(odd, sector_link[...], sector_pair[...])
    below = jnp.where(odd, sector_pair[...], sector_link[...])
    odd = radial % 2 == 1
    inner = jnp.where(odd, radial_pair[...], radial_link[...])
    outer = jnp.where(odd, radial_link[...], radial_pair[...])
    rho, flux = slice(0, cells_radius), slice(cells_radius, 2 * cells_radius)
    end = cells_theta - 1
    forcing[...] = partial[...]
    forcing[0] = forcing[0] + (0.5 * below[flux] + diffusion * below[rho])
    forcing[end] = forcing[end] + (diffusion * above[rho] - 0.5 * above[flux])
    inside = diffusion * (radial > 0).astype(F32)
    outside = diffusion * (radial < radials - 1).astype(F32)
    forcing[:, 0, :] = forcing[:, 0, :] + inside * inner
    forcing[:, cells_radius - 1, :] = forcing[:, cells_radius - 1, :] + outside * outer
    following[...] = density[...] + time_step * forcing[...]
    copies = [pltpu.make_async_copy(following, density_next, sems.at[0])]
    copies[0].start()
    mine = basis[...]
    for r in range(0, cells_radius, GROUP):
        modes = sine_modes(mine, [forcing[:, r + i, :] for i in range(GROUP)])
        for i in range(GROUP):
            lane = slice(i * cells_theta, (i + 1) * cells_theta)
            for d in range(sectors):
                staged[d, (r + i) * own : (r + i + 1) * own, :] = modes[
                    d * own : (d + 1) * own, lane
                ]
        rows = pl.ds(r * own, GROUP * own)
        copy = pltpu.make_async_copy(
            staged.at[:, rows, :], send.at[:, rows, :], sems.at[len(copies)]
        )
        copy.start()
        copies.append(copy)
    for copy in copies:
        copy.wait()


def acoustic_kernel(
    n_radius, density, heat_rate, acoustic, pair, link, basis, state, *slots
):
    sector = lax.axis_index("sector")
    cells_theta, cells_radius, cells_axial = density.shape
    sectors = len(slots)
    own = cells_axial // sectors
    share = (lax.axis_index("radial") == 0).astype(F32)
    odd = sector % 2 == 1
    above = jnp.where(odd, link[...], pair[...])
    below = jnp.where(odd, pair[...], link[...])
    heat = None
    for r in range(cells_radius):
        rho = density[:, r, :]
        term = heat_rate[:, r, :] * rho * rho
        heat = term if heat is None else heat + term
    skip = 2 * cells_radius

    def extended(k):
        rows = slice(skip + k * EDGE, skip + (k + 1) * EDGE)
        middle = acoustic[k] if k < 3 else heat
        return jnp.concatenate([below[rows], middle, above[rows]], 0)

    press, along, axial = extended(0) * share, extended(1) * share, extended(2) * share
    warm = extended(3) * (heat_coupling / n_radius)
    count = press.shape[0]
    lanes = lax.broadcasted_iota(jnp.int32, press.shape, 1)
    for _ in range(SUBSTEPS):
        press_up = pltpu.roll(press, count - 1, 0)
        press_axial = jnp.where(lanes == cells_axial - 1, 0.0, pltpu.roll(press, cells_axial - 1, 1))
        along = along - wave_speed * (press_up - press)
        axial = axial - wave_speed * (press_axial - press)
        along_down = pltpu.roll(along, 1, 0)
        axial_down = jnp.where(lanes == 0, 0.0, pltpu.roll(axial, 1, 1))
        press = press - wave_speed * ((along - along_down) + (axial - axial_down)) + warm
    middle = slice(EDGE, EDGE + cells_theta)
    state[0] = press[middle]
    state[1] = along[middle]
    state[2] = axial[middle]
    mine = jnp.concatenate(
        [basis[pl.ds(pl.multiple_of((sector ^ k) * own, 8), own), :] for k in range(sectors)], 0
    )
    modes = sine_modes(mine, [feedback * press[middle]])
    for k, slot in enumerate(slots):
        slot[...] = modes[k * own : (k + 1) * own]


def transformed(values, table, store):
    sectors = len(values)
    quarter, half = sectors // 4, sectors // 2

    def joined(parts):
        return jnp.concatenate(parts, 1) if len(parts) > 1 else parts[0]

    even = [values[s] + values[s + half] for s in range(half)]
    odd = [values[s] - values[s + half] for s in range(half)]
    both = [even[s] + even[s + quarter] for s in range(quarter)]
    apart = [even[s] - even[s + quarter] for s in range(quarter)]
    at = 0
    for parts, pieces in zip((both, apart, odd), table_parts(table)):
        width = pieces[0].shape[1]
        store(slice(at, at + width), product(split(joined(parts)), pieces, NN))
        at += width


def table_parts(table):
    n_theta = table.shape[1]
    quarter, half = n_theta // 4, n_theta // 2
    top, bottom = slice(0, quarter), slice(quarter, quarter + half)
    columns = [slice(i * quarter, (i + 1) * quarter) for i in range(4)]
    return (
        (table[top, columns[0]], table[top, columns[1]]),
        (table[top, columns[2]], table[top, columns[3]]),
        (table[bottom, :half], table[bottom, half:]),
    )


def forward_kernel(edge, received, table, modes, pair, link):
    sectors, columns, _ = received.shape
    radial_odd = lax.axis_index("radial") % 2 == 1

    def store(lane, out):
        modes[:, lane] = out
        first, last = out[:edge], out[columns - edge :]
        pair[:, lane] = jnp.where(radial_odd, first, last)
        link[:, lane] = jnp.where(radial_odd, last, first)

    transformed([received[s] for s in range(sectors)], table, store)


def wave_kernel(*refs):
    slots, (table, wave, pieces) = refs[:-3], refs[-3:]
    sector = lax.axis_index("sector")
    for k, slot in enumerate(slots):
        pieces[sector ^ k] = slot[...]

    def store(lane, out):
        wave[:, lane] = out

    transformed([pieces[s] for s in range(len(slots))], table, store)


def solve_kernel(
    modes, pair, link, wave, inverse, scaled, axial, table, state_in, send, state, solved
):
    radials = lax.axis_size("radial")
    radial = lax.axis_index("radial")
    sector = lax.axis_index("sector")
    columns, n_theta = modes.shape
    each = axial.shape[1]
    cells_radius = columns // each
    has_inner = (radial > 0).astype(F32)
    has_outer = (radial < radials - 1).astype(F32)
    radial_odd = radial % 2 == 1
    eigen = axial[sector]
    step = eigen.shape[1]
    total = cells_radius + 2 * HALO
    for block in range(n_theta // step):
        lane = slice(block * step, (block + 1) * step)
        inv = jnp.broadcast_to(inverse[:, lane], (each, step))
        inv_inner, inv_outer = inv * has_inner, inv * has_outer
        last_scale = jnp.broadcast_to(scaled[:, lane], (each, step))
        add = wave[:, lane]

        def row_of(i):
            i -= HALO
            if 0 <= i < cells_radius:
                return modes[i * each : (i + 1) * each, lane]
            odd_one, even_one = (pair, link) if i < 0 else (link, pair)
            i = i + HALO if i < 0 else i - cells_radius
            rows = slice(i * each, (i + 1) * each)
            return jnp.where(radial_odd, odd_one[rows, lane], even_one[rows, lane])

        def scale_of(i):
            if i < HALO:
                return inv_inner
            return inv if i < HALO + cells_radius else inv_outer

        right = [row_of(i) + add for i in range(total)]
        x = [right[i] * scale_of(i) for i in range(total)]
        for sweep in range(1, SWEEPS):
            fresh = [None] * total
            for i in range(sweep, total - sweep):
                scale = last_scale if sweep == SWEEPS - 1 else scale_of(i)
                fresh[i] = (right[i] + (x[i + 1] + x[i - 1]) + eigen * x[i]) * scale
            x = fresh
        for i in range(cells_radius):
            solved[i * each : (i + 1) * each, lane] = x[i + HALO]

    sectors, _, width = send.shape
    outs, at = [], 0
    for pieces in table_parts(table):
        lane = slice(at, at + pieces[0].shape[1])
        outs.append(product(split(solved[:, lane]), pieces, NT))
        at = lane.stop
    both, apart, odd = outs
    even = jnp.concatenate([both + apart, both - apart], 1)
    for s in range(sectors // 2):
        lane = slice(s * width, (s + 1) * width)
        send[s] = even[:, lane] + odd[:, lane]
        send[s + sectors // 2] = even[:, lane] - odd[:, lane]


def pressure_kernel(received, basis, pressure):
    sectors = received.shape[0]
    cells_radius = pressure.shape[1]
    own = received.shape[1] // cells_radius
    high, low = split(basis[...])
    right = jnp.concatenate(
        [jnp.concatenate([high, low], 1), jnp.concatenate([high, jnp.zeros_like(low)], 1)], 0
    )
    cells_axial = high.shape[1]
    for r in range(cells_radius):
        rows = [received[d, r * own : (r + 1) * own, :] for d in range(sectors)]
        modes = jnp.concatenate(rows, 0)
        left = jnp.concatenate(split(modes.T), 1)
        out = lax.dot_general(left, right, (NN, ((), ())), preferred_element_type=F32)
        pressure[:, r, :] = out[:, :cells_axial] + out[:, cells_axial:]


def call(kernel, outs, ins, scratch=(), limit=24 * 1024 * 1024, **more):
    moved = sum(math.prod(o.shape) * 4 for o in outs)
    return pl.pallas_call(
        kernel,
        out_shape=outs,
        in_specs=ins,
        out_specs=more.pop("out_specs", [VMEM] * len(outs)),
        scratch_shapes=list(scratch),
        cost_estimate=pl.CostEstimate(flops=0, bytes_accessed=3 * moved, transcendentals=0),
        compiler_params=pltpu.CompilerParams(vmem_limit_bytes=limit),
        **more,
    )


def shape(*dims):
    return jax.ShapeDtypeStruct(dims, F32)


def paired(pair, link, axis, closed):
    count = lax.axis_size(axis)
    first = [(i, i ^ 1) for i in range(count)]
    second = [(i, (i + 1) % count) for i in range(1, count if closed else count - 1, 2)]
    second += [(j, i) for i, j in second]
    return lax.ppermute(pair, axis, first), lax.ppermute(link, axis, second)


def swapped(value, axis, bits):
    return lax.ppermute(value, axis, [(i, i ^ bits) for i in range(lax.axis_size(axis))])


def summed(value, axis):
    step = 1
    while step < lax.axis_size(axis):
        value = value + swapped(value, axis, step)
        step *= 2
    return value


def exchanged(value):
    return lax.all_to_all(value, "sector", split_axis=0, concat_axis=0, tiled=True)


def shards(density, swirl, heat_rate, acoustic, mode_impedance, mouth_azimuth, mouth_radius):
    sectors = lax.axis_size("sector")
    radials = lax.axis_size("radial")
    cells_theta, cells_radius, cells_axial = density.shape
    n_theta = cells_theta * sectors
    n_radius = cells_radius * radials
    own = cells_axial // sectors
    columns = cells_radius * own
    edge = HALO * own

    basis, eigen = axial_tables(cells_axial)
    basis = jnp.asarray(basis.astype(np.float32))
    eigen = jnp.asarray(
        np.broadcast_to(eigen.reshape(sectors, own, 1), (sectors, own, 128)).astype(np.float32)
    )
    parts = [halves(table) for table in azimuth_tables(n_theta)]
    table = jnp.asarray(
        np.concatenate(
            [np.concatenate(parts[0] + parts[1], 1), np.concatenate(parts[2], 1)], 0
        )
    )
    fixed, weight = diagonal_tables(n_theta)
    inverse = (1.0 / (jnp.asarray(fixed) + mode_rows(mode_impedance)))[None, :]
    scaled = inverse * jnp.asarray(weight)[None, :]

    packed = 2 * cells_radius + 4 * EDGE
    row_block = shape(cells_theta, cells_axial)
    edges = call(
        edges_kernel,
        [row_block] * 2 + [shape(packed, cells_axial)] * 2,
        [HBM] * 4,
        [
            pltpu.VMEM((2, EDGE, cells_radius, cells_axial), F32),
            pltpu.VMEM((2, EDGE, cells_radius, cells_axial), F32),
            pltpu.VMEM((2, 1, cells_radius, cells_axial), F32),
            pltpu.VMEM((2, 3, EDGE, cells_axial), F32),
            pltpu.VMEM((2, cells_theta, cells_axial), F32),
            pltpu.SemaphoreType.DMA((10,)),
        ],
        limit=None,
    )(density, swirl, heat_rate, acoustic)
    sector_halo = paired(edges[2], edges[3], "sector", True)
    radial_halo = paired(edges[0], edges[1], "radial", False)

    (partial,) = call(
        lambda *refs: flow_kernel(n_theta, *refs),
        [shape(*density.shape)],
        [SMEM] * 2 + [VMEM] * 2,
    )(mouth_azimuth, mouth_radius, density, swirl)
    density_next, send = call(
        spread_kernel,
        [shape(*density.shape), shape(sectors, columns, cells_theta)],
        [VMEM] * 7,
        [pltpu.VMEM(density.shape, F32)] * 2
        + [pltpu.VMEM((sectors, columns, cells_theta), F32)]
        + [pltpu.SemaphoreType.DMA((1 + cells_radius // GROUP,))],
        out_specs=[HBM] * 2,
    )(partial, density, *radial_halo, *sector_halo, basis)
    received = exchanged(send)

    state, *slots = call(
        lambda *refs: acoustic_kernel(n_radius, *refs),
        [shape(*acoustic.shape)] + [shape(own, cells_theta)] * sectors,
        [VMEM] * 6,
    )(density, heat_rate, acoustic, *sector_halo, basis)
    slots = [slots[0]] + [swapped(slots[k], "sector", k) for k in range(1, sectors)]

    modes, pair, link = call(
        lambda *refs: forward_kernel(edge, *refs),
        [shape(columns, n_theta)] + [shape(edge, n_theta)] * 2,
        [VMEM] * 2,
    )(received, table)
    (wave,) = call(
        wave_kernel,
        [shape(own, n_theta)],
        [VMEM] * (sectors + 1),
        [pltpu.VMEM((sectors, own, cells_theta), F32)],
    )(*slots, table)
    send, state = call(
        solve_kernel,
        [shape(sectors, columns, cells_theta), shape(*acoustic.shape)],
        [VMEM] * 8 + [HBM],
        [pltpu.VMEM((columns, n_theta), F32)],
        out_specs=[VMEM, HBM],
        input_output_aliases={8: 1},
    )(
        modes, *paired(pair, link, "radial", False), summed(wave, "radial"), inverse, scaled, eigen,
        table, state,
    )
    acoustic_next = summed(state, "radial")

    (pressure,) = call(pressure_kernel, [shape(*density.shape)], [VMEM] * 2)(exchanged(send), basis)
    return density_next, pressure, acoustic_next


def solution(mesh):
    return jax.shard_map(
        shards,
        mesh=mesh,
        in_specs=(
            P("sector", "radial", None),
            P("sector", "radial", None),
            P("sector", "radial", None),
            P(None, "sector", None),
            P(),
            P(),
            P(),
        ),
        out_specs=(
            P("sector", "radial", None),
            P("sector", "radial", None),
            P(None, "sector", None),
        ),
        check_vma=False,
    )
```

```python
import math

import jax
import jax.numpy as jnp
import numpy as np
from jax import lax
from jax.experimental import pallas as pl
from jax.experimental.pallas import tpu as pltpu
from jax.sharding import PartitionSpec as P


BURNERS = 16
MOUTH = 8
SWEEPS = 4
SUBSTEPS = 8

time_step = 0.2
diffusion = 0.05
inflow_rate = 0.5
wave_speed = 0.5
heat_coupling = 0.5
feedback = 0.5

F32 = jnp.float32
BF16 = jnp.bfloat16
HALO = SWEEPS - 1
EDGE = 8
VMEM = pl.BlockSpec(memory_space=pltpu.VMEM)
SMEM = pl.BlockSpec(memory_space=pltpu.SMEM)
HBM = pl.BlockSpec(memory_space=pltpu.HBM)


def halves(table):
    high = table.astype(BF16)
    low = (table - high.astype(np.float64)).astype(BF16)
    return high, low


def axial_tables(cells):
    index = np.arange(1, cells + 1, dtype=np.float64)
    basis = math.sqrt(2.0 / (cells + 1)) * np.sin(
        np.pi * ((index[:, None] * index[None, :]) % (2 * (cells + 1))) / (cells + 1)
    )
    return basis, 2.0 * np.cos(np.pi * index / (cells + 1))


def mode_classes(n_theta):
    half = n_theta // 2
    multiples = np.arange(0, half, 4)
    first = (
        np.concatenate([multiples, [half], multiples[1:]]),
        np.concatenate([np.zeros(len(multiples) + 1), np.ones(len(multiples) - 1)]),
    )
    twos = np.arange(2, half, 4)
    second = (np.concatenate([twos, twos]), np.repeat([0, 1], len(twos)))
    ones, threes = np.arange(1, half, 4), np.arange(3, half, 4)
    third = (np.concatenate([ones, threes, ones, threes]), np.repeat([0, 1], half // 2))
    return first, second, third


def azimuth_tables(n_theta):
    bases = []
    for (order, odd), rows in zip(mode_classes(n_theta), (n_theta // 4, n_theta // 4, n_theta // 2)):
        phase = (np.arange(rows)[:, None] * order[None, :].astype(np.int64)) % n_theta
        angle = phase * (2.0 * np.pi / n_theta)
        bases.append(np.where(odd[None, :] == 0, np.cos(angle), np.sin(angle)))
    return bases


def diagonal_tables(n_theta):
    half = n_theta // 2
    order = np.concatenate([part[0] for part in mode_classes(n_theta)])
    shifted = 2.0 - 2.0 * np.cos(order * (2.0 * np.pi / n_theta))
    weight = np.where((order == 0) | (order == half), 1.0, 2.0) / n_theta
    return (4.0 + shifted).astype(np.float32), weight.astype(np.float32)


def split(value):
    high = value.astype(BF16)
    return high, (value - high.astype(F32)).astype(BF16)


def product(left, right, dims):
    def one(a, b):
        return lax.dot_general(a, b, (dims, ((), ())), preferred_element_type=F32)

    return one(left[0], right[0]) + (one(left[1], right[0]) + one(left[0], right[1]))


NN = ((1,), (0,))
NT = ((1,), (1,))


def edges_kernel(density, swirl, heat_rate, acoustic, pair, link, rho, rate, spin, wave, sems):
    cells_theta, cells_radius, _ = density.shape
    odd = lax.axis_index("sector") % 2
    copies = []

    def fetch(source, target):
        copy = pltpu.make_async_copy(source, target, sems.at[len(copies)])
        copy.start()
        copies.append(copy)

    for side, begin, row in ((0, 0, 0), (1, cells_theta - EDGE, cells_theta - 1)):
        fetch(density.at[pl.ds(begin, EDGE)], rho.at[side])
        fetch(heat_rate.at[pl.ds(begin, EDGE)], rate.at[side])
        fetch(swirl.at[pl.ds(row, 1)], spin.at[side])
        fetch(acoustic.at[:, pl.ds(begin, EDGE)], wave.at[side])
    for copy in copies:
        copy.wait()
    for out, side in ((pair, 1 - odd), (link, odd)):
        edge = jnp.where(side == 0, rho[0, 0], rho[1, EDGE - 1])
        out[0:cells_radius] = edge
        out[cells_radius : 2 * cells_radius] = edge * spin[side, 0]
        at = 2 * cells_radius
        for k in range(3):
            out[at : at + EDGE] = wave[side, k]
            at += EDGE
        heat = jnp.sum(rate[side] * rho[side] * rho[side], axis=1)
        out[at : at + EDGE] = heat


def flow_rows(n_theta, mouth_azimuth, mouth_radius, density, swirl, forcing):
    sector = lax.axis_index("sector")
    radial = lax.axis_index("radial")
    cells_theta, cells_radius, cells_axial = density.shape
    shape = (cells_radius, cells_axial)
    rows = lax.broadcasted_iota(jnp.int32, shape, 0)
    lanes = lax.broadcasted_iota(jnp.int32, shape, 1)
    segment = n_theta // BURNERS
    part = min(segment, cells_theta)
    zero = jnp.zeros(shape, F32)

    def at(t):
        if t < 0 or t >= cells_theta:
            return zero, zero
        rho = density[t]
        return rho, rho * swirl[t]

    window = [at(-1), at(0)]
    for t in range(cells_theta):
        window.append(at(t + 1))
        (rho_down, flux_down), (rho, _), (rho_up, flux_up) = window
        window = window[1:]
        if t % part == 0:
            burner = (sector * cells_theta + t) // segment
            start = burner * segment + mouth_azimuth[burner] - sector * cells_theta
            radius = mouth_radius[burner] - radial * cells_radius
            mouth = ((rows >= radius) & (rows < radius + MOUTH)).astype(F32)
            mouth = mouth * (inflow_rate / time_step)
        gain = mouth * ((start <= t) & (t < start + MOUTH)).astype(F32)
        r_up = jnp.where(rows == cells_radius - 1, 0.0, pltpu.roll(rho, cells_radius - 1, 0))
        r_down = jnp.where(rows == 0, 0.0, pltpu.roll(rho, 1, 0))
        z_up = jnp.where(lanes == cells_axial - 1, 0.0, pltpu.roll(rho, cells_axial - 1, 1))
        z_down = jnp.where(lanes == 0, 0.0, pltpu.roll(rho, 1, 1))
        twice = 2.0 * rho
        laplace = (rho_up + rho_down - twice) + (r_up + r_down - twice) + (z_up + z_down - twice)
        forcing[t] = -0.5 * (flux_up - flux_down) + diffusion * laplace + gain * (1.0 - rho)


def add_halos(forcing, radial_pair, radial_link, sector_pair, sector_link):
    radials = lax.axis_size("radial")
    radial = lax.axis_index("radial")
    cells_theta, cells_radius, _ = forcing.shape
    odd = lax.axis_index("sector") % 2 == 1
    above = jnp.where(odd, sector_link[...], sector_pair[...])
    below = jnp.where(odd, sector_pair[...], sector_link[...])
    odd = radial % 2 == 1
    inner = jnp.where(odd, radial_pair[...], radial_link[...])
    outer = jnp.where(odd, radial_link[...], radial_pair[...])
    rho, flux = slice(0, cells_radius), slice(cells_radius, 2 * cells_radius)
    end = cells_theta - 1
    forcing[0] = forcing[0] + (0.5 * below[flux] + diffusion * below[rho])
    forcing[end] = forcing[end] + (diffusion * above[rho] - 0.5 * above[flux])
    inside = diffusion * (radial > 0).astype(F32)
    outside = diffusion * (radial < radials - 1).astype(F32)
    forcing[:, 0, :] = forcing[:, 0, :] + inside * inner
    forcing[:, cells_radius - 1, :] = forcing[:, cells_radius - 1, :] + outside * outer
    return above, below


def flow_kernel(
    n_theta, mouth_azimuth, mouth_radius, density, swirl, heat_rate, _, forcing, heat, pair, link
):
    cells_theta, cells_radius, _ = density.shape
    odd = lax.axis_index("radial") % 2 == 1
    first, last = density[:, 0, :], density[:, cells_radius - 1, :]
    pair[...] = jnp.where(odd, first, last)
    link[...] = jnp.where(odd, last, first)
    flow_rows(n_theta, mouth_azimuth, mouth_radius, density, swirl, forcing)
    for t in range(0, cells_theta, 8):
        rho = density[t : t + 8]
        heat[t : t + 8] = jnp.sum(heat_rate[t : t + 8] * rho * rho, axis=1)


def sine_modes(basis, fields):
    high, low = split(basis)
    count = high.shape[0]
    left = jnp.concatenate(
        [jnp.concatenate([high, high], 1), jnp.concatenate([low, jnp.zeros_like(low)], 1)], 0
    )
    right = jnp.concatenate([jnp.concatenate(split(field), 1) for field in fields], 0)
    out = lax.dot_general(left, right, (NT, ((), ())), preferred_element_type=F32)
    return out[:count] + out[count:]


GROUP = 4


def first_kernel(
    n_radius, partial, heat, acoustic, radial_pair, radial_link, sector_pair, sector_link, basis,
    state, send, forcing, following, staged, sems
):
    radial = lax.axis_index("radial")
    cells_theta, cells_radius, cells_axial = partial.shape
    sectors = send.shape[0]
    own = cells_axial // sectors
    forcing[...] = partial[...]
    above, below = add_halos(forcing, radial_pair, radial_link, sector_pair, sector_link)
    copies = []

    def leave(begin, count):
        rows = pl.ds(begin, count)
        copy = pltpu.make_async_copy(
            staged.at[:, rows, :], send.at[:, rows, :], sems.at[len(copies)]
        )
        copy.start()
        copies.append(copy)

    mine = basis[...]
    for r in range(0, cells_radius, GROUP):
        modes = sine_modes(mine, [forcing[:, r + i, :] for i in range(GROUP)])
        for i in range(GROUP):
            lane = slice(i * cells_theta, (i + 1) * cells_theta)
            for d in range(sectors):
                staged[d, (r + i) * own : (r + i + 1) * own, :] = modes[
                    d * own : (d + 1) * own, lane
                ]
        leave(r * own, GROUP * own)

    share = (radial == 0).astype(F32)
    skip = 2 * cells_radius

    def extended(k):
        rows = slice(skip + k * EDGE, skip + (k + 1) * EDGE)
        middle = acoustic[k] if k < 3 else heat[...]
        return jnp.concatenate([below[rows], middle, above[rows]], 0)

    press, along, axial = extended(0) * share, extended(1) * share, extended(2) * share
    warm = extended(3) * (heat_coupling / n_radius)
    count = press.shape[0]
    lanes = lax.broadcasted_iota(jnp.int32, press.shape, 1)
    for _ in range(SUBSTEPS):
        press_up = pltpu.roll(press, count - 1, 0)
        press_axial = jnp.where(lanes == cells_axial - 1, 0.0, pltpu.roll(press, cells_axial - 1, 1))
        along = along - wave_speed * (press_up - press)
        axial = axial - wave_speed * (press_axial - press)
        along_down = pltpu.roll(along, 1, 0)
        axial_down = jnp.where(lanes == 0, 0.0, pltpu.roll(axial, 1, 1))
        press = press - wave_speed * ((along - along_down) + (axial - axial_down)) + warm
    middle = slice(EDGE, EDGE + cells_theta)
    following[0] = press[middle]
    following[1] = along[middle]
    following[2] = axial[middle]
    copies.append(pltpu.make_async_copy(following, state, sems.at[len(copies)]))
    copies[-1].start()
    modes = sine_modes(mine, [feedback * press[middle]])
    columns = cells_radius * own
    for d in range(sectors):
        staged[d, columns : columns + own, :] = modes[d * own : (d + 1) * own]
    leave(columns, own)
    for copy in copies:
        copy.wait()


def transformed(values, table, store):
    sectors = len(values)
    quarter, half = sectors // 4, sectors // 2

    def joined(parts):
        return jnp.concatenate(parts, 1) if len(parts) > 1 else parts[0]

    even = [values[s] + values[s + half] for s in range(half)]
    odd = [values[s] - values[s + half] for s in range(half)]
    both = [even[s] + even[s + quarter] for s in range(quarter)]
    apart = [even[s] - even[s + quarter] for s in range(quarter)]
    at = 0
    for parts, pieces in zip((both, apart, odd), table_parts(table)):
        width = pieces[0].shape[1]
        store(slice(at, at + width), product(split(joined(parts)), pieces, NN))
        at += width


def table_parts(table):
    n_theta = table.shape[1]
    quarter, half = n_theta // 4, n_theta // 2
    top, bottom = slice(0, quarter), slice(quarter, quarter + half)
    columns = [slice(i * quarter, (i + 1) * quarter) for i in range(4)]
    return (
        (table[top, columns[0]], table[top, columns[1]]),
        (table[top, columns[2]], table[top, columns[3]]),
        (table[bottom, :half], table[bottom, half:]),
    )


def forward_kernel(edge, received, table, *refs):
    modes, pair, link, wave = refs[-4:]
    sectors = received.shape[0]
    columns = modes.shape[0]
    radial_odd = lax.axis_index("radial") % 2 == 1

    def store(lane, out):
        modes[:, lane] = out[:columns]
        first, last = out[:edge], out[columns - edge : columns]
        pair[:, lane] = jnp.where(radial_odd, first, last)
        link[:, lane] = jnp.where(radial_odd, last, first)
        wave[:, lane] = out[columns:]

    transformed([received[s] for s in range(sectors)], table, store)


def solve_kernel(
    modes, pair, link, wave, other_wave, impedance, fixed, weight, axial, table, send, solved
):
    radials = lax.axis_size("radial")
    radial = lax.axis_index("radial")
    sector = lax.axis_index("sector")
    columns, n_theta = modes.shape
    each = axial.shape[1]
    cells_radius = columns // each
    has_inner = (radial > 0).astype(F32)
    has_outer = (radial < radials - 1).astype(F32)
    radial_odd = radial % 2 == 1
    eigen = axial[sector]
    step = eigen.shape[1]
    total = cells_radius + 2 * HALO
    for block in range(n_theta // step):
        lane = slice(block * step, (block + 1) * step)
        row = 1.0 / (fixed[:, lane] + impedance[:, lane])
        inv = jnp.broadcast_to(row, (each, step))
        inv_inner, inv_outer = inv * has_inner, inv * has_outer
        last_scale = jnp.broadcast_to(row * weight[:, lane], (each, step))
        add = wave[:, lane] + other_wave[:, lane]

        def row_of(i):
            i -= HALO
            if 0 <= i < cells_radius:
                return modes[i * each : (i + 1) * each, lane]
            odd_one, even_one = (pair, link) if i < 0 else (link, pair)
            i = i + HALO if i < 0 else i - cells_radius
            rows = slice(i * each, (i + 1) * each)
            return jnp.where(radial_odd, odd_one[rows, lane], even_one[rows, lane])

        def scale_of(i):
            if i < HALO:
                return inv_inner
            return inv if i < HALO + cells_radius else inv_outer

        right = [row_of(i) + add for i in range(total)]
        x = [right[i] * scale_of(i) for i in range(total)]
        for sweep in range(1, SWEEPS):
            fresh = [None] * total
            for i in range(sweep, total - sweep):
                scale = last_scale if sweep == SWEEPS - 1 else scale_of(i)
                fresh[i] = (right[i] + (x[i + 1] + x[i - 1]) + eigen * x[i]) * scale
            x = fresh
        for i in range(cells_radius):
            solved[i * each : (i + 1) * each, lane] = x[i + HALO]

    sectors, _, width = send.shape
    outs, at = [], 0
    for pieces in table_parts(table):
        lane = slice(at, at + pieces[0].shape[1])
        outs.append(product(split(solved[:, lane]), pieces, NT))
        at = lane.stop
    both, apart, odd = outs
    even = jnp.concatenate([both + apart, both - apart], 1)
    for s in range(sectors // 2):
        lane = slice(s * width, (s + 1) * width)
        send[s] = even[:, lane] + odd[:, lane]
        send[s + sectors // 2] = even[:, lane] - odd[:, lane]


def pressure_kernel(received, basis, pressure_out, pressure, sems):
    sectors = received.shape[0]
    cells_radius = pressure.shape[1]
    own = received.shape[1] // cells_radius
    high, low = split(basis[...])
    right = jnp.concatenate(
        [jnp.concatenate([high, low], 1), jnp.concatenate([high, jnp.zeros_like(low)], 1)], 0
    )
    cells_axial = high.shape[1]
    copies = []
    for r in range(cells_radius):
        rows = [received[d, r * own : (r + 1) * own, :] for d in range(sectors)]
        modes = jnp.concatenate(rows, 0)
        left = jnp.concatenate(split(modes.T), 1)
        out = lax.dot_general(left, right, (NN, ((), ())), preferred_element_type=F32)
        pressure[:, r, :] = out[:, :cells_axial] + out[:, cells_axial:]
        if r % 8 == 7:
            rows = pl.ds(r - 7, 8)
            copy = pltpu.make_async_copy(
                pressure.at[:, rows, :], pressure_out.at[:, rows, :], sems.at[r // 8]
            )
            copy.start()
            copies.append(copy)
    for copy in copies:
        copy.wait()


def impedance_kernel(impedance, _, rows):
    half = impedance.shape[1] - 1
    count = half // 4
    pieces, rest = [], jnp.broadcast_to(impedance[:, :half], (8, half))
    for _ in range(3):
        piece = rest.astype(BF16)
        pieces.append(piece)
        rest = rest - piece.astype(F32)
    index = lax.broadcasted_iota(jnp.int32, (half, count), 0)
    target = 4 * lax.broadcasted_iota(jnp.int32, (half, count), 1)
    by_four = []
    for q in range(4):
        pick = (index == target + q).astype(F32).astype(BF16)
        parts = [
            lax.dot_general(piece, pick, (NN, ((), ())), preferred_element_type=F32)
            for piece in pieces
        ]
        by_four.append((parts[0] + (parts[1] + parts[2]))[:1])
    q0, q1, q2, q3 = by_four
    lanes = lax.broadcasted_iota(jnp.int32, (1, count), 1)
    last = jnp.broadcast_to(impedance[:, half:], (1, count))
    rows[...] = jnp.concatenate([q0, jnp.where(lanes == 0, last, q0), q2, q2, q1, q3, q1, q3], 1)


def add_kernel(left, right, out):
    out[...] = left[...] + right[...]


def step_kernel(
    n_theta, mouth_azimuth, mouth_radius, density, swirl, radial_pair, radial_link, sector_pair,
    sector_link, density_next, forcing
):
    flow_rows(n_theta, mouth_azimuth, mouth_radius, density, swirl, forcing)
    add_halos(forcing, radial_pair, radial_link, sector_pair, sector_link)
    density_next[...] = density[...] + time_step * forcing[...]


def call(kernel, outs, ins, scratch=(), limit=12 * 1024 * 1024, **more):
    moved = sum(math.prod(o.shape) * 4 for o in outs)
    return pl.pallas_call(
        kernel,
        out_shape=outs,
        in_specs=ins,
        out_specs=more.pop("out_specs", [VMEM] * len(outs)),
        scratch_shapes=list(scratch),
        cost_estimate=pl.CostEstimate(flops=0, bytes_accessed=3 * moved, transcendentals=0),
        compiler_params=pltpu.CompilerParams(vmem_limit_bytes=limit),
        **more,
    )


def shape(*dims):
    return jax.ShapeDtypeStruct(dims, F32)


def paired(pair, link, axis, closed):
    count = lax.axis_size(axis)
    first = [(i, i ^ 1) for i in range(count)]
    second = [(i, (i + 1) % count) for i in range(1, count if closed else count - 1, 2)]
    second += [(j, i) for i, j in second]
    return lax.ppermute(pair, axis, first), lax.ppermute(link, axis, second)


def swapped(value, axis, bits):
    return lax.ppermute(value, axis, [(i, i ^ bits) for i in range(lax.axis_size(axis))])


def halves_of_sum(value, axis):
    step = 1
    while True:
        other = swapped(value, axis, step)
        step *= 2
        if step >= lax.axis_size(axis):
            return value, other
        value = added(value, other)


def added(left, right):
    return call(add_kernel, [shape(*left.shape)], [VMEM] * 2, limit=4 * 1024 * 1024)(left, right)[0]


def in_hbm(value):
    return pltpu.with_memory_space_constraint(value, pltpu.HBM)


def in_vmem(value):
    return pltpu.with_memory_space_constraint(value, pltpu.VMEM)


def exchanged(value):
    return lax.all_to_all(value, "sector", split_axis=0, concat_axis=0, tiled=True)


def section(density, swirl, heat_rate, acoustic, mode_impedance, mouth_azimuth, mouth_radius):
    sectors = lax.axis_size("sector")
    radials = lax.axis_size("radial")
    cells_theta, cells_radius, cells_axial = density.shape
    n_theta = cells_theta * sectors
    n_radius = cells_radius * radials
    own = cells_axial // sectors
    columns = cells_radius * own
    edge = HALO * own

    basis, eigen = axial_tables(cells_axial)
    basis = jnp.asarray(basis.astype(np.float32))
    eigen = jnp.asarray(
        np.broadcast_to(eigen.reshape(sectors, own, 1), (sectors, own, 128)).astype(np.float32)
    )
    parts = [halves(table) for table in azimuth_tables(n_theta)]
    table = jnp.asarray(
        np.concatenate(
            [np.concatenate(parts[0] + parts[1], 1), np.concatenate(parts[2], 1)], 0
        )
    )
    fixed, weight = diagonal_tables(n_theta)
    fixed, weight = jnp.asarray(fixed)[None, :], jnp.asarray(weight)[None, :]
    (impedance,) = call(impedance_kernel, [shape(1, n_theta)], [VMEM] * 2)(
        mode_impedance[None, :], table
    )

    packed = 2 * cells_radius + 4 * EDGE
    row_block = shape(cells_theta, cells_axial)
    pair, link = call(
        edges_kernel,
        [shape(packed, cells_axial)] * 2,
        [HBM] * 4,
        [
            pltpu.VMEM((2, EDGE, cells_radius, cells_axial), F32),
            pltpu.VMEM((2, EDGE, cells_radius, cells_axial), F32),
            pltpu.VMEM((2, 1, cells_radius, cells_axial), F32),
            pltpu.VMEM((2, 3, EDGE, cells_axial), F32),
            pltpu.SemaphoreType.DMA((8,)),
        ],
    )(*[in_hbm(value) for value in (density, swirl, heat_rate, acoustic)])
    sector_halo = paired(pair, link, "sector", True)
    edge_rows = pair
    partial, heat, pair, link = call(
        lambda *refs: flow_kernel(n_theta, *refs),
        [shape(*density.shape)] + [row_block] * 3,
        [SMEM] * 2 + [VMEM] * 3 + [HBM],
    )(mouth_azimuth, mouth_radius, density, swirl, heat_rate, edge_rows)
    radial_halo = paired(pair, link, "radial", False)
    state, send = call(
        lambda *refs: first_kernel(n_radius, *refs),
        [
            pltpu.HBM(acoustic.shape, F32),
            pltpu.HBM((sectors, columns + own, cells_theta), F32),
        ],
        [VMEM] * 8,
        [
            pltpu.VMEM(density.shape, F32),
            pltpu.VMEM(acoustic.shape, F32),
            pltpu.VMEM((sectors, columns + own, cells_theta), F32),
            pltpu.SemaphoreType.DMA((2 + cells_radius // GROUP,)),
        ],
        out_specs=[HBM, HBM],
    )(partial, heat, acoustic, *radial_halo, *sector_halo, basis)
    received = exchanged(send)
    (density_next,) = call(
        lambda *refs: step_kernel(n_theta, *refs),
        [shape(*density.shape)],
        [SMEM] * 2 + [VMEM] * 6,
        [pltpu.VMEM(density.shape, F32)],
    )(mouth_azimuth, mouth_radius, density, swirl, *radial_halo, *sector_halo)
    acoustic_next = added(*halves_of_sum(state, "radial"))

    modes, pair, link, wave = call(
        lambda *refs: forward_kernel(edge, *refs),
        [shape(columns, n_theta)] + [shape(edge, n_theta)] * 2 + [shape(own, n_theta)],
        [VMEM] * 2 + [HBM] * 3,
    )(in_vmem(received), table, in_hbm(density_next), in_hbm(acoustic_next), impedance)
    (send,) = call(
        solve_kernel,
        [shape(sectors, columns, cells_theta)],
        [VMEM] * 10,
        [pltpu.VMEM((columns, n_theta), F32)],
    )(
        modes, *paired(pair, link, "radial", False), *halves_of_sum(wave, "radial"), impedance,
        fixed, weight, eigen, table,
    )
    (pressure,) = call(
        pressure_kernel,
        [shape(*density.shape)],
        [VMEM] * 2,
        [pltpu.VMEM(density.shape, F32), pltpu.SemaphoreType.DMA((cells_radius // 8,))],
        out_specs=[HBM],
    )(exchanged(send), basis)
    return density_next, pressure, acoustic_next


def solution(mesh):
    return jax.shard_map(
        section,
        mesh=mesh,
        in_specs=(
            P("sector", "radial", None),
            P("sector", "radial", None),
            P("sector", "radial", None),
            P(None, "sector", None),
            P(),
            P(),
            P(),
        ),
        out_specs=(
            P("sector", "radial", None),
            P("sector", "radial", None),
            P(None, "sector", None),
        ),
        check_vma=False,
    )
```

```python
import math

import jax
import jax.numpy as jnp
import numpy as np
from jax import lax
from jax.experimental import pallas as pl
from jax.experimental.pallas import tpu as pltpu
from jax.sharding import PartitionSpec as P


BURNERS = 16
MOUTH = 8
SWEEPS = 4
SUBSTEPS = 8

time_step = 0.2
diffusion = 0.05
inflow_rate = 0.5
wave_speed = 0.5
heat_coupling = 0.5
feedback = 0.5

F32 = jnp.float32
BF16 = jnp.bfloat16
HALO = SWEEPS - 1
EDGE = 8
VMEM = pl.BlockSpec(memory_space=pltpu.VMEM)
SMEM = pl.BlockSpec(memory_space=pltpu.SMEM)
HBM = pl.BlockSpec(memory_space=pltpu.HBM)


def halves(table):
    high = table.astype(BF16)
    low = (table - high.astype(np.float64)).astype(BF16)
    return high, low


def axial_tables(cells):
    index = np.arange(1, cells + 1, dtype=np.float64)
    basis = math.sqrt(2.0 / (cells + 1)) * np.sin(
        np.pi * ((index[:, None] * index[None, :]) % (2 * (cells + 1))) / (cells + 1)
    )
    return basis, 2.0 * np.cos(np.pi * index / (cells + 1))


def mode_classes(n_theta):
    half = n_theta // 2
    multiples = np.arange(0, half, 4)
    first = (
        np.concatenate([multiples, [half], multiples[1:]]),
        np.concatenate([np.zeros(len(multiples) + 1), np.ones(len(multiples) - 1)]),
    )
    twos = np.arange(2, half, 4)
    second = (np.concatenate([twos, twos]), np.repeat([0, 1], len(twos)))
    ones, threes = np.arange(1, half, 4), np.arange(3, half, 4)
    third = (np.concatenate([ones, threes, ones, threes]), np.repeat([0, 1], half // 2))
    return first, second, third


def azimuth_tables(n_theta):
    bases = []
    for (order, odd), rows in zip(mode_classes(n_theta), (n_theta // 4, n_theta // 4, n_theta // 2)):
        phase = (np.arange(rows)[:, None] * order[None, :].astype(np.int64)) % n_theta
        angle = phase * (2.0 * np.pi / n_theta)
        bases.append(np.where(odd[None, :] == 0, np.cos(angle), np.sin(angle)))
    return bases


def diagonal_tables(n_theta):
    half = n_theta // 2
    order = np.concatenate([part[0] for part in mode_classes(n_theta)])
    shifted = 2.0 - 2.0 * np.cos(order * (2.0 * np.pi / n_theta))
    weight = np.where((order == 0) | (order == half), 1.0, 2.0) / n_theta
    return (4.0 + shifted).astype(np.float32), weight.astype(np.float32)


def split(value):
    high = value.astype(BF16)
    return high, (value - high.astype(F32)).astype(BF16)


def product(left, right, dims):
    def one(a, b):
        return lax.dot_general(a, b, (dims, ((), ())), preferred_element_type=F32)

    return one(left[0], right[0]) + (one(left[1], right[0]) + one(left[0], right[1]))


NN = ((1,), (0,))
NT = ((1,), (1,))


def edges_kernel(density, swirl, heat_rate, acoustic, pair, link, rho, rate, spin, wave, sems):
    cells_theta, cells_radius, _ = density.shape
    odd = lax.axis_index("sector") % 2
    copies = []

    def fetch(source, target):
        copy = pltpu.make_async_copy(source, target, sems.at[len(copies)])
        copy.start()
        copies.append(copy)

    for side, begin, row in ((0, 0, 0), (1, cells_theta - EDGE, cells_theta - 1)):
        fetch(density.at[pl.ds(begin, EDGE)], rho.at[side])
        fetch(heat_rate.at[pl.ds(begin, EDGE)], rate.at[side])
        fetch(swirl.at[pl.ds(row, 1)], spin.at[side])
        fetch(acoustic.at[:, pl.ds(begin, EDGE)], wave.at[side])
    for copy in copies:
        copy.wait()
    for out, side in ((pair, 1 - odd), (link, odd)):
        edge = jnp.where(side == 0, rho[0, 0], rho[1, EDGE - 1])
        out[0:cells_radius] = edge
        out[cells_radius : 2 * cells_radius] = edge * spin[side, 0]
        at = 2 * cells_radius
        for k in range(3):
            out[at : at + EDGE] = wave[side, k]
            at += EDGE
        heat = jnp.sum(rate[side] * rho[side] * rho[side], axis=1)
        out[at : at + EDGE] = heat


def flow_rows(n_theta, mouth_azimuth, mouth_radius, density, swirl, forcing):
    sector = lax.axis_index("sector")
    radial = lax.axis_index("radial")
    cells_theta, cells_radius, cells_axial = density.shape
    shape = (cells_radius, cells_axial)
    rows = lax.broadcasted_iota(jnp.int32, shape, 0)
    lanes = lax.broadcasted_iota(jnp.int32, shape, 1)
    segment = n_theta // BURNERS
    part = min(segment, cells_theta)
    zero = jnp.zeros(shape, F32)

    def at(t):
        if t < 0 or t >= cells_theta:
            return zero, zero
        rho = density[t]
        return rho, rho * swirl[t]

    window = [at(-1), at(0)]
    for t in range(cells_theta):
        window.append(at(t + 1))
        (rho_down, flux_down), (rho, _), (rho_up, flux_up) = window
        window = window[1:]
        if t % part == 0:
            burner = (sector * cells_theta + t) // segment
            start = burner * segment + mouth_azimuth[burner] - sector * cells_theta
            radius = mouth_radius[burner] - radial * cells_radius
            mouth = ((rows >= radius) & (rows < radius + MOUTH)).astype(F32)
            mouth = mouth * (inflow_rate / time_step)
        gain = mouth * ((start <= t) & (t < start + MOUTH)).astype(F32)
        r_up = jnp.where(rows == cells_radius - 1, 0.0, pltpu.roll(rho, cells_radius - 1, 0))
        r_down = jnp.where(rows == 0, 0.0, pltpu.roll(rho, 1, 0))
        z_up = jnp.where(lanes == cells_axial - 1, 0.0, pltpu.roll(rho, cells_axial - 1, 1))
        z_down = jnp.where(lanes == 0, 0.0, pltpu.roll(rho, 1, 1))
        twice = 2.0 * rho
        laplace = (rho_up + rho_down - twice) + (r_up + r_down - twice) + (z_up + z_down - twice)
        forcing[t] = -0.5 * (flux_up - flux_down) + diffusion * laplace + gain * (1.0 - rho)


def add_halos(forcing, radial_pair, radial_link, sector_pair, sector_link):
    radials = lax.axis_size("radial")
    radial = lax.axis_index("radial")
    cells_theta, cells_radius, _ = forcing.shape
    odd = lax.axis_index("sector") % 2 == 1
    above = jnp.where(odd, sector_link[...], sector_pair[...])
    below = jnp.where(odd, sector_pair[...], sector_link[...])
    odd = radial % 2 == 1
    inner = jnp.where(odd, radial_pair[...], radial_link[...])
    outer = jnp.where(odd, radial_link[...], radial_pair[...])
    rho, flux = slice(0, cells_radius), slice(cells_radius, 2 * cells_radius)
    end = cells_theta - 1
    forcing[0] = forcing[0] + (0.5 * below[flux] + diffusion * below[rho])
    forcing[end] = forcing[end] + (diffusion * above[rho] - 0.5 * above[flux])
    inside = diffusion * (radial > 0).astype(F32)
    outside = diffusion * (radial < radials - 1).astype(F32)
    forcing[:, 0, :] = forcing[:, 0, :] + inside * inner
    forcing[:, cells_radius - 1, :] = forcing[:, cells_radius - 1, :] + outside * outer
    return above, below


def flow_kernel(
    n_theta, mouth_azimuth, mouth_radius, density, swirl, heat_rate, _, forcing, heat, pair, link
):
    cells_theta, cells_radius, _ = density.shape
    odd = lax.axis_index("radial") % 2 == 1
    first, last = density[:, 0, :], density[:, cells_radius - 1, :]
    pair[...] = jnp.where(odd, first, last)
    link[...] = jnp.where(odd, last, first)
    flow_rows(n_theta, mouth_azimuth, mouth_radius, density, swirl, forcing)
    for t in range(0, cells_theta, 8):
        rho = density[t : t + 8]
        heat[t : t + 8] = jnp.sum(heat_rate[t : t + 8] * rho * rho, axis=1)


def sine_modes(basis, fields):
    high, low = split(basis)
    count = high.shape[0]
    left = jnp.concatenate(
        [jnp.concatenate([high, high], 1), jnp.concatenate([low, jnp.zeros_like(low)], 1)], 0
    )
    right = jnp.concatenate([jnp.concatenate(split(field), 1) for field in fields], 0)
    out = lax.dot_general(left, right, (NT, ((), ())), preferred_element_type=F32)
    return out[:count] + out[count:]


GROUP = 4


def first_kernel(
    n_radius, partial, heat, acoustic, radial_pair, radial_link, sector_pair, sector_link, basis,
    state, send, forcing, following, staged, sems
):
    radial = lax.axis_index("radial")
    cells_theta, cells_radius, cells_axial = partial.shape
    sectors = send.shape[0]
    own = cells_axial // sectors
    forcing[...] = partial[...]
    above, below = add_halos(forcing, radial_pair, radial_link, sector_pair, sector_link)
    copies = []

    def leave(begin, count):
        rows = pl.ds(begin, count)
        copy = pltpu.make_async_copy(
            staged.at[:, rows, :], send.at[:, rows, :], sems.at[len(copies)]
        )
        copy.start()
        copies.append(copy)

    mine = basis[...]
    for r in range(0, cells_radius, GROUP):
        modes = sine_modes(mine, [forcing[:, r + i, :] for i in range(GROUP)])
        for i in range(GROUP):
            lane = slice(i * cells_theta, (i + 1) * cells_theta)
            for d in range(sectors):
                staged[d, (r + i) * own : (r + i + 1) * own, :] = modes[
                    d * own : (d + 1) * own, lane
                ]
        leave(r * own, GROUP * own)

    share = (radial == 0).astype(F32)
    skip = 2 * cells_radius

    def extended(k):
        rows = slice(skip + k * EDGE, skip + (k + 1) * EDGE)
        middle = acoustic[k] if k < 3 else heat[...]
        return jnp.concatenate([below[rows], middle, above[rows]], 0)

    press, along, axial = extended(0) * share, extended(1) * share, extended(2) * share
    warm = extended(3) * (heat_coupling / n_radius)
    count = press.shape[0]
    lanes = lax.broadcasted_iota(jnp.int32, press.shape, 1)
    for _ in range(SUBSTEPS):
        press_up = pltpu.roll(press, count - 1, 0)
        press_axial = jnp.where(lanes == cells_axial - 1, 0.0, pltpu.roll(press, cells_axial - 1, 1))
        along = along - wave_speed * (press_up - press)
        axial = axial - wave_speed * (press_axial - press)
        along_down = pltpu.roll(along, 1, 0)
        axial_down = jnp.where(lanes == 0, 0.0, pltpu.roll(axial, 1, 1))
        press = press - wave_speed * ((along - along_down) + (axial - axial_down)) + warm
    middle = slice(EDGE, EDGE + cells_theta)
    following[0] = press[middle]
    following[1] = along[middle]
    following[2] = axial[middle]
    copies.append(pltpu.make_async_copy(following, state, sems.at[len(copies)]))
    copies[-1].start()
    modes = sine_modes(mine, [feedback * press[middle]])
    columns = cells_radius * own
    for d in range(sectors):
        staged[d, columns : columns + own, :] = modes[d * own : (d + 1) * own]
    leave(columns, own)
    for copy in copies:
        copy.wait()


def transformed(values, table, store):
    sectors = len(values)
    quarter, half = sectors // 4, sectors // 2

    def joined(parts):
        return jnp.concatenate(parts, 1) if len(parts) > 1 else parts[0]

    even = [values[s] + values[s + half] for s in range(half)]
    odd = [values[s] - values[s + half] for s in range(half)]
    both = [even[s] + even[s + quarter] for s in range(quarter)]
    apart = [even[s] - even[s + quarter] for s in range(quarter)]
    at = 0
    for parts, pieces in zip((both, apart, odd), table_parts(table)):
        width = pieces[0].shape[1]
        store(slice(at, at + width), product(split(joined(parts)), pieces, NN))
        at += width


def table_parts(table):
    n_theta = table.shape[1]
    quarter, half = n_theta // 4, n_theta // 2
    top, bottom = slice(0, quarter), slice(quarter, quarter + half)
    columns = [slice(i * quarter, (i + 1) * quarter) for i in range(4)]
    return (
        (table[top, columns[0]], table[top, columns[1]]),
        (table[top, columns[2]], table[top, columns[3]]),
        (table[bottom, :half], table[bottom, half:]),
    )


def forward_kernel(edge, received, table, *refs):
    modes, pair, link, wave = refs[-4:]
    sectors = received.shape[0]
    columns = modes.shape[0]
    radial_odd = lax.axis_index("radial") % 2 == 1

    def store(lane, out):
        modes[:, lane] = out[:columns]
        first, last = out[:edge], out[columns - edge : columns]
        pair[:edge, lane] = jnp.where(radial_odd, first, last)
        link[:edge, lane] = jnp.where(radial_odd, last, first)
        wave[:, lane] = out[columns:]
        if pair.shape[0] > edge:
            pair[edge:, lane] = out[columns:]
            link[edge:, lane] = out[columns:]

    transformed([received[s] for s in range(sectors)], table, store)


def solve_kernel(
    modes, pair, link, wave, other_wave, impedance, fixed, weight, axial, table, send, solved
):
    radials = lax.axis_size("radial")
    radial = lax.axis_index("radial")
    sector = lax.axis_index("sector")
    columns, n_theta = modes.shape
    each = axial.shape[1]
    cells_radius = columns // each
    has_inner = (radial > 0).astype(F32)
    has_outer = (radial < radials - 1).astype(F32)
    radial_odd = radial % 2 == 1
    eigen = axial[sector]
    step = eigen.shape[1]
    total = cells_radius + 2 * HALO
    for block in range(n_theta // step):
        lane = slice(block * step, (block + 1) * step)
        row = 1.0 / (fixed[:, lane] + impedance[:, lane])
        inv = jnp.broadcast_to(row, (each, step))
        inv_inner, inv_outer = inv * has_inner, inv * has_outer
        last_scale = jnp.broadcast_to(row * weight[:, lane], (each, step))
        add = wave[:, lane] + other_wave[:, lane]
        edge = HALO * each
        if pair.shape[0] > edge:
            add = add + (pair[edge:, lane] + link[edge:, lane])

        def row_of(i):
            i -= HALO
            if 0 <= i < cells_radius:
                return modes[i * each : (i + 1) * each, lane]
            odd_one, even_one = (pair, link) if i < 0 else (link, pair)
            i = i + HALO if i < 0 else i - cells_radius
            rows = slice(i * each, (i + 1) * each)
            return jnp.where(radial_odd, odd_one[rows, lane], even_one[rows, lane])

        def scale_of(i):
            if i < HALO:
                return inv_inner
            return inv if i < HALO + cells_radius else inv_outer

        right = [row_of(i) + add for i in range(total)]
        x = [right[i] * scale_of(i) for i in range(total)]
        for sweep in range(1, SWEEPS):
            fresh = [None] * total
            for i in range(sweep, total - sweep):
                scale = last_scale if sweep == SWEEPS - 1 else scale_of(i)
                fresh[i] = (right[i] + (x[i + 1] + x[i - 1]) + eigen * x[i]) * scale
            x = fresh
        for i in range(cells_radius):
            solved[i * each : (i + 1) * each, lane] = x[i + HALO]

    sectors, _, width = send.shape
    outs, at = [], 0
    for pieces in table_parts(table):
        lane = slice(at, at + pieces[0].shape[1])
        outs.append(product(split(solved[:, lane]), pieces, NT))
        at = lane.stop
    both, apart, odd = outs
    even = jnp.concatenate([both + apart, both - apart], 1)
    for s in range(sectors // 2):
        lane = slice(s * width, (s + 1) * width)
        send[s] = even[:, lane] + odd[:, lane]
        send[s + sectors // 2] = even[:, lane] - odd[:, lane]


def pressure_kernel(received, basis, pressure_out, pressure, sems):
    sectors = received.shape[0]
    cells_radius = pressure.shape[1]
    own = received.shape[1] // cells_radius
    high, low = split(basis[...])
    right = jnp.concatenate(
        [jnp.concatenate([high, low], 1), jnp.concatenate([high, jnp.zeros_like(low)], 1)], 0
    )
    cells_axial = high.shape[1]
    copies = []
    for r in range(cells_radius):
        rows = [received[d, r * own : (r + 1) * own, :] for d in range(sectors)]
        modes = jnp.concatenate(rows, 0)
        left = jnp.concatenate(split(modes.T), 1)
        out = lax.dot_general(left, right, (NN, ((), ())), preferred_element_type=F32)
        pressure[:, r, :] = out[:, :cells_axial] + out[:, cells_axial:]
        if r % 8 == 7:
            rows = pl.ds(r - 7, 8)
            copy = pltpu.make_async_copy(
                pressure.at[:, rows, :], pressure_out.at[:, rows, :], sems.at[r // 8]
            )
            copy.start()
            copies.append(copy)
    for copy in copies:
        copy.wait()


def impedance_kernel(impedance, _, rows):
    half = impedance.shape[1] - 1
    count = half // 4
    pieces, rest = [], jnp.broadcast_to(impedance[:, :half], (8, half))
    for _ in range(3):
        piece = rest.astype(BF16)
        pieces.append(piece)
        rest = rest - piece.astype(F32)
    index = lax.broadcasted_iota(jnp.int32, (half, count), 0)
    target = 4 * lax.broadcasted_iota(jnp.int32, (half, count), 1)
    by_four = []
    for q in range(4):
        pick = (index == target + q).astype(F32).astype(BF16)
        parts = [
            lax.dot_general(piece, pick, (NN, ((), ())), preferred_element_type=F32)
            for piece in pieces
        ]
        by_four.append((parts[0] + (parts[1] + parts[2]))[:1])
    q0, q1, q2, q3 = by_four
    lanes = lax.broadcasted_iota(jnp.int32, (1, count), 1)
    last = jnp.broadcast_to(impedance[:, half:], (1, count))
    rows[...] = jnp.concatenate([q0, jnp.where(lanes == 0, last, q0), q2, q2, q1, q3, q1, q3], 1)


def add_kernel(left, right, out):
    out[...] = left[...] + right[...]


def step_kernel(
    n_theta, mouth_azimuth, mouth_radius, density, swirl, radial_pair, radial_link, sector_pair,
    sector_link, density_next, forcing
):
    flow_rows(n_theta, mouth_azimuth, mouth_radius, density, swirl, forcing)
    add_halos(forcing, radial_pair, radial_link, sector_pair, sector_link)
    density_next[...] = density[...] + time_step * forcing[...]


def call(kernel, outs, ins, scratch=(), limit=12 * 1024 * 1024, **more):
    moved = sum(math.prod(o.shape) * 4 for o in outs)
    return pl.pallas_call(
        kernel,
        out_shape=outs,
        in_specs=ins,
        out_specs=more.pop("out_specs", [VMEM] * len(outs)),
        scratch_shapes=list(scratch),
        cost_estimate=pl.CostEstimate(flops=0, bytes_accessed=3 * moved, transcendentals=0),
        compiler_params=pltpu.CompilerParams(vmem_limit_bytes=limit),
        **more,
    )


def shape(*dims):
    return jax.ShapeDtypeStruct(dims, F32)


def paired(pair, link, axis, closed):
    count = lax.axis_size(axis)
    first = [(i, i ^ 1) for i in range(count)]
    second = [(i, (i + 1) % count) for i in range(1, count if closed else count - 1, 2)]
    second += [(j, i) for i, j in second]
    return lax.ppermute(pair, axis, first), lax.ppermute(link, axis, second)


def swapped(value, axis, bits):
    return lax.ppermute(value, axis, [(i, i ^ bits) for i in range(lax.axis_size(axis))])


def halves_of_sum(value, axis):
    step = 1
    while True:
        other = swapped(value, axis, step)
        step *= 2
        if step >= lax.axis_size(axis):
            return value, other
        value = added(value, other)


def added(left, right):
    return call(add_kernel, [shape(*left.shape)], [VMEM] * 2, limit=4 * 1024 * 1024)(left, right)[0]


def in_hbm(value):
    return pltpu.with_memory_space_constraint(value, pltpu.HBM)


def in_vmem(value):
    return pltpu.with_memory_space_constraint(value, pltpu.VMEM)


def exchanged(value):
    return lax.all_to_all(value, "sector", split_axis=0, concat_axis=0, tiled=True)


def section(density, swirl, heat_rate, acoustic, mode_impedance, mouth_azimuth, mouth_radius):
    sectors = lax.axis_size("sector")
    radials = lax.axis_size("radial")
    cells_theta, cells_radius, cells_axial = density.shape
    n_theta = cells_theta * sectors
    n_radius = cells_radius * radials
    own = cells_axial // sectors
    columns = cells_radius * own
    edge = HALO * own

    basis, eigen = axial_tables(cells_axial)
    basis = jnp.asarray(basis.astype(np.float32))
    eigen = jnp.asarray(
        np.broadcast_to(eigen.reshape(sectors, own, 1), (sectors, own, 128)).astype(np.float32)
    )
    parts = [halves(table) for table in azimuth_tables(n_theta)]
    table = jnp.asarray(
        np.concatenate(
            [np.concatenate(parts[0] + parts[1], 1), np.concatenate(parts[2], 1)], 0
        )
    )
    fixed, weight = diagonal_tables(n_theta)
    fixed, weight = jnp.asarray(fixed)[None, :], jnp.asarray(weight)[None, :]
    (impedance,) = call(impedance_kernel, [shape(1, n_theta)], [VMEM] * 2)(
        mode_impedance[None, :], table
    )

    packed = 2 * cells_radius + 4 * EDGE
    row_block = shape(cells_theta, cells_axial)
    pair, link = call(
        edges_kernel,
        [shape(packed, cells_axial)] * 2,
        [HBM] * 4,
        [
            pltpu.VMEM((2, EDGE, cells_radius, cells_axial), F32),
            pltpu.VMEM((2, EDGE, cells_radius, cells_axial), F32),
            pltpu.VMEM((2, 1, cells_radius, cells_axial), F32),
            pltpu.VMEM((2, 3, EDGE, cells_axial), F32),
            pltpu.SemaphoreType.DMA((8,)),
        ],
    )(*[in_hbm(value) for value in (density, swirl, heat_rate, acoustic)])
    sector_halo = paired(pair, link, "sector", True)
    edge_rows = pair
    partial, heat, pair, link = call(
        lambda *refs: flow_kernel(n_theta, *refs),
        [shape(*density.shape)] + [row_block] * 3,
        [SMEM] * 2 + [VMEM] * 3 + [HBM],
    )(mouth_azimuth, mouth_radius, density, swirl, heat_rate, edge_rows)
    radial_halo = paired(pair, link, "radial", False)
    state, send = call(
        lambda *refs: first_kernel(n_radius, *refs),
        [
            pltpu.HBM(acoustic.shape, F32),
            pltpu.HBM((sectors, columns + own, cells_theta), F32),
        ],
        [VMEM] * 8,
        [
            pltpu.VMEM(density.shape, F32),
            pltpu.VMEM(acoustic.shape, F32),
            pltpu.VMEM((sectors, columns + own, cells_theta), F32),
            pltpu.SemaphoreType.DMA((2 + cells_radius // GROUP,)),
        ],
        out_specs=[HBM, HBM],
    )(partial, heat, acoustic, *radial_halo, *sector_halo, basis)
    received = exchanged(send)
    (density_next,) = call(
        lambda *refs: step_kernel(n_theta, *refs),
        [shape(*density.shape)],
        [SMEM] * 2 + [VMEM] * 6,
        [pltpu.VMEM(density.shape, F32)],
    )(mouth_azimuth, mouth_radius, density, swirl, *radial_halo, *sector_halo)
    acoustic_next = added(*halves_of_sum(state, "radial"))

    direct = radials == 4
    message = edge + own if direct else edge
    modes, pair, link, wave = call(
        lambda *refs: forward_kernel(edge, *refs),
        [shape(columns, n_theta)] + [shape(message, n_theta)] * 2 + [shape(own, n_theta)],
        [VMEM] * 2 + [HBM] * 3,
    )(in_vmem(received), table, in_hbm(density_next), in_hbm(acoustic_next), impedance)
    halo = paired(pair, link, "radial", direct)
    waves = (wave, swapped(wave, "radial", 2)) if direct else halves_of_sum(wave, "radial")
    (send,) = call(
        solve_kernel,
        [shape(sectors, columns, cells_theta)],
        [VMEM] * 10,
        [pltpu.VMEM((columns, n_theta), F32)],
    )(modes, *halo, *waves, impedance, fixed, weight, eigen, table)
    (pressure,) = call(
        pressure_kernel,
        [shape(*density.shape)],
        [VMEM] * 2,
        [pltpu.VMEM(density.shape, F32), pltpu.SemaphoreType.DMA((cells_radius // 8,))],
        out_specs=[HBM],
    )(exchanged(send), basis)
    return density_next, pressure, acoustic_next


def solution(mesh):
    return jax.shard_map(
        section,
        mesh=mesh,
        in_specs=(
            P("sector", "radial", None),
            P("sector", "radial", None),
            P("sector", "radial", None),
            P(None, "sector", None),
            P(),
            P(),
            P(),
        ),
        out_specs=(
            P("sector", "radial", None),
            P("sector", "radial", None),
            P(None, "sector", None),
        ),
        check_vma=False,
    )
```

```python
import math

import jax
import jax.numpy as jnp
import numpy as np
from jax import lax
from jax.experimental import pallas as pl
from jax.experimental.pallas import tpu as pltpu
from jax.sharding import PartitionSpec as P


BURNERS = 16
MOUTH = 8
SWEEPS = 4
SUBSTEPS = 8

time_step = 0.2
diffusion = 0.05
inflow_rate = 0.5
wave_speed = 0.5
heat_coupling = 0.5
feedback = 0.5

F32 = jnp.float32
BF16 = jnp.bfloat16
HALO = SWEEPS - 1
EDGE = 8
VMEM = pl.BlockSpec(memory_space=pltpu.VMEM)
SMEM = pl.BlockSpec(memory_space=pltpu.SMEM)
HBM = pl.BlockSpec(memory_space=pltpu.HBM)


def halves(table):
    high = table.astype(BF16)
    low = (table - high.astype(np.float64)).astype(BF16)
    return high, low


def axial_tables(cells):
    index = np.arange(1, cells + 1, dtype=np.float64)
    basis = math.sqrt(2.0 / (cells + 1)) * np.sin(
        np.pi * ((index[:, None] * index[None, :]) % (2 * (cells + 1))) / (cells + 1)
    )
    return basis, 2.0 * np.cos(np.pi * index / (cells + 1))


def mode_classes(n_theta):
    half = n_theta // 2
    multiples = np.arange(0, half, 4)
    first = (
        np.concatenate([multiples, [half], multiples[1:]]),
        np.concatenate([np.zeros(len(multiples) + 1), np.ones(len(multiples) - 1)]),
    )
    twos = np.arange(2, half, 4)
    second = (np.concatenate([twos, twos]), np.repeat([0, 1], len(twos)))
    ones, threes = np.arange(1, half, 4), np.arange(3, half, 4)
    third = (np.concatenate([ones, threes, ones, threes]), np.repeat([0, 1], half // 2))
    return first, second, third


def azimuth_tables(n_theta):
    bases = []
    for (order, odd), rows in zip(mode_classes(n_theta), (n_theta // 4, n_theta // 4, n_theta // 2)):
        phase = (np.arange(rows)[:, None] * order[None, :].astype(np.int64)) % n_theta
        angle = phase * (2.0 * np.pi / n_theta)
        bases.append(np.where(odd[None, :] == 0, np.cos(angle), np.sin(angle)))
    return bases


def diagonal_tables(n_theta):
    half = n_theta // 2
    order = np.concatenate([part[0] for part in mode_classes(n_theta)])
    shifted = 2.0 - 2.0 * np.cos(order * (2.0 * np.pi / n_theta))
    weight = np.where((order == 0) | (order == half), 1.0, 2.0) / n_theta
    return (4.0 + shifted).astype(np.float32), weight.astype(np.float32)


def split(value):
    high = value.astype(BF16)
    return high, (value - high.astype(F32)).astype(BF16)


def product(left, right, dims):
    def one(a, b):
        return lax.dot_general(a, b, (dims, ((), ())), preferred_element_type=F32)

    return one(left[0], right[0]) + (one(left[1], right[0]) + one(left[0], right[1]))


NN = ((1,), (0,))
NT = ((1,), (1,))


def edges_kernel(density, swirl, heat_rate, acoustic, pair, link, rho, rate, spin, wave, sems):
    cells_theta, cells_radius, _ = density.shape
    odd = lax.axis_index("sector") % 2
    copies = []

    def fetch(source, target):
        copy = pltpu.make_async_copy(source, target, sems.at[len(copies)])
        copy.start()
        copies.append(copy)

    for side, begin, row in ((0, 0, 0), (1, cells_theta - EDGE, cells_theta - 1)):
        fetch(density.at[pl.ds(begin, EDGE)], rho.at[side])
        fetch(heat_rate.at[pl.ds(begin, EDGE)], rate.at[side])
        fetch(swirl.at[pl.ds(row, 1)], spin.at[side])
        fetch(acoustic.at[:, pl.ds(begin, EDGE)], wave.at[side])
    for copy in copies:
        copy.wait()
    for out, side in ((pair, 1 - odd), (link, odd)):
        edge = jnp.where(side == 0, rho[0, 0], rho[1, EDGE - 1])
        out[0:cells_radius] = edge
        out[cells_radius : 2 * cells_radius] = edge * spin[side, 0]
        at = 2 * cells_radius
        for k in range(3):
            out[at : at + EDGE] = wave[side, k]
            at += EDGE
        heat = jnp.sum(rate[side] * rho[side] * rho[side], axis=1)
        out[at : at + EDGE] = heat


def flat(ref):
    cells_theta, cells_radius, cells_axial = ref.shape
    return ref.reshape(cells_theta * cells_radius, cells_axial)


def plane(shape, r):
    return pl.ds(r, shape[0], stride=shape[1])


def flow_rows(n_theta, mouth_azimuth, mouth_radius, density, swirl, forcing):
    sector = lax.axis_index("sector")
    radial = lax.axis_index("radial")
    cells_theta, cells_radius, cells_axial = density.shape
    shape = (cells_radius, cells_axial)
    rows = lax.broadcasted_iota(jnp.int32, shape, 0)
    lanes = lax.broadcasted_iota(jnp.int32, shape, 1)
    segment = n_theta // BURNERS
    part = min(segment, cells_theta)
    zero = jnp.zeros(shape, F32)

    def at(t):
        if t < 0 or t >= cells_theta:
            return zero, zero
        rho = density[t]
        return rho, rho * swirl[t]

    window = [at(-1), at(0)]
    for t in range(cells_theta):
        window.append(at(t + 1))
        (rho_down, flux_down), (rho, _), (rho_up, flux_up) = window
        window = window[1:]
        if t % part == 0:
            burner = (sector * cells_theta + t) // segment
            start = burner * segment + mouth_azimuth[burner] - sector * cells_theta
            radius = mouth_radius[burner] - radial * cells_radius
            mouth = ((rows >= radius) & (rows < radius + MOUTH)).astype(F32)
            mouth = mouth * (inflow_rate / time_step)
        gain = mouth * ((start <= t) & (t < start + MOUTH)).astype(F32)
        r_up = jnp.where(rows == cells_radius - 1, 0.0, pltpu.roll(rho, cells_radius - 1, 0))
        r_down = jnp.where(rows == 0, 0.0, pltpu.roll(rho, 1, 0))
        z_up = jnp.where(lanes == cells_axial - 1, 0.0, pltpu.roll(rho, cells_axial - 1, 1))
        z_down = jnp.where(lanes == 0, 0.0, pltpu.roll(rho, 1, 1))
        twice = 2.0 * rho
        laplace = (rho_up + rho_down - twice) + (r_up + r_down - twice) + (z_up + z_down - twice)
        forcing[t] = -0.5 * (flux_up - flux_down) + diffusion * laplace + gain * (1.0 - rho)


def add_halos(forcing, radial_pair, radial_link, sector_pair, sector_link):
    radials = lax.axis_size("radial")
    radial = lax.axis_index("radial")
    cells_theta, cells_radius, _ = forcing.shape
    odd = lax.axis_index("sector") % 2 == 1
    above = jnp.where(odd, sector_link[...], sector_pair[...])
    below = jnp.where(odd, sector_pair[...], sector_link[...])
    odd = radial % 2 == 1
    inner = jnp.where(odd, radial_pair[...], radial_link[...])
    outer = jnp.where(odd, radial_link[...], radial_pair[...])
    rho, flux = slice(0, cells_radius), slice(cells_radius, 2 * cells_radius)
    end = cells_theta - 1
    forcing[0] = forcing[0] + (0.5 * below[flux] + diffusion * below[rho])
    forcing[end] = forcing[end] + (diffusion * above[rho] - 0.5 * above[flux])
    inside = diffusion * (radial > 0).astype(F32)
    outside = diffusion * (radial < radials - 1).astype(F32)
    rows = flat(forcing)
    for r, term in ((0, inside * inner), (cells_radius - 1, outside * outer)):
        at = plane(forcing.shape, r)
        rows[at, :] = rows[at, :] + term
    return above, below


def flow_kernel(
    n_theta, mouth_azimuth, mouth_radius, density, swirl, heat_rate, _, forcing, heat, pair, link
):
    cells_theta, cells_radius, _ = density.shape
    odd = lax.axis_index("radial") % 2 == 1
    rows = flat(density)
    first, last = (rows[plane(density.shape, r), :] for r in (0, cells_radius - 1))
    pair[...] = jnp.where(odd, first, last)
    link[...] = jnp.where(odd, last, first)
    flow_rows(n_theta, mouth_azimuth, mouth_radius, density, swirl, forcing)
    for t in range(0, cells_theta, 8):
        rho = density[t : t + 8]
        heat[t : t + 8] = jnp.sum(heat_rate[t : t + 8] * rho * rho, axis=1)


def sine_modes(basis, fields):
    high, low = split(basis)
    count = high.shape[0]
    left = jnp.concatenate(
        [jnp.concatenate([high, high], 1), jnp.concatenate([low, jnp.zeros_like(low)], 1)], 0
    )
    right = jnp.concatenate([jnp.concatenate(split(field), 1) for field in fields], 0)
    out = lax.dot_general(left, right, (NT, ((), ())), preferred_element_type=F32)
    return out[:count] + out[count:]


GROUP = 4


def first_kernel(
    n_radius, partial, heat, acoustic, radial_pair, radial_link, sector_pair, sector_link, basis,
    state, send, forcing, following, staged, sems
):
    radial = lax.axis_index("radial")
    cells_theta, cells_radius, cells_axial = partial.shape
    sectors = send.shape[0]
    own = cells_axial // sectors
    forcing[...] = partial[...]
    above, below = add_halos(forcing, radial_pair, radial_link, sector_pair, sector_link)
    copies = []

    def leave(begin, count):
        part = pl.ds(begin, count)
        copy = pltpu.make_async_copy(
            staged.at[:, part, :], send.at[:, part, :], sems.at[len(copies)]
        )
        copy.start()
        copies.append(copy)

    mine, rows = basis[...], flat(forcing)
    for r in range(0, cells_radius, GROUP):
        modes = sine_modes(mine, [rows[plane(forcing.shape, r + i), :] for i in range(GROUP)])
        for i in range(GROUP):
            lane = slice(i * cells_theta, (i + 1) * cells_theta)
            for d in range(sectors):
                staged[d, (r + i) * own : (r + i + 1) * own, :] = modes[
                    d * own : (d + 1) * own, lane
                ]
        leave(r * own, GROUP * own)

    share = (radial == 0).astype(F32)
    skip = 2 * cells_radius

    def extended(k):
        rows = slice(skip + k * EDGE, skip + (k + 1) * EDGE)
        middle = acoustic[k] if k < 3 else heat[...]
        return jnp.concatenate([below[rows], middle, above[rows]], 0)

    press, along, axial = extended(0) * share, extended(1) * share, extended(2) * share
    warm = extended(3) * (heat_coupling / n_radius)
    count = press.shape[0]
    lanes = lax.broadcasted_iota(jnp.int32, press.shape, 1)
    for _ in range(SUBSTEPS):
        press_up = pltpu.roll(press, count - 1, 0)
        press_axial = jnp.where(lanes == cells_axial - 1, 0.0, pltpu.roll(press, cells_axial - 1, 1))
        along = along - wave_speed * (press_up - press)
        axial = axial - wave_speed * (press_axial - press)
        along_down = pltpu.roll(along, 1, 0)
        axial_down = jnp.where(lanes == 0, 0.0, pltpu.roll(axial, 1, 1))
        press = press - wave_speed * ((along - along_down) + (axial - axial_down)) + warm
    middle = slice(EDGE, EDGE + cells_theta)
    following[0] = press[middle]
    following[1] = along[middle]
    following[2] = axial[middle]
    copies.append(pltpu.make_async_copy(following, state, sems.at[len(copies)]))
    copies[-1].start()
    modes = sine_modes(mine, [feedback * press[middle]])
    columns = cells_radius * own
    for d in range(sectors):
        staged[d, columns : columns + own, :] = modes[d * own : (d + 1) * own]
    leave(columns, own)
    for copy in copies:
        copy.wait()


def transformed(values, table, store):
    sectors = len(values)
    quarter, half = sectors // 4, sectors // 2

    def joined(parts):
        return jnp.concatenate(parts, 1) if len(parts) > 1 else parts[0]

    even = [values[s] + values[s + half] for s in range(half)]
    odd = [values[s] - values[s + half] for s in range(half)]
    both = [even[s] + even[s + quarter] for s in range(quarter)]
    apart = [even[s] - even[s + quarter] for s in range(quarter)]
    at = 0
    for parts, pieces in zip((both, apart, odd), table_parts(table)):
        width = pieces[0].shape[1]
        store(slice(at, at + width), product(split(joined(parts)), pieces, NN))
        at += width


def table_parts(table):
    n_theta = table.shape[1]
    quarter, half = n_theta // 4, n_theta // 2
    top, bottom = slice(0, quarter), slice(quarter, quarter + half)
    columns = [slice(i * quarter, (i + 1) * quarter) for i in range(4)]
    return (
        (table[top, columns[0]], table[top, columns[1]]),
        (table[top, columns[2]], table[top, columns[3]]),
        (table[bottom, :half], table[bottom, half:]),
    )


def forward_kernel(edge, received, table, *refs):
    modes, pair, link, wave = refs[-4:]
    sectors = received.shape[0]
    columns = modes.shape[0]
    radial_odd = lax.axis_index("radial") % 2 == 1

    def store(lane, out):
        modes[:, lane] = out[:columns]
        first, last = out[:edge], out[columns - edge : columns]
        pair[:edge, lane] = jnp.where(radial_odd, first, last)
        pair[edge:, lane] = out[columns:]
        link[:, lane] = jnp.where(radial_odd, last, first)
        wave[:, lane] = out[columns:]

    transformed([received[s] for s in range(sectors)], table, store)


def solve_kernel(
    modes, pair, link, wave, other_wave, impedance, fixed, weight, axial, table, send, solved
):
    radials = lax.axis_size("radial")
    radial = lax.axis_index("radial")
    sector = lax.axis_index("sector")
    columns, n_theta = modes.shape
    each = axial.shape[1]
    cells_radius = columns // each
    has_inner = (radial > 0).astype(F32)
    has_outer = (radial < radials - 1).astype(F32)
    radial_odd = radial % 2 == 1
    eigen = axial[sector]
    step = eigen.shape[1]
    total = cells_radius + 2 * HALO
    for block in range(n_theta // step):
        lane = slice(block * step, (block + 1) * step)
        row = 1.0 / (fixed[:, lane] + impedance[:, lane])
        inv = jnp.broadcast_to(row, (each, step))
        inv_inner, inv_outer = inv * has_inner, inv * has_outer
        last_scale = jnp.broadcast_to(row * weight[:, lane], (each, step))
        add = wave[:, lane] + other_wave[:, lane]

        def row_of(i):
            i -= HALO
            if 0 <= i < cells_radius:
                return modes[i * each : (i + 1) * each, lane]
            odd_one, even_one = (pair, link) if i < 0 else (link, pair)
            i = i + HALO if i < 0 else i - cells_radius
            rows = slice(i * each, (i + 1) * each)
            return jnp.where(radial_odd, odd_one[rows, lane], even_one[rows, lane])

        def scale_of(i):
            if i < HALO:
                return inv_inner
            return inv if i < HALO + cells_radius else inv_outer

        right = [row_of(i) + add for i in range(total)]
        x = [right[i] * scale_of(i) for i in range(total)]
        for sweep in range(1, SWEEPS):
            fresh = [None] * total
            for i in range(sweep, total - sweep):
                scale = last_scale if sweep == SWEEPS - 1 else scale_of(i)
                fresh[i] = (right[i] + (x[i + 1] + x[i - 1]) + eigen * x[i]) * scale
            x = fresh
        for i in range(cells_radius):
            solved[i * each : (i + 1) * each, lane] = x[i + HALO]

    sectors, _, width = send.shape
    outs, at = [], 0
    for pieces in table_parts(table):
        lane = slice(at, at + pieces[0].shape[1])
        outs.append(product(split(solved[:, lane]), pieces, NT))
        at = lane.stop
    both, apart, odd = outs
    even = jnp.concatenate([both + apart, both - apart], 1)
    for s in range(sectors // 2):
        lane = slice(s * width, (s + 1) * width)
        send[s] = even[:, lane] + odd[:, lane]
        send[s + sectors // 2] = even[:, lane] - odd[:, lane]


def pressure_kernel(received, basis, pressure_out, pressure, sems):
    sectors = received.shape[0]
    cells_radius = pressure.shape[1]
    own = received.shape[1] // cells_radius
    high, low = split(basis[...])
    right = jnp.concatenate(
        [jnp.concatenate([high, low], 1), jnp.concatenate([high, jnp.zeros_like(low)], 1)], 0
    )
    cells_axial = high.shape[1]
    copies = []
    for r in range(cells_radius):
        rows = [received[d, r * own : (r + 1) * own, :] for d in range(sectors)]
        modes = jnp.concatenate(rows, 0)
        left = jnp.concatenate(split(modes.T), 1)
        out = lax.dot_general(left, right, (NN, ((), ())), preferred_element_type=F32)
        flat(pressure)[plane(pressure.shape, r), :] = out[:, :cells_axial] + out[:, cells_axial:]
        if r % 8 == 7:
            rows = pl.ds(r - 7, 8)
            copy = pltpu.make_async_copy(
                pressure.at[:, rows, :], pressure_out.at[:, rows, :], sems.at[r // 8]
            )
            copy.start()
            copies.append(copy)
    for copy in copies:
        copy.wait()


def impedance_kernel(impedance, _, rows):
    half = impedance.shape[1] - 1
    count = half // 4
    pieces, rest = [], jnp.broadcast_to(impedance[:, :half], (8, half))
    for _ in range(3):
        piece = rest.astype(BF16)
        pieces.append(piece)
        rest = rest - piece.astype(F32)
    index = lax.broadcasted_iota(jnp.int32, (half, count), 0)
    target = 4 * lax.broadcasted_iota(jnp.int32, (half, count), 1)
    by_four = []
    for q in range(4):
        pick = (index == target + q).astype(F32).astype(BF16)
        parts = [
            lax.dot_general(piece, pick, (NN, ((), ())), preferred_element_type=F32)
            for piece in pieces
        ]
        by_four.append((parts[0] + (parts[1] + parts[2]))[:1])
    q0, q1, q2, q3 = by_four
    lanes = lax.broadcasted_iota(jnp.int32, (1, count), 1)
    last = jnp.broadcast_to(impedance[:, half:], (1, count))
    rows[...] = jnp.concatenate([q0, jnp.where(lanes == 0, last, q0), q2, q2, q1, q3, q1, q3], 1)


def partner_kernel(edge, wave, pair, out):
    out[...] = wave[...] + pair[edge:, :]


def add_kernel(left, right, out):
    out[...] = left[...] + right[...]


def step_kernel(
    n_theta, mouth_azimuth, mouth_radius, density, swirl, radial_pair, radial_link, sector_pair,
    sector_link, density_next, forcing
):
    flow_rows(n_theta, mouth_azimuth, mouth_radius, density, swirl, forcing)
    add_halos(forcing, radial_pair, radial_link, sector_pair, sector_link)
    density_next[...] = density[...] + time_step * forcing[...]


def call(kernel, outs, ins, scratch=(), limit=12 * 1024 * 1024, **more):
    moved = sum(math.prod(o.shape) * 4 for o in outs)
    return pl.pallas_call(
        kernel,
        out_shape=outs,
        in_specs=ins,
        out_specs=more.pop("out_specs", [VMEM] * len(outs)),
        scratch_shapes=list(scratch),
        cost_estimate=pl.CostEstimate(flops=0, bytes_accessed=3 * moved, transcendentals=0),
        compiler_params=pltpu.CompilerParams(vmem_limit_bytes=limit),
        **more,
    )


def shape(*dims):
    return jax.ShapeDtypeStruct(dims, F32)


def paired(pair, link, axis, closed):
    count = lax.axis_size(axis)
    first = [(i, i ^ 1) for i in range(count)]
    second = [(i, (i + 1) % count) for i in range(1, count if closed else count - 1, 2)]
    second += [(j, i) for i, j in second]
    return lax.ppermute(pair, axis, first), lax.ppermute(link, axis, second)


def swapped(value, axis, bits):
    return lax.ppermute(value, axis, [(i, i ^ bits) for i in range(lax.axis_size(axis))])


def halves_of_sum(value, axis, step=1):
    if step >= lax.axis_size(axis):
        return value, jnp.zeros_like(value)
    while True:
        other = swapped(value, axis, step)
        step *= 2
        if step >= lax.axis_size(axis):
            return value, other
        value = added(value, other)


def added(left, right):
    return call(add_kernel, [shape(*left.shape)], [VMEM] * 2, limit=4 * 1024 * 1024)(left, right)[0]


def in_hbm(value):
    return pltpu.with_memory_space_constraint(value, pltpu.HBM)


def in_vmem(value):
    return pltpu.with_memory_space_constraint(value, pltpu.VMEM)


def exchanged(value):
    return lax.all_to_all(value, "sector", split_axis=0, concat_axis=0, tiled=True)


def section(density, swirl, heat_rate, acoustic, mode_impedance, mouth_azimuth, mouth_radius):
    sectors = lax.axis_size("sector")
    radials = lax.axis_size("radial")
    cells_theta, cells_radius, cells_axial = density.shape
    n_theta = cells_theta * sectors
    n_radius = cells_radius * radials
    own = cells_axial // sectors
    columns = cells_radius * own
    edge = HALO * own

    basis, eigen = axial_tables(cells_axial)
    basis = jnp.asarray(basis.astype(np.float32))
    eigen = jnp.asarray(
        np.broadcast_to(eigen.reshape(sectors, own, 1), (sectors, own, 128)).astype(np.float32)
    )
    parts = [halves(table) for table in azimuth_tables(n_theta)]
    table = jnp.asarray(
        np.concatenate(
            [np.concatenate(parts[0] + parts[1], 1), np.concatenate(parts[2], 1)], 0
        )
    )
    fixed, weight = diagonal_tables(n_theta)
    fixed, weight = jnp.asarray(fixed)[None, :], jnp.asarray(weight)[None, :]
    (impedance,) = call(impedance_kernel, [shape(1, n_theta)], [VMEM] * 2)(
        mode_impedance[None, :], table
    )

    packed = 2 * cells_radius + 4 * EDGE
    row_block = shape(cells_theta, cells_axial)
    pair, link = call(
        edges_kernel,
        [shape(packed, cells_axial)] * 2,
        [HBM] * 4,
        [
            pltpu.VMEM((2, EDGE, cells_radius, cells_axial), F32),
            pltpu.VMEM((2, EDGE, cells_radius, cells_axial), F32),
            pltpu.VMEM((2, 1, cells_radius, cells_axial), F32),
            pltpu.VMEM((2, 3, EDGE, cells_axial), F32),
            pltpu.SemaphoreType.DMA((8,)),
        ],
    )(*[in_hbm(value) for value in (density, swirl, heat_rate, acoustic)])
    sector_halo = paired(pair, link, "sector", True)
    edge_rows = pair
    partial, heat, pair, link = call(
        lambda *refs: flow_kernel(n_theta, *refs),
        [shape(*density.shape)] + [row_block] * 3,
        [SMEM] * 2 + [VMEM] * 3 + [HBM],
    )(mouth_azimuth, mouth_radius, density, swirl, heat_rate, edge_rows)
    radial_halo = paired(pair, link, "radial", False)
    state, send = call(
        lambda *refs: first_kernel(n_radius, *refs),
        [
            pltpu.HBM(acoustic.shape, F32),
            pltpu.HBM((sectors, columns + own, cells_theta), F32),
        ],
        [VMEM] * 8,
        [
            pltpu.VMEM(density.shape, F32),
            pltpu.VMEM(acoustic.shape, F32),
            pltpu.VMEM((sectors, columns + own, cells_theta), F32),
            pltpu.SemaphoreType.DMA((2 + cells_radius // GROUP,)),
        ],
        out_specs=[HBM, HBM],
    )(partial, heat, acoustic, *radial_halo, *sector_halo, basis)
    received = exchanged(send)
    (density_next,) = call(
        lambda *refs: step_kernel(n_theta, *refs),
        [shape(*density.shape)],
        [SMEM] * 2 + [VMEM] * 6,
        [pltpu.VMEM(density.shape, F32)],
    )(mouth_azimuth, mouth_radius, density, swirl, *radial_halo, *sector_halo)
    acoustic_next = added(*halves_of_sum(state, "radial"))

    modes, pair, link, wave = call(
        lambda *refs: forward_kernel(edge, *refs),
        [
            shape(columns, n_theta),
            shape(edge + own, n_theta),
            shape(edge, n_theta),
            shape(own, n_theta),
        ],
        [VMEM] * 2 + [HBM] * 3,
    )(in_vmem(received), table, in_hbm(density_next), in_hbm(acoustic_next), impedance)
    halo = paired(pair, link, "radial", False)
    (wave,) = call(
        lambda *refs: partner_kernel(edge, *refs), [shape(own, n_theta)], [VMEM] * 2
    )(wave, halo[0])
    (send,) = call(
        solve_kernel,
        [shape(sectors, columns, cells_theta)],
        [VMEM] * 10,
        [pltpu.VMEM((columns, n_theta), F32)],
    )(modes, *halo, *halves_of_sum(wave, "radial", 2), impedance, fixed, weight, eigen, table)
    (pressure,) = call(
        pressure_kernel,
        [shape(*density.shape)],
        [VMEM] * 2,
        [pltpu.VMEM(density.shape, F32), pltpu.SemaphoreType.DMA((cells_radius // 8,))],
        out_specs=[HBM],
    )(exchanged(send), basis)
    return density_next, pressure, acoustic_next


def solution(mesh):
    return jax.shard_map(
        section,
        mesh=mesh,
        in_specs=(
            P("sector", "radial", None),
            P("sector", "radial", None),
            P("sector", "radial", None),
            P(None, "sector", None),
            P(),
            P(),
            P(),
        ),
        out_specs=(
            P("sector", "radial", None),
            P("sector", "radial", None),
            P(None, "sector", None),
        ),
        check_vma=False,
    )
```

```python
import math

import jax
import jax.numpy as jnp
import numpy as np
from jax import lax
from jax.experimental import pallas as pl
from jax.experimental.pallas import tpu as pltpu
from jax.sharding import PartitionSpec as P


BURNERS = 16
MOUTH = 8
SWEEPS = 4
SUBSTEPS = 8

time_step = 0.2
diffusion = 0.05
inflow_rate = 0.5
wave_speed = 0.5
heat_coupling = 0.5
feedback = 0.5

F32 = jnp.float32
BF16 = jnp.bfloat16
HALO = SWEEPS - 1
EDGE = 8
VMEM = pl.BlockSpec(memory_space=pltpu.VMEM)
SMEM = pl.BlockSpec(memory_space=pltpu.SMEM)
HBM = pl.BlockSpec(memory_space=pltpu.HBM)


def halves(table):
    high = table.astype(BF16)
    low = (table - high.astype(np.float64)).astype(BF16)
    return high, low


def axial_tables(cells):
    index = np.arange(1, cells + 1, dtype=np.float64)
    basis = math.sqrt(2.0 / (cells + 1)) * np.sin(
        np.pi * ((index[:, None] * index[None, :]) % (2 * (cells + 1))) / (cells + 1)
    )
    return basis, 2.0 * np.cos(np.pi * index / (cells + 1))


def mode_classes(n_theta):
    half = n_theta // 2
    multiples = np.arange(0, half, 4)
    first = (
        np.concatenate([multiples, [half], multiples[1:]]),
        np.concatenate([np.zeros(len(multiples) + 1), np.ones(len(multiples) - 1)]),
    )
    twos = np.arange(2, half, 4)
    second = (np.concatenate([twos, twos]), np.repeat([0, 1], len(twos)))
    ones, threes = np.arange(1, half, 4), np.arange(3, half, 4)
    third = (np.concatenate([ones, threes, ones, threes]), np.repeat([0, 1], half // 2))
    return first, second, third


def azimuth_tables(n_theta):
    bases = []
    for (order, odd), rows in zip(mode_classes(n_theta), (n_theta // 4, n_theta // 4, n_theta // 2)):
        phase = (np.arange(rows)[:, None] * order[None, :].astype(np.int64)) % n_theta
        angle = phase * (2.0 * np.pi / n_theta)
        bases.append(np.where(odd[None, :] == 0, np.cos(angle), np.sin(angle)))
    return bases


def diagonal_tables(n_theta):
    half = n_theta // 2
    order = np.concatenate([part[0] for part in mode_classes(n_theta)])
    shifted = 2.0 - 2.0 * np.cos(order * (2.0 * np.pi / n_theta))
    weight = np.where((order == 0) | (order == half), 1.0, 2.0) / n_theta
    return (4.0 + shifted).astype(np.float32), weight.astype(np.float32)


def split(value):
    high = value.astype(BF16)
    return high, (value - high.astype(F32)).astype(BF16)


def product(left, right, dims):
    def one(a, b):
        return lax.dot_general(a, b, (dims, ((), ())), preferred_element_type=F32)

    return one(left[0], right[0]) + (one(left[1], right[0]) + one(left[0], right[1]))


NN = ((1,), (0,))
NT = ((1,), (1,))


def edges_kernel(density, swirl, heat_rate, acoustic, pair, link, rho, rate, spin, wave, sems):
    cells_theta, cells_radius, _ = density.shape
    odd = lax.axis_index("sector") % 2
    copies = []

    def fetch(source, target):
        copy = pltpu.make_async_copy(source, target, sems.at[len(copies)])
        copy.start()
        copies.append(copy)

    for side, begin, row in ((0, 0, 0), (1, cells_theta - EDGE, cells_theta - 1)):
        fetch(density.at[pl.ds(begin, EDGE)], rho.at[side])
        fetch(heat_rate.at[pl.ds(begin, EDGE)], rate.at[side])
        fetch(swirl.at[pl.ds(row, 1)], spin.at[side])
        fetch(acoustic.at[:, pl.ds(begin, EDGE)], wave.at[side])
    for copy in copies:
        copy.wait()
    for out, side in ((pair, 1 - odd), (link, odd)):
        edge = jnp.where(side == 0, rho[0, 0], rho[1, EDGE - 1])
        out[0:cells_radius] = edge
        out[cells_radius : 2 * cells_radius] = edge * spin[side, 0]
        at = 2 * cells_radius
        for k in range(3):
            out[at : at + EDGE] = wave[side, k]
            at += EDGE
        heat = jnp.sum(rate[side] * rho[side] * rho[side], axis=1)
        out[at : at + EDGE] = heat


def flat(ref):
    cells_theta, cells_radius, cells_axial = ref.shape
    return ref.reshape(cells_theta * cells_radius, cells_axial)


def plane(shape, r):
    return pl.ds(r, shape[0], stride=shape[1])


def flow_rows(n_theta, mouth_azimuth, mouth_radius, density, swirl, forcing):
    sector = lax.axis_index("sector")
    radial = lax.axis_index("radial")
    cells_theta, cells_radius, cells_axial = density.shape
    shape = (cells_radius, cells_axial)
    rows = lax.broadcasted_iota(jnp.int32, shape, 0)
    lanes = lax.broadcasted_iota(jnp.int32, shape, 1)
    segment = n_theta // BURNERS
    part = min(segment, cells_theta)
    zero = jnp.zeros(shape, F32)

    def at(t):
        if t < 0 or t >= cells_theta:
            return zero, zero
        rho = density[t]
        return rho, rho * swirl[t]

    window = [at(-1), at(0)]
    for t in range(cells_theta):
        window.append(at(t + 1))
        (rho_down, flux_down), (rho, _), (rho_up, flux_up) = window
        window = window[1:]
        if t % part == 0:
            burner = (sector * cells_theta + t) // segment
            start = burner * segment + mouth_azimuth[burner] - sector * cells_theta
            radius = mouth_radius[burner] - radial * cells_radius
            mouth = ((rows >= radius) & (rows < radius + MOUTH)).astype(F32)
            mouth = mouth * (inflow_rate / time_step)
        gain = mouth * ((start <= t) & (t < start + MOUTH)).astype(F32)
        r_up = jnp.where(rows == cells_radius - 1, 0.0, pltpu.roll(rho, cells_radius - 1, 0))
        r_down = jnp.where(rows == 0, 0.0, pltpu.roll(rho, 1, 0))
        z_up = jnp.where(lanes == cells_axial - 1, 0.0, pltpu.roll(rho, cells_axial - 1, 1))
        z_down = jnp.where(lanes == 0, 0.0, pltpu.roll(rho, 1, 1))
        twice = 2.0 * rho
        laplace = (rho_up + rho_down - twice) + (r_up + r_down - twice) + (z_up + z_down - twice)
        forcing[t] = -0.5 * (flux_up - flux_down) + diffusion * laplace + gain * (1.0 - rho)


def add_halos(forcing, radial_pair, radial_link, sector_pair, sector_link):
    radials = lax.axis_size("radial")
    radial = lax.axis_index("radial")
    cells_theta, cells_radius, _ = forcing.shape
    odd = lax.axis_index("sector") % 2 == 1
    above = jnp.where(odd, sector_link[...], sector_pair[...])
    below = jnp.where(odd, sector_pair[...], sector_link[...])
    odd = radial % 2 == 1
    inner = jnp.where(odd, radial_pair[...], radial_link[...])
    outer = jnp.where(odd, radial_link[...], radial_pair[...])
    rho, flux = slice(0, cells_radius), slice(cells_radius, 2 * cells_radius)
    end = cells_theta - 1
    forcing[0] = forcing[0] + (0.5 * below[flux] + diffusion * below[rho])
    forcing[end] = forcing[end] + (diffusion * above[rho] - 0.5 * above[flux])
    inside = diffusion * (radial > 0).astype(F32)
    outside = diffusion * (radial < radials - 1).astype(F32)
    rows = flat(forcing)
    for r, term in ((0, inside * inner), (cells_radius - 1, outside * outer)):
        at = plane(forcing.shape, r)
        rows[at, :] = rows[at, :] + term


def flow_kernel(
    n_theta, mouth_azimuth, mouth_radius, density, swirl, heat_rate, _, forcing, heat, pair, link
):
    cells_theta, cells_radius, _ = density.shape
    odd = lax.axis_index("radial") % 2 == 1
    rows = flat(density)
    first, last = (rows[plane(density.shape, r), :] for r in (0, cells_radius - 1))
    pair[...] = jnp.where(odd, first, last)
    link[...] = jnp.where(odd, last, first)
    flow_rows(n_theta, mouth_azimuth, mouth_radius, density, swirl, forcing)
    for t in range(0, cells_theta, 8):
        rho = density[t : t + 8]
        heat[t : t + 8] = jnp.sum(heat_rate[t : t + 8] * rho * rho, axis=1)


def sine_modes(basis, fields):
    high, low = split(basis)
    count = high.shape[0]
    left = jnp.concatenate(
        [jnp.concatenate([high, high], 1), jnp.concatenate([low, jnp.zeros_like(low)], 1)], 0
    )
    right = jnp.concatenate([jnp.concatenate(split(field), 1) for field in fields], 0)
    out = lax.dot_general(left, right, (NT, ((), ())), preferred_element_type=F32)
    return out[:count] + out[count:]


GROUP = 4


def first_kernel(
    partial, radial_pair, radial_link, sector_pair, sector_link, basis, send, forcing, staged, sems
):
    cells_theta, cells_radius, cells_axial = partial.shape
    sectors = send.shape[0]
    own = cells_axial // sectors
    forcing[...] = partial[...]
    add_halos(forcing, radial_pair, radial_link, sector_pair, sector_link)
    copies = []

    def leave(begin, count):
        part = pl.ds(begin, count)
        copy = pltpu.make_async_copy(
            staged.at[:, part, :], send.at[:, part, :], sems.at[len(copies)]
        )
        copy.start()
        copies.append(copy)

    mine, rows = basis[...], flat(forcing)
    for r in range(0, cells_radius, GROUP):
        modes = sine_modes(mine, [rows[plane(forcing.shape, r + i), :] for i in range(GROUP)])
        for i in range(GROUP):
            lane = slice(i * cells_theta, (i + 1) * cells_theta)
            for d in range(sectors):
                staged[d, (r + i) * own : (r + i + 1) * own, :] = modes[
                    d * own : (d + 1) * own, lane
                ]
        leave(r * own, GROUP * own)

    for copy in copies:
        copy.wait()


def acoustic_kernel(n_radius, heat, acoustic, pair, link, share_press, share_rest, following, sem):
    radial = lax.axis_index("radial")
    cells_theta, cells_axial = heat.shape
    odd = lax.axis_index("sector") % 2 == 1
    above = jnp.where(odd, link[...], pair[...])
    below = jnp.where(odd, pair[...], link[...])
    share = (radial == 0).astype(F32)
    skip = above.shape[0] - 4 * EDGE

    def extended(k):
        rows = slice(skip + k * EDGE, skip + (k + 1) * EDGE)
        middle = acoustic[k] if k < 3 else heat[...]
        return jnp.concatenate([below[rows], middle, above[rows]], 0)

    press, along, axial = extended(0) * share, extended(1) * share, extended(2) * share
    warm = extended(3) * (heat_coupling / n_radius)
    count = press.shape[0]
    lanes = lax.broadcasted_iota(jnp.int32, press.shape, 1)
    for _ in range(SUBSTEPS):
        press_up = pltpu.roll(press, count - 1, 0)
        press_axial = jnp.where(lanes == cells_axial - 1, 0.0, pltpu.roll(press, cells_axial - 1, 1))
        along = along - wave_speed * (press_up - press)
        axial = axial - wave_speed * (press_axial - press)
        along_down = pltpu.roll(along, 1, 0)
        axial_down = jnp.where(lanes == 0, 0.0, pltpu.roll(axial, 1, 1))
        press = press - wave_speed * ((along - along_down) + (axial - axial_down)) + warm
    middle = slice(EDGE, EDGE + cells_theta)
    share_press[...] = press[middle]
    following[0] = along[middle]
    following[1] = axial[middle]
    copy = pltpu.make_async_copy(following, share_rest, sem)
    copy.start()
    copy.wait()


def part_kernel(press, basis, *parts):
    count, own = len(parts), parts[0].shape[1]
    sector, radial = lax.axis_index("sector"), lax.axis_index("radial")
    rows = [
        basis[pl.ds(pl.multiple_of((sector ^ (radial * count + j)) * own, 8), own), :]
        for j in range(count)
    ]
    modes = sine_modes(jnp.concatenate(rows, 0), [feedback * press[...]])
    for j in range(count):
        parts[j][0] = modes[j * own : (j + 1) * own]


def acoustic_next_kernel(press, left, right, acoustic_next):
    acoustic_next[0] = press[...]
    acoustic_next[1:] = left[...] + right[...]


def wave_kernel(count, *refs):
    parts, (table, wave, pieces) = refs[:-3], refs[-3:]
    sector, radial = lax.axis_index("sector"), lax.axis_index("radial")
    for i, part in enumerate(parts):
        offset, j = divmod(i, count)
        pieces[sector ^ ((radial ^ offset) * count + j)] = part[...].reshape(part.shape[-2:])

    def store(lane, out):
        wave[:, lane] = out

    transformed([pieces[s] for s in range(pieces.shape[0])], table, store)


def transformed(values, table, store):
    sectors = len(values)
    quarter, half = sectors // 4, sectors // 2

    def joined(parts):
        return jnp.concatenate(parts, 1) if len(parts) > 1 else parts[0]

    even = [values[s] + values[s + half] for s in range(half)]
    odd = [values[s] - values[s + half] for s in range(half)]
    both = [even[s] + even[s + quarter] for s in range(quarter)]
    apart = [even[s] - even[s + quarter] for s in range(quarter)]
    at = 0
    for parts, pieces in zip((both, apart, odd), table_parts(table)):
        width = pieces[0].shape[1]
        store(slice(at, at + width), product(split(joined(parts)), pieces, NN))
        at += width


def table_parts(table):
    n_theta = table.shape[1]
    quarter, half = n_theta // 4, n_theta // 2
    top, bottom = slice(0, quarter), slice(quarter, quarter + half)
    columns = [slice(i * quarter, (i + 1) * quarter) for i in range(4)]
    return (
        (table[top, columns[0]], table[top, columns[1]]),
        (table[top, columns[2]], table[top, columns[3]]),
        (table[bottom, :half], table[bottom, half:]),
    )


def forward_kernel(edge, received, table, *refs):
    modes, pair, link = refs[-3:]
    sectors, columns, _ = received.shape
    radial_odd = lax.axis_index("radial") % 2 == 1

    def store(lane, out):
        modes[:, lane] = out
        first, last = out[:edge], out[columns - edge :]
        pair[:, lane] = jnp.where(radial_odd, first, last)
        link[:, lane] = jnp.where(radial_odd, last, first)

    transformed([received[s] for s in range(sectors)], table, store)


def solve_kernel(
    modes, pair, link, wave, impedance, fixed, weight, axial, table, send, solved
):
    radials = lax.axis_size("radial")
    radial = lax.axis_index("radial")
    sector = lax.axis_index("sector")
    columns, n_theta = modes.shape
    each = axial.shape[1]
    cells_radius = columns // each
    has_inner = (radial > 0).astype(F32)
    has_outer = (radial < radials - 1).astype(F32)
    radial_odd = radial % 2 == 1
    eigen = axial[sector]
    step = eigen.shape[1]
    total = cells_radius + 2 * HALO
    for block in range(n_theta // step):
        lane = slice(block * step, (block + 1) * step)
        row = 1.0 / (fixed[:, lane] + impedance[:, lane])
        inv = jnp.broadcast_to(row, (each, step))
        inv_inner, inv_outer = inv * has_inner, inv * has_outer
        last_scale = jnp.broadcast_to(row * weight[:, lane], (each, step))
        add = wave[:, lane]

        def row_of(i):
            i -= HALO
            if 0 <= i < cells_radius:
                return modes[i * each : (i + 1) * each, lane]
            odd_one, even_one = (pair, link) if i < 0 else (link, pair)
            i = i + HALO if i < 0 else i - cells_radius
            rows = slice(i * each, (i + 1) * each)
            return jnp.where(radial_odd, odd_one[rows, lane], even_one[rows, lane])

        def scale_of(i):
            if i < HALO:
                return inv_inner
            return inv if i < HALO + cells_radius else inv_outer

        right = [row_of(i) + add for i in range(total)]
        x = [right[i] * scale_of(i) for i in range(total)]
        for sweep in range(1, SWEEPS):
            fresh = [None] * total
            for i in range(sweep, total - sweep):
                scale = last_scale if sweep == SWEEPS - 1 else scale_of(i)
                fresh[i] = (right[i] + (x[i + 1] + x[i - 1]) + eigen * x[i]) * scale
            x = fresh
        for i in range(cells_radius):
            solved[i * each : (i + 1) * each, lane] = x[i + HALO]

    sectors, _, width = send.shape
    outs, at = [], 0
    for pieces in table_parts(table):
        lane = slice(at, at + pieces[0].shape[1])
        outs.append(product(split(solved[:, lane]), pieces, NT))
        at = lane.stop
    both, apart, odd = outs
    even = jnp.concatenate([both + apart, both - apart], 1)
    for s in range(sectors // 2):
        lane = slice(s * width, (s + 1) * width)
        send[s] = even[:, lane] + odd[:, lane]
        send[s + sectors // 2] = even[:, lane] - odd[:, lane]


def pressure_kernel(received, basis, pressure_out, pressure, sems):
    sectors = received.shape[0]
    cells_radius = pressure.shape[1]
    own = received.shape[1] // cells_radius
    high, low = split(basis[...])
    right = jnp.concatenate(
        [jnp.concatenate([high, low], 1), jnp.concatenate([high, jnp.zeros_like(low)], 1)], 0
    )
    cells_axial = high.shape[1]
    copies = []
    for r in range(cells_radius):
        rows = [received[d, r * own : (r + 1) * own, :] for d in range(sectors)]
        modes = jnp.concatenate(rows, 0)
        left = jnp.concatenate(split(modes.T), 1)
        out = lax.dot_general(left, right, (NN, ((), ())), preferred_element_type=F32)
        flat(pressure)[plane(pressure.shape, r), :] = out[:, :cells_axial] + out[:, cells_axial:]
        if r % 8 == 7:
            rows = pl.ds(r - 7, 8)
            copy = pltpu.make_async_copy(
                pressure.at[:, rows, :], pressure_out.at[:, rows, :], sems.at[r // 8]
            )
            copy.start()
            copies.append(copy)
    for copy in copies:
        copy.wait()


def impedance_kernel(impedance, _, rows):
    half = impedance.shape[1] - 1
    count = half // 4
    pieces, rest = [], jnp.broadcast_to(impedance[:, :half], (8, half))
    for _ in range(3):
        piece = rest.astype(BF16)
        pieces.append(piece)
        rest = rest - piece.astype(F32)
    index = lax.broadcasted_iota(jnp.int32, (half, count), 0)
    target = 4 * lax.broadcasted_iota(jnp.int32, (half, count), 1)
    by_four = []
    for q in range(4):
        pick = (index == target + q).astype(F32).astype(BF16)
        parts = [
            lax.dot_general(piece, pick, (NN, ((), ())), preferred_element_type=F32)
            for piece in pieces
        ]
        by_four.append((parts[0] + (parts[1] + parts[2]))[:1])
    q0, q1, q2, q3 = by_four
    lanes = lax.broadcasted_iota(jnp.int32, (1, count), 1)
    last = jnp.broadcast_to(impedance[:, half:], (1, count))
    rows[...] = jnp.concatenate([q0, jnp.where(lanes == 0, last, q0), q2, q2, q1, q3, q1, q3], 1)


def add_kernel(left, right, out):
    out[...] = left[...] + right[...]


def step_kernel(
    n_theta, mouth_azimuth, mouth_radius, density, swirl, radial_pair, radial_link, sector_pair,
    sector_link, density_next, forcing
):
    flow_rows(n_theta, mouth_azimuth, mouth_radius, density, swirl, forcing)
    add_halos(forcing, radial_pair, radial_link, sector_pair, sector_link)
    density_next[...] = density[...] + time_step * forcing[...]


def call(kernel, outs, ins, scratch=(), limit=12 * 1024 * 1024, **more):
    moved = sum(math.prod(o.shape) * 4 for o in outs)
    return pl.pallas_call(
        kernel,
        out_shape=outs,
        in_specs=ins,
        out_specs=more.pop("out_specs", [VMEM] * len(outs)),
        scratch_shapes=list(scratch),
        cost_estimate=pl.CostEstimate(flops=0, bytes_accessed=3 * moved, transcendentals=0),
        compiler_params=pltpu.CompilerParams(vmem_limit_bytes=limit),
        **more,
    )


def shape(*dims):
    return jax.ShapeDtypeStruct(dims, F32)


def paired(pair, link, axis, closed):
    count = lax.axis_size(axis)
    first = [(i, i ^ 1) for i in range(count)]
    second = [(i, (i + 1) % count) for i in range(1, count if closed else count - 1, 2)]
    second += [(j, i) for i, j in second]
    return lax.ppermute(pair, axis, first), lax.ppermute(link, axis, second)


def swapped(value, axis, bits):
    return lax.ppermute(value, axis, [(i, i ^ bits) for i in range(lax.axis_size(axis))])


def halves_of_sum(value, axis, step=1):
    if step >= lax.axis_size(axis):
        return value, jnp.zeros_like(value)
    while True:
        other = swapped(value, axis, step)
        step *= 2
        if step >= lax.axis_size(axis):
            return value, other
        value = added(value, other)


def spread_part(part, j, count):
    sectors, radials = lax.axis_size("sector"), lax.axis_size("radial")
    pairs = [
        (s * radials + r, (s ^ (r * count + j)) * radials + r)
        for s in range(sectors)
        for r in range(radials)
    ]
    return lax.ppermute(part, ("sector", "radial"), pairs)


def added(left, right):
    return call(add_kernel, [shape(*left.shape)], [VMEM] * 2, limit=4 * 1024 * 1024)(left, right)[0]


def in_hbm(value):
    return pltpu.with_memory_space_constraint(value, pltpu.HBM)


def in_vmem(value):
    return pltpu.with_memory_space_constraint(value, pltpu.VMEM)


def exchanged(value):
    return lax.all_to_all(value, "sector", split_axis=0, concat_axis=0, tiled=True)


def section(density, swirl, heat_rate, acoustic, mode_impedance, mouth_azimuth, mouth_radius):
    sectors = lax.axis_size("sector")
    radials = lax.axis_size("radial")
    cells_theta, cells_radius, cells_axial = density.shape
    n_theta = cells_theta * sectors
    n_radius = cells_radius * radials
    own = cells_axial // sectors
    columns = cells_radius * own
    edge = HALO * own

    basis, eigen = axial_tables(cells_axial)
    basis = jnp.asarray(basis.astype(np.float32))
    eigen = jnp.asarray(
        np.broadcast_to(eigen.reshape(sectors, own, 1), (sectors, own, 128)).astype(np.float32)
    )
    parts = [halves(table) for table in azimuth_tables(n_theta)]
    table = jnp.asarray(
        np.concatenate(
            [np.concatenate(parts[0] + parts[1], 1), np.concatenate(parts[2], 1)], 0
        )
    )
    fixed, weight = diagonal_tables(n_theta)
    fixed, weight = jnp.asarray(fixed)[None, :], jnp.asarray(weight)[None, :]
    (impedance,) = call(impedance_kernel, [shape(1, n_theta)], [VMEM] * 2)(
        mode_impedance[None, :], table
    )

    packed = 2 * cells_radius + 4 * EDGE
    row_block = shape(cells_theta, cells_axial)
    pair, link = call(
        edges_kernel,
        [shape(packed, cells_axial)] * 2,
        [HBM] * 4,
        [
            pltpu.VMEM((2, EDGE, cells_radius, cells_axial), F32),
            pltpu.VMEM((2, EDGE, cells_radius, cells_axial), F32),
            pltpu.VMEM((2, 1, cells_radius, cells_axial), F32),
            pltpu.VMEM((2, 3, EDGE, cells_axial), F32),
            pltpu.SemaphoreType.DMA((8,)),
        ],
    )(*[in_hbm(value) for value in (density, swirl, heat_rate, acoustic)])
    sector_halo = paired(pair, link, "sector", True)
    edge_rows = pair
    partial, heat, pair, link = call(
        lambda *refs: flow_kernel(n_theta, *refs),
        [shape(*density.shape)] + [row_block] * 3,
        [SMEM] * 2 + [VMEM] * 3 + [HBM],
    )(mouth_azimuth, mouth_radius, density, swirl, heat_rate, edge_rows)
    radial_halo = paired(pair, link, "radial", False)
    (send,) = call(
        first_kernel,
        [pltpu.HBM((sectors, columns, cells_theta), F32)],
        [VMEM] * 6,
        [
            pltpu.VMEM(density.shape, F32),
            pltpu.VMEM((sectors, columns, cells_theta), F32),
            pltpu.SemaphoreType.DMA((cells_radius // GROUP,)),
        ],
        out_specs=[HBM],
    )(partial, *radial_halo, *sector_halo, basis)
    received = exchanged(send)

    rest_shape = (2, cells_theta, cells_axial)
    press, rest = call(
        lambda *refs: acoustic_kernel(n_radius, *refs),
        [row_block, pltpu.HBM(rest_shape, F32)],
        [VMEM] * 4,
        [pltpu.VMEM(rest_shape, F32), pltpu.SemaphoreType.DMA],
        out_specs=[VMEM, HBM],
    )(heat, acoustic, *sector_halo)
    press = added(*halves_of_sum(press, "radial"))
    count = sectors // radials
    parts = call(part_kernel, [shape(1, own, cells_theta)] * count, [VMEM] * 2)(press, basis)
    parts = [spread_part(part, j, count) for j, part in enumerate(parts)]
    step = 1
    while step < radials:
        parts += [swapped(value, "radial", step) for value in parts]
        step *= 2
    (wave,) = call(
        lambda *refs: wave_kernel(count, *refs),
        [shape(own, n_theta)],
        [VMEM] * (sectors + 1),
        [pltpu.VMEM((sectors, own, cells_theta), F32)],
    )(*parts, table)
    rest = halves_of_sum(rest, "radial")
    (acoustic_next,) = call(acoustic_next_kernel, [shape(*acoustic.shape)], [VMEM] * 3)(
        press, *rest
    )
    (density_next,) = call(
        lambda *refs: step_kernel(n_theta, *refs),
        [shape(*density.shape)],
        [SMEM] * 2 + [VMEM] * 6,
        [pltpu.VMEM(density.shape, F32)],
    )(mouth_azimuth, mouth_radius, density, swirl, *radial_halo, *sector_halo)

    modes, pair, link = call(
        lambda *refs: forward_kernel(edge, *refs),
        [shape(columns, n_theta), shape(edge, n_theta), shape(edge, n_theta)],
        [VMEM] * 2 + [HBM] * 4,
    )(in_vmem(received), table, in_hbm(density_next), in_hbm(acoustic_next), impedance, wave)
    (send,) = call(
        solve_kernel,
        [shape(sectors, columns, cells_theta)],
        [VMEM] * 9,
        [pltpu.VMEM((columns, n_theta), F32)],
    )(modes, *paired(pair, link, "radial", False), wave, impedance, fixed, weight, eigen, table)
    (pressure,) = call(
        pressure_kernel,
        [shape(*density.shape)],
        [VMEM] * 2,
        [pltpu.VMEM(density.shape, F32), pltpu.SemaphoreType.DMA((cells_radius // 8,))],
        out_specs=[HBM],
    )(exchanged(send), basis)
    return density_next, pressure, acoustic_next


def solution(mesh):
    return jax.shard_map(
        section,
        mesh=mesh,
        in_specs=(
            P("sector", "radial", None),
            P("sector", "radial", None),
            P("sector", "radial", None),
            P(None, "sector", None),
            P(),
            P(),
            P(),
        ),
        out_specs=(
            P("sector", "radial", None),
            P("sector", "radial", None),
            P(None, "sector", None),
        ),
        check_vma=False,
    )
```

```python
import math

import jax
import jax.numpy as jnp
import numpy as np
from jax import lax
from jax.experimental import pallas as pl
from jax.experimental.pallas import tpu as pltpu
from jax.sharding import PartitionSpec as P


BURNERS = 16
MOUTH = 8
SWEEPS = 4
SUBSTEPS = 8

time_step = 0.2
diffusion = 0.05
inflow_rate = 0.5
wave_speed = 0.5
heat_coupling = 0.5
feedback = 0.5

F32 = jnp.float32
BF16 = jnp.bfloat16
HALO = SWEEPS - 1
EDGE = 8
VMEM = pl.BlockSpec(memory_space=pltpu.VMEM)
SMEM = pl.BlockSpec(memory_space=pltpu.SMEM)
HBM = pl.BlockSpec(memory_space=pltpu.HBM)


def halves(table):
    high = table.astype(BF16)
    low = (table - high.astype(np.float64)).astype(BF16)
    return high, low


def axial_tables(cells):
    index = np.arange(1, cells + 1, dtype=np.float64)
    basis = math.sqrt(2.0 / (cells + 1)) * np.sin(
        np.pi * ((index[:, None] * index[None, :]) % (2 * (cells + 1))) / (cells + 1)
    )
    return basis, 2.0 * np.cos(np.pi * index / (cells + 1))


def mode_classes(n_theta):
    half = n_theta // 2
    multiples = np.arange(0, half, 4)
    first = (
        np.concatenate([multiples, [half], multiples[1:]]),
        np.concatenate([np.zeros(len(multiples) + 1), np.ones(len(multiples) - 1)]),
    )
    twos = np.arange(2, half, 4)
    second = (np.concatenate([twos, twos]), np.repeat([0, 1], len(twos)))
    ones, threes = np.arange(1, half, 4), np.arange(3, half, 4)
    third = (np.concatenate([ones, threes, ones, threes]), np.repeat([0, 1], half // 2))
    return first, second, third


def azimuth_tables(n_theta):
    bases = []
    for (order, odd), rows in zip(mode_classes(n_theta), (n_theta // 4, n_theta // 4, n_theta // 2)):
        phase = (np.arange(rows)[:, None] * order[None, :].astype(np.int64)) % n_theta
        angle = phase * (2.0 * np.pi / n_theta)
        bases.append(np.where(odd[None, :] == 0, np.cos(angle), np.sin(angle)))
    return bases


def diagonal_tables(n_theta):
    half = n_theta // 2
    order = np.concatenate([part[0] for part in mode_classes(n_theta)])
    shifted = 2.0 - 2.0 * np.cos(order * (2.0 * np.pi / n_theta))
    weight = np.where((order == 0) | (order == half), 1.0, 2.0) / n_theta
    return (4.0 + shifted).astype(np.float32), weight.astype(np.float32)


def split(value):
    high = value.astype(BF16)
    return high, (value - high.astype(F32)).astype(BF16)


def product(left, right, dims):
    def one(a, b):
        return lax.dot_general(a, b, (dims, ((), ())), preferred_element_type=F32)

    return one(left[0], right[0]) + (one(left[1], right[0]) + one(left[0], right[1]))


NN = ((1,), (0,))
NT = ((1,), (1,))


def edges_kernel(density, swirl, heat_rate, acoustic, pair, link, rho, rate, spin, wave, sems):
    cells_theta, cells_radius, _ = density.shape
    odd = lax.axis_index("sector") % 2
    copies = []

    def fetch(source, target):
        copy = pltpu.make_async_copy(source, target, sems.at[len(copies)])
        copy.start()
        copies.append(copy)

    for side, begin, row in ((0, 0, 0), (1, cells_theta - EDGE, cells_theta - 1)):
        fetch(density.at[pl.ds(begin, EDGE)], rho.at[side])
        fetch(heat_rate.at[pl.ds(begin, EDGE)], rate.at[side])
        fetch(swirl.at[pl.ds(row, 1)], spin.at[side])
        fetch(acoustic.at[:, pl.ds(begin, EDGE)], wave.at[side])
    for copy in copies:
        copy.wait()
    for out, side in ((pair, 1 - odd), (link, odd)):
        edge = jnp.where(side == 0, rho[0, 0], rho[1, EDGE - 1])
        out[0:cells_radius] = edge
        out[cells_radius : 2 * cells_radius] = edge * spin[side, 0]
        at = 2 * cells_radius
        for k in range(3):
            out[at : at + EDGE] = wave[side, k]
            at += EDGE
        heat = jnp.sum(rate[side] * rho[side] * rho[side], axis=1)
        out[at : at + EDGE] = heat


def flat(ref):
    cells_theta, cells_radius, cells_axial = ref.shape
    return ref.reshape(cells_theta * cells_radius, cells_axial)


def plane(shape, r):
    return pl.ds(r, shape[0], stride=shape[1])


def flow_rows(n_theta, mouth_azimuth, mouth_radius, density, swirl, forcing):
    sector = lax.axis_index("sector")
    radial = lax.axis_index("radial")
    cells_theta, cells_radius, cells_axial = density.shape
    shape = (cells_radius, cells_axial)
    rows = lax.broadcasted_iota(jnp.int32, shape, 0)
    lanes = lax.broadcasted_iota(jnp.int32, shape, 1)
    segment = n_theta // BURNERS
    part = min(segment, cells_theta)
    zero = jnp.zeros(shape, F32)

    def at(t):
        if t < 0 or t >= cells_theta:
            return zero, zero
        rho = density[t]
        return rho, rho * swirl[t]

    window = [at(-1), at(0)]
    for t in range(cells_theta):
        window.append(at(t + 1))
        (rho_down, flux_down), (rho, _), (rho_up, flux_up) = window
        window = window[1:]
        if t % part == 0:
            burner = (sector * cells_theta + t) // segment
            start = burner * segment + mouth_azimuth[burner] - sector * cells_theta
            radius = mouth_radius[burner] - radial * cells_radius
            mouth = ((rows >= radius) & (rows < radius + MOUTH)).astype(F32)
            mouth = mouth * (inflow_rate / time_step)
        gain = mouth * ((start <= t) & (t < start + MOUTH)).astype(F32)
        r_up = jnp.where(rows == cells_radius - 1, 0.0, pltpu.roll(rho, cells_radius - 1, 0))
        r_down = jnp.where(rows == 0, 0.0, pltpu.roll(rho, 1, 0))
        z_up = jnp.where(lanes == cells_axial - 1, 0.0, pltpu.roll(rho, cells_axial - 1, 1))
        z_down = jnp.where(lanes == 0, 0.0, pltpu.roll(rho, 1, 1))
        twice = 2.0 * rho
        laplace = (rho_up + rho_down - twice) + (r_up + r_down - twice) + (z_up + z_down - twice)
        forcing[t] = -0.5 * (flux_up - flux_down) + diffusion * laplace + gain * (1.0 - rho)


def add_halos(forcing, radial_pair, radial_link, sector_pair, sector_link):
    radials = lax.axis_size("radial")
    radial = lax.axis_index("radial")
    cells_theta, cells_radius, _ = forcing.shape
    odd = lax.axis_index("sector") % 2 == 1
    above = jnp.where(odd, sector_link[...], sector_pair[...])
    below = jnp.where(odd, sector_pair[...], sector_link[...])
    odd = radial % 2 == 1
    inner = jnp.where(odd, radial_pair[...], radial_link[...])
    outer = jnp.where(odd, radial_link[...], radial_pair[...])
    rho, flux = slice(0, cells_radius), slice(cells_radius, 2 * cells_radius)
    end = cells_theta - 1
    forcing[0] = forcing[0] + (0.5 * below[flux] + diffusion * below[rho])
    forcing[end] = forcing[end] + (diffusion * above[rho] - 0.5 * above[flux])
    inside = diffusion * (radial > 0).astype(F32)
    outside = diffusion * (radial < radials - 1).astype(F32)
    rows = flat(forcing)
    for r, term in ((0, inside * inner), (cells_radius - 1, outside * outer)):
        at = plane(forcing.shape, r)
        rows[at, :] = rows[at, :] + term
    return above, below


def flow_kernel(
    n_theta, mouth_azimuth, mouth_radius, density, swirl, heat_rate, _, forcing, heat, pair, link
):
    cells_theta, cells_radius, _ = density.shape
    odd = lax.axis_index("radial") % 2 == 1
    rows = flat(density)
    first, last = (rows[plane(density.shape, r), :] for r in (0, cells_radius - 1))
    pair[...] = jnp.where(odd, first, last)
    link[...] = jnp.where(odd, last, first)
    flow_rows(n_theta, mouth_azimuth, mouth_radius, density, swirl, forcing)
    for t in range(0, cells_theta, 8):
        rho = density[t : t + 8]
        heat[t : t + 8] = jnp.sum(heat_rate[t : t + 8] * rho * rho, axis=1)


def sine_modes(basis, fields):
    high, low = split(basis)
    count = high.shape[0]
    left = jnp.concatenate(
        [jnp.concatenate([high, high], 1), jnp.concatenate([low, jnp.zeros_like(low)], 1)], 0
    )
    right = jnp.concatenate([jnp.concatenate(split(field), 1) for field in fields], 0)
    out = lax.dot_general(left, right, (NT, ((), ())), preferred_element_type=F32)
    return out[:count] + out[count:]


GROUP = 4


def first_kernel(
    n_radius, partial, heat, acoustic, radial_pair, radial_link, sector_pair, sector_link, basis,
    state, send, forcing, following, staged, sems
):
    radial = lax.axis_index("radial")
    cells_theta, cells_radius, cells_axial = partial.shape
    sectors = send.shape[0]
    own = cells_axial // sectors
    forcing[...] = partial[...]
    above, below = add_halos(forcing, radial_pair, radial_link, sector_pair, sector_link)
    copies = []

    def leave(begin, count):
        part = pl.ds(begin, count)
        copy = pltpu.make_async_copy(
            staged.at[:, part, :], send.at[:, part, :], sems.at[len(copies)]
        )
        copy.start()
        copies.append(copy)

    mine, rows = basis[...], flat(forcing)
    for r in range(0, cells_radius, GROUP):
        modes = sine_modes(mine, [rows[plane(forcing.shape, r + i), :] for i in range(GROUP)])
        for i in range(GROUP):
            lane = slice(i * cells_theta, (i + 1) * cells_theta)
            for d in range(sectors):
                staged[d, (r + i) * own : (r + i + 1) * own, :] = modes[
                    d * own : (d + 1) * own, lane
                ]
        leave(r * own, GROUP * own)

    share = (radial == 0).astype(F32)
    skip = 2 * cells_radius

    def extended(k):
        rows = slice(skip + k * EDGE, skip + (k + 1) * EDGE)
        middle = acoustic[k] if k < 3 else heat[...]
        return jnp.concatenate([below[rows], middle, above[rows]], 0)

    press, along, axial = extended(0) * share, extended(1) * share, extended(2) * share
    warm = extended(3) * (heat_coupling / n_radius)
    count = press.shape[0]
    lanes = lax.broadcasted_iota(jnp.int32, press.shape, 1)
    for _ in range(SUBSTEPS):
        press_up = pltpu.roll(press, count - 1, 0)
        press_axial = jnp.where(lanes == cells_axial - 1, 0.0, pltpu.roll(press, cells_axial - 1, 1))
        along = along - wave_speed * (press_up - press)
        axial = axial - wave_speed * (press_axial - press)
        along_down = pltpu.roll(along, 1, 0)
        axial_down = jnp.where(lanes == 0, 0.0, pltpu.roll(axial, 1, 1))
        press = press - wave_speed * ((along - along_down) + (axial - axial_down)) + warm
    middle = slice(EDGE, EDGE + cells_theta)
    following[0] = press[middle]
    following[1] = along[middle]
    following[2] = axial[middle]
    copies.append(pltpu.make_async_copy(following, state, sems.at[len(copies)]))
    copies[-1].start()
    modes = sine_modes(mine, [feedback * press[middle]])
    columns = cells_radius * own
    for d in range(sectors):
        staged[d, columns : columns + own, :] = modes[d * own : (d + 1) * own]
    leave(columns, own)
    for copy in copies:
        copy.wait()


def transformed(values, table, store):
    sectors = len(values)
    quarter, half = sectors // 4, sectors // 2

    def joined(parts):
        return jnp.concatenate(parts, 1) if len(parts) > 1 else parts[0]

    even = [values[s] + values[s + half] for s in range(half)]
    odd = [values[s] - values[s + half] for s in range(half)]
    both = [even[s] + even[s + quarter] for s in range(quarter)]
    apart = [even[s] - even[s + quarter] for s in range(quarter)]
    at = 0
    for parts, pieces in zip((both, apart, odd), table_parts(table)):
        width = pieces[0].shape[1]
        store(slice(at, at + width), product(split(joined(parts)), pieces, NN))
        at += width


def table_parts(table):
    n_theta = table.shape[1]
    quarter, half = n_theta // 4, n_theta // 2
    top, bottom = slice(0, quarter), slice(quarter, quarter + half)
    columns = [slice(i * quarter, (i + 1) * quarter) for i in range(4)]
    return (
        (table[top, columns[0]], table[top, columns[1]]),
        (table[top, columns[2]], table[top, columns[3]]),
        (table[bottom, :half], table[bottom, half:]),
    )


def forward_kernel(edge, received, table, *refs):
    modes, pair, link = refs[-3:]
    sectors = received.shape[0]
    columns = modes.shape[0]
    radial_odd = lax.axis_index("radial") % 2 == 1

    def store(lane, out):
        modes[:, lane] = out
        first, last = out[:edge], out[columns - edge :]
        pair[:, lane] = jnp.where(radial_odd, first, last)
        link[:, lane] = jnp.where(radial_odd, last, first)

    transformed([received[s, :columns, :] for s in range(sectors)], table, store)


def wave_kernel(received, table, wave):
    columns = received.shape[1] - wave.shape[0]

    def store(lane, out):
        wave[:, lane] = out

    transformed([received[s, columns:, :] for s in range(received.shape[0])], table, store)


def solve_kernel(
    modes, pair, link, wave, other_wave, impedance, fixed, weight, axial, table, send, solved
):
    radials = lax.axis_size("radial")
    radial = lax.axis_index("radial")
    sector = lax.axis_index("sector")
    columns, n_theta = modes.shape
    each = axial.shape[1]
    cells_radius = columns // each
    has_inner = (radial > 0).astype(F32)
    has_outer = (radial < radials - 1).astype(F32)
    radial_odd = radial % 2 == 1
    eigen = axial[sector]
    step = eigen.shape[1]
    total = cells_radius + 2 * HALO
    for block in range(n_theta // step):
        lane = slice(block * step, (block + 1) * step)
        row = 1.0 / (fixed[:, lane] + impedance[:, lane])
        inv = jnp.broadcast_to(row, (each, step))
        inv_inner, inv_outer = inv * has_inner, inv * has_outer
        last_scale = jnp.broadcast_to(row * weight[:, lane], (each, step))
        add = wave[:, lane] + other_wave[:, lane]

        def row_of(i):
            i -= HALO
            if 0 <= i < cells_radius:
                return modes[i * each : (i + 1) * each, lane]
            odd_one, even_one = (pair, link) if i < 0 else (link, pair)
            i = i + HALO if i < 0 else i - cells_radius
            rows = slice(i * each, (i + 1) * each)
            return jnp.where(radial_odd, odd_one[rows, lane], even_one[rows, lane])

        def scale_of(i):
            if i < HALO:
                return inv_inner
            return inv if i < HALO + cells_radius else inv_outer

        right = [row_of(i) + add for i in range(total)]
        x = [right[i] * scale_of(i) for i in range(total)]
        for sweep in range(1, SWEEPS):
            fresh = [None] * total
            for i in range(sweep, total - sweep):
                scale = last_scale if sweep == SWEEPS - 1 else scale_of(i)
                fresh[i] = (right[i] + (x[i + 1] + x[i - 1]) + eigen * x[i]) * scale
            x = fresh
        for i in range(cells_radius):
            solved[i * each : (i + 1) * each, lane] = x[i + HALO]

    sectors, _, width = send.shape
    outs, at = [], 0
    for pieces in table_parts(table):
        lane = slice(at, at + pieces[0].shape[1])
        outs.append(product(split(solved[:, lane]), pieces, NT))
        at = lane.stop
    both, apart, odd = outs
    even = jnp.concatenate([both + apart, both - apart], 1)
    for s in range(sectors // 2):
        lane = slice(s * width, (s + 1) * width)
        send[s] = even[:, lane] + odd[:, lane]
        send[s + sectors // 2] = even[:, lane] - odd[:, lane]


def pressure_kernel(received, basis, pressure_out, pressure, sems):
    sectors = received.shape[0]
    cells_radius = pressure.shape[1]
    own = received.shape[1] // cells_radius
    high, low = split(basis[...])
    right = jnp.concatenate(
        [jnp.concatenate([high, low], 1), jnp.concatenate([high, jnp.zeros_like(low)], 1)], 0
    )
    cells_axial = high.shape[1]
    copies = []
    for r in range(cells_radius):
        rows = [received[d, r * own : (r + 1) * own, :] for d in range(sectors)]
        modes = jnp.concatenate(rows, 0)
        left = jnp.concatenate(split(modes.T), 1)
        out = lax.dot_general(left, right, (NN, ((), ())), preferred_element_type=F32)
        flat(pressure)[plane(pressure.shape, r), :] = out[:, :cells_axial] + out[:, cells_axial:]
        if r % 8 == 7:
            rows = pl.ds(r - 7, 8)
            copy = pltpu.make_async_copy(
                pressure.at[:, rows, :], pressure_out.at[:, rows, :], sems.at[r // 8]
            )
            copy.start()
            copies.append(copy)
    for copy in copies:
        copy.wait()


def impedance_kernel(impedance, _, rows):
    half = impedance.shape[1] - 1
    count = half // 4
    pieces, rest = [], jnp.broadcast_to(impedance[:, :half], (8, half))
    for _ in range(3):
        piece = rest.astype(BF16)
        pieces.append(piece)
        rest = rest - piece.astype(F32)
    index = lax.broadcasted_iota(jnp.int32, (half, count), 0)
    target = 4 * lax.broadcasted_iota(jnp.int32, (half, count), 1)
    by_four = []
    for q in range(4):
        pick = (index == target + q).astype(F32).astype(BF16)
        parts = [
            lax.dot_general(piece, pick, (NN, ((), ())), preferred_element_type=F32)
            for piece in pieces
        ]
        by_four.append((parts[0] + (parts[1] + parts[2]))[:1])
    q0, q1, q2, q3 = by_four
    lanes = lax.broadcasted_iota(jnp.int32, (1, count), 1)
    last = jnp.broadcast_to(impedance[:, half:], (1, count))
    rows[...] = jnp.concatenate([q0, jnp.where(lanes == 0, last, q0), q2, q2, q1, q3, q1, q3], 1)


def add_kernel(left, right, out):
    out[...] = left[...] + right[...]


def step_kernel(
    n_theta, mouth_azimuth, mouth_radius, density, swirl, radial_pair, radial_link, sector_pair,
    sector_link, density_next, forcing
):
    flow_rows(n_theta, mouth_azimuth, mouth_radius, density, swirl, forcing)
    add_halos(forcing, radial_pair, radial_link, sector_pair, sector_link)
    density_next[...] = density[...] + time_step * forcing[...]


def call(kernel, outs, ins, scratch=(), limit=12 * 1024 * 1024, **more):
    moved = sum(math.prod(o.shape) * 4 for o in outs)
    return pl.pallas_call(
        kernel,
        out_shape=outs,
        in_specs=ins,
        out_specs=more.pop("out_specs", [VMEM] * len(outs)),
        scratch_shapes=list(scratch),
        cost_estimate=pl.CostEstimate(flops=0, bytes_accessed=3 * moved, transcendentals=0),
        compiler_params=pltpu.CompilerParams(vmem_limit_bytes=limit),
        **more,
    )


def shape(*dims):
    return jax.ShapeDtypeStruct(dims, F32)


def paired(pair, link, axis, closed):
    count = lax.axis_size(axis)
    first = [(i, i ^ 1) for i in range(count)]
    second = [(i, (i + 1) % count) for i in range(1, count if closed else count - 1, 2)]
    second += [(j, i) for i, j in second]
    return lax.ppermute(pair, axis, first), lax.ppermute(link, axis, second)


def swapped(value, axis, bits):
    return lax.ppermute(value, axis, [(i, i ^ bits) for i in range(lax.axis_size(axis))])


def halves_of_sum(value, axis, step=1):
    if step >= lax.axis_size(axis):
        return value, jnp.zeros_like(value)
    while True:
        other = swapped(value, axis, step)
        step *= 2
        if step >= lax.axis_size(axis):
            return value, other
        value = added(value, other)


def added(left, right):
    return call(add_kernel, [shape(*left.shape)], [VMEM] * 2, limit=4 * 1024 * 1024)(left, right)[0]


def in_hbm(value):
    return pltpu.with_memory_space_constraint(value, pltpu.HBM)


def in_vmem(value):
    return pltpu.with_memory_space_constraint(value, pltpu.VMEM)


def exchanged(value):
    return lax.all_to_all(value, "sector", split_axis=0, concat_axis=0, tiled=True)


def section(density, swirl, heat_rate, acoustic, mode_impedance, mouth_azimuth, mouth_radius):
    sectors = lax.axis_size("sector")
    radials = lax.axis_size("radial")
    cells_theta, cells_radius, cells_axial = density.shape
    n_theta = cells_theta * sectors
    n_radius = cells_radius * radials
    own = cells_axial // sectors
    columns = cells_radius * own
    edge = HALO * own

    basis, eigen = axial_tables(cells_axial)
    basis = jnp.asarray(basis.astype(np.float32))
    eigen = jnp.asarray(
        np.broadcast_to(eigen.reshape(sectors, own, 1), (sectors, own, 128)).astype(np.float32)
    )
    parts = [halves(table) for table in azimuth_tables(n_theta)]
    table = jnp.asarray(
        np.concatenate(
            [np.concatenate(parts[0] + parts[1], 1), np.concatenate(parts[2], 1)], 0
        )
    )
    fixed, weight = diagonal_tables(n_theta)
    fixed, weight = jnp.asarray(fixed)[None, :], jnp.asarray(weight)[None, :]
    (impedance,) = call(impedance_kernel, [shape(1, n_theta)], [VMEM] * 2)(
        mode_impedance[None, :], table
    )

    packed = 2 * cells_radius + 4 * EDGE
    row_block = shape(cells_theta, cells_axial)
    pair, link = call(
        edges_kernel,
        [shape(packed, cells_axial)] * 2,
        [HBM] * 4,
        [
            pltpu.VMEM((2, EDGE, cells_radius, cells_axial), F32),
            pltpu.VMEM((2, EDGE, cells_radius, cells_axial), F32),
            pltpu.VMEM((2, 1, cells_radius, cells_axial), F32),
            pltpu.VMEM((2, 3, EDGE, cells_axial), F32),
            pltpu.SemaphoreType.DMA((8,)),
        ],
    )(*[in_hbm(value) for value in (density, swirl, heat_rate, acoustic)])
    sector_halo = paired(pair, link, "sector", True)
    edge_rows = pair
    partial, heat, pair, link = call(
        lambda *refs: flow_kernel(n_theta, *refs),
        [shape(*density.shape)] + [row_block] * 3,
        [SMEM] * 2 + [VMEM] * 3 + [HBM],
    )(mouth_azimuth, mouth_radius, density, swirl, heat_rate, edge_rows)
    radial_halo = paired(pair, link, "radial", False)
    state, send = call(
        lambda *refs: first_kernel(n_radius, *refs),
        [
            pltpu.HBM(acoustic.shape, F32),
            pltpu.HBM((sectors, columns + own, cells_theta), F32),
        ],
        [VMEM] * 8,
        [
            pltpu.VMEM(density.shape, F32),
            pltpu.VMEM(acoustic.shape, F32),
            pltpu.VMEM((sectors, columns + own, cells_theta), F32),
            pltpu.SemaphoreType.DMA((2 + cells_radius // GROUP,)),
        ],
        out_specs=[HBM, HBM],
    )(partial, heat, acoustic, *radial_halo, *sector_halo, basis)
    received = exchanged(send)
    (density_next,) = call(
        lambda *refs: step_kernel(n_theta, *refs),
        [shape(*density.shape)],
        [SMEM] * 2 + [VMEM] * 6,
        [pltpu.VMEM(density.shape, F32)],
    )(mouth_azimuth, mouth_radius, density, swirl, *radial_halo, *sector_halo)
    acoustic_next = added(*halves_of_sum(state, "radial"))

    received = in_vmem(received)
    (wave,) = call(wave_kernel, [shape(own, n_theta)], [VMEM] * 2)(received, table)
    partner = swapped(wave, "radial", 1)
    modes, pair, link = call(
        lambda *refs: forward_kernel(edge, *refs),
        [shape(columns, n_theta), shape(edge, n_theta), shape(edge, n_theta)],
        [VMEM] * 2 + [HBM] * 4,
    )(received, table, in_hbm(density_next), in_hbm(acoustic_next), impedance, wave)
    wave = halves_of_sum(added(wave, partner), "radial", 2)
    halo = paired(pair, link, "radial", False)
    (send,) = call(
        solve_kernel,
        [shape(sectors, columns, cells_theta)],
        [VMEM] * 10,
        [pltpu.VMEM((columns, n_theta), F32)],
    )(modes, *halo, *wave, impedance, fixed, weight, eigen, table)
    (pressure,) = call(
        pressure_kernel,
        [shape(*density.shape)],
        [VMEM] * 2,
        [pltpu.VMEM(density.shape, F32), pltpu.SemaphoreType.DMA((cells_radius // 8,))],
        out_specs=[HBM],
    )(exchanged(send), basis)
    return density_next, pressure, acoustic_next


def solution(mesh):
    return jax.shard_map(
        section,
        mesh=mesh,
        in_specs=(
            P("sector", "radial", None),
            P("sector", "radial", None),
            P("sector", "radial", None),
            P(None, "sector", None),
            P(),
            P(),
            P(),
        ),
        out_specs=(
            P("sector", "radial", None),
            P("sector", "radial", None),
            P(None, "sector", None),
        ),
        check_vma=False,
    )
```

```python
import math

import jax
import jax.numpy as jnp
import numpy as np
from jax import lax
from jax.experimental import pallas as pl
from jax.experimental.pallas import tpu as pltpu
from jax.sharding import PartitionSpec as P


BURNERS = 16
MOUTH = 8
SWEEPS = 4
SUBSTEPS = 8

time_step = 0.2
diffusion = 0.05
inflow_rate = 0.5
wave_speed = 0.5
heat_coupling = 0.5
feedback = 0.5

F32 = jnp.float32
BF16 = jnp.bfloat16
HALO = SWEEPS - 1
EDGE = 8
VMEM = pl.BlockSpec(memory_space=pltpu.VMEM)
SMEM = pl.BlockSpec(memory_space=pltpu.SMEM)
HBM = pl.BlockSpec(memory_space=pltpu.HBM)


def halves(table):
    high = table.astype(BF16)
    low = (table - high.astype(np.float64)).astype(BF16)
    return high, low


def axial_tables(cells):
    index = np.arange(1, cells + 1, dtype=np.float64)
    basis = math.sqrt(2.0 / (cells + 1)) * np.sin(
        np.pi * ((index[:, None] * index[None, :]) % (2 * (cells + 1))) / (cells + 1)
    )
    return basis, 2.0 * np.cos(np.pi * index / (cells + 1))


def mode_classes(n_theta):
    half = n_theta // 2
    multiples = np.arange(0, half, 4)
    first = (
        np.concatenate([multiples, [half], multiples[1:]]),
        np.concatenate([np.zeros(len(multiples) + 1), np.ones(len(multiples) - 1)]),
    )
    twos = np.arange(2, half, 4)
    second = (np.concatenate([twos, twos]), np.repeat([0, 1], len(twos)))
    ones, threes = np.arange(1, half, 4), np.arange(3, half, 4)
    third = (np.concatenate([ones, threes, ones, threes]), np.repeat([0, 1], half // 2))
    return first, second, third


def azimuth_tables(n_theta):
    bases = []
    for (order, odd), rows in zip(mode_classes(n_theta), (n_theta // 4, n_theta // 4, n_theta // 2)):
        phase = (np.arange(rows)[:, None] * order[None, :].astype(np.int64)) % n_theta
        angle = phase * (2.0 * np.pi / n_theta)
        bases.append(np.where(odd[None, :] == 0, np.cos(angle), np.sin(angle)))
    return bases


def diagonal_tables(n_theta):
    half = n_theta // 2
    order = np.concatenate([part[0] for part in mode_classes(n_theta)])
    shifted = 2.0 - 2.0 * np.cos(order * (2.0 * np.pi / n_theta))
    weight = np.where((order == 0) | (order == half), 1.0, 2.0) / n_theta
    return (4.0 + shifted).astype(np.float32), weight.astype(np.float32)


def split(value):
    high = value.astype(BF16)
    return high, (value - high.astype(F32)).astype(BF16)


def product(left, right, dims):
    def one(a, b):
        return lax.dot_general(a, b, (dims, ((), ())), preferred_element_type=F32)

    return one(left[0], right[0]) + (one(left[1], right[0]) + one(left[0], right[1]))


NN = ((1,), (0,))
NT = ((1,), (1,))


def edges_kernel(density, swirl, heat_rate, acoustic, pair, link, rho, rate, spin, wave, sems):
    cells_theta, cells_radius, _ = density.shape
    odd = lax.axis_index("sector") % 2
    copies = []

    def fetch(source, target):
        copy = pltpu.make_async_copy(source, target, sems.at[len(copies)])
        copy.start()
        copies.append(copy)

    for side, begin, row in ((0, 0, 0), (1, cells_theta - EDGE, cells_theta - 1)):
        fetch(density.at[pl.ds(begin, EDGE)], rho.at[side])
        fetch(heat_rate.at[pl.ds(begin, EDGE)], rate.at[side])
        fetch(swirl.at[pl.ds(row, 1)], spin.at[side])
        fetch(acoustic.at[:, pl.ds(begin, EDGE)], wave.at[side])
    for copy in copies:
        copy.wait()
    for out, side in ((pair, 1 - odd), (link, odd)):
        edge = jnp.where(side == 0, rho[0, 0], rho[1, EDGE - 1])
        out[0:cells_radius] = edge
        out[cells_radius : 2 * cells_radius] = edge * spin[side, 0]
        at = 2 * cells_radius
        for k in range(3):
            out[at : at + EDGE] = wave[side, k]
            at += EDGE
        heat = jnp.sum(rate[side] * rho[side] * rho[side], axis=1)
        out[at : at + EDGE] = heat


def flat(ref):
    cells_theta, cells_radius, cells_axial = ref.shape
    return ref.reshape(cells_theta * cells_radius, cells_axial)


def plane(shape, r):
    return pl.ds(r, shape[0], stride=shape[1])


def flow_rows(n_theta, mouth_azimuth, mouth_radius, density, swirl, forcing):
    sector = lax.axis_index("sector")
    radial = lax.axis_index("radial")
    cells_theta, cells_radius, cells_axial = density.shape
    shape = (cells_radius, cells_axial)
    rows = lax.broadcasted_iota(jnp.int32, shape, 0)
    lanes = lax.broadcasted_iota(jnp.int32, shape, 1)
    segment = n_theta // BURNERS
    part = min(segment, cells_theta)
    zero = jnp.zeros(shape, F32)

    def at(t):
        if t < 0 or t >= cells_theta:
            return zero, zero
        rho = density[t]
        return rho, rho * swirl[t]

    window = [at(-1), at(0)]
    for t in range(cells_theta):
        window.append(at(t + 1))
        (rho_down, flux_down), (rho, _), (rho_up, flux_up) = window
        window = window[1:]
        if t % part == 0:
            burner = (sector * cells_theta + t) // segment
            start = burner * segment + mouth_azimuth[burner] - sector * cells_theta
            radius = mouth_radius[burner] - radial * cells_radius
            mouth = ((rows >= radius) & (rows < radius + MOUTH)).astype(F32)
            mouth = mouth * (inflow_rate / time_step)
        gain = mouth * ((start <= t) & (t < start + MOUTH)).astype(F32)
        r_up = jnp.where(rows == cells_radius - 1, 0.0, pltpu.roll(rho, cells_radius - 1, 0))
        r_down = jnp.where(rows == 0, 0.0, pltpu.roll(rho, 1, 0))
        z_up = jnp.where(lanes == cells_axial - 1, 0.0, pltpu.roll(rho, cells_axial - 1, 1))
        z_down = jnp.where(lanes == 0, 0.0, pltpu.roll(rho, 1, 1))
        twice = 2.0 * rho
        laplace = (rho_up + rho_down - twice) + (r_up + r_down - twice) + (z_up + z_down - twice)
        forcing[t] = -0.5 * (flux_up - flux_down) + diffusion * laplace + gain * (1.0 - rho)


def add_halos(forcing, radial_pair, radial_link, sector_pair, sector_link):
    radials = lax.axis_size("radial")
    radial = lax.axis_index("radial")
    cells_theta, cells_radius, _ = forcing.shape
    odd = lax.axis_index("sector") % 2 == 1
    above = jnp.where(odd, sector_link[...], sector_pair[...])
    below = jnp.where(odd, sector_pair[...], sector_link[...])
    odd = radial % 2 == 1
    inner = jnp.where(odd, radial_pair[...], radial_link[...])
    outer = jnp.where(odd, radial_link[...], radial_pair[...])
    rho, flux = slice(0, cells_radius), slice(cells_radius, 2 * cells_radius)
    end = cells_theta - 1
    forcing[0] = forcing[0] + (0.5 * below[flux] + diffusion * below[rho])
    forcing[end] = forcing[end] + (diffusion * above[rho] - 0.5 * above[flux])
    inside = diffusion * (radial > 0).astype(F32)
    outside = diffusion * (radial < radials - 1).astype(F32)
    rows = flat(forcing)
    for r, term in ((0, inside * inner), (cells_radius - 1, outside * outer)):
        at = plane(forcing.shape, r)
        rows[at, :] = rows[at, :] + term
    return above, below


def flow_kernel(
    n_theta, mouth_azimuth, mouth_radius, density, swirl, heat_rate, _, forcing, heat, pair, link
):
    cells_theta, cells_radius, _ = density.shape
    odd = lax.axis_index("radial") % 2 == 1
    rows = flat(density)
    first, last = (rows[plane(density.shape, r), :] for r in (0, cells_radius - 1))
    pair[...] = jnp.where(odd, first, last)
    link[...] = jnp.where(odd, last, first)
    flow_rows(n_theta, mouth_azimuth, mouth_radius, density, swirl, forcing)
    for t in range(0, cells_theta, 8):
        rho = density[t : t + 8]
        heat[t : t + 8] = jnp.sum(heat_rate[t : t + 8] * rho * rho, axis=1)


def sine_modes(basis, fields):
    high, low = split(basis)
    count = high.shape[0]
    left = jnp.concatenate(
        [jnp.concatenate([high, high], 1), jnp.concatenate([low, jnp.zeros_like(low)], 1)], 0
    )
    right = jnp.concatenate([jnp.concatenate(split(field), 1) for field in fields], 0)
    out = lax.dot_general(left, right, (NT, ((), ())), preferred_element_type=F32)
    return out[:count] + out[count:]


GROUP = 4


def first_kernel(
    partial, heat, radial_pair, radial_link, sector_pair, sector_link, basis, send, wide_heat,
    forcing, staged, sems
):
    cells_theta, cells_radius, cells_axial = partial.shape
    sectors = send.shape[0]
    own = cells_axial // sectors
    forcing[...] = partial[...]
    above, below = add_halos(forcing, radial_pair, radial_link, sector_pair, sector_link)
    at = above.shape[0] - EDGE
    wide_heat[:EDGE] = below[at:]
    wide_heat[EDGE : EDGE + cells_theta] = heat[...]
    wide_heat[EDGE + cells_theta :] = above[at:]
    copies = []

    def leave(begin, count):
        part = pl.ds(begin, count)
        copy = pltpu.make_async_copy(
            staged.at[:, part, :], send.at[:, part, :], sems.at[len(copies)]
        )
        copy.start()
        copies.append(copy)

    mine, rows = basis[...], flat(forcing)
    for r in range(0, cells_radius, GROUP):
        modes = sine_modes(mine, [rows[plane(forcing.shape, r + i), :] for i in range(GROUP)])
        for i in range(GROUP):
            lane = slice(i * cells_theta, (i + 1) * cells_theta)
            for d in range(sectors):
                staged[d, (r + i) * own : (r + i + 1) * own, :] = modes[
                    d * own : (d + 1) * own, lane
                ]
        leave(r * own, GROUP * own)

    for copy in copies:
        copy.wait()


def acoustic_kernel(
    n_radius, heat, other_heat, acoustic, pair, link, basis, acoustic_next, *parts
):
    sector, radial = lax.axis_index("sector"), lax.axis_index("radial")
    cells_theta, cells_axial = acoustic.shape[1:]
    odd = sector % 2 == 1
    above = jnp.where(odd, link[...], pair[...])
    below = jnp.where(odd, pair[...], link[...])
    skip = above.shape[0] - 4 * EDGE

    def extended(k):
        rows = slice(skip + k * EDGE, skip + (k + 1) * EDGE)
        return jnp.concatenate([below[rows], acoustic[k], above[rows]], 0)

    press, along, axial = extended(0), extended(1), extended(2)
    warm = (heat[...] + other_heat[...]) * (heat_coupling / n_radius)
    count = press.shape[0]
    lanes = lax.broadcasted_iota(jnp.int32, press.shape, 1)
    for _ in range(SUBSTEPS):
        press_up = pltpu.roll(press, count - 1, 0)
        press_axial = jnp.where(lanes == cells_axial - 1, 0.0, pltpu.roll(press, cells_axial - 1, 1))
        along = along - wave_speed * (press_up - press)
        axial = axial - wave_speed * (press_axial - press)
        along_down = pltpu.roll(along, 1, 0)
        axial_down = jnp.where(lanes == 0, 0.0, pltpu.roll(axial, 1, 1))
        press = press - wave_speed * ((along - along_down) + (axial - axial_down)) + warm
    middle = slice(EDGE, EDGE + cells_theta)
    for k, field in enumerate((press, along, axial)):
        acoustic_next[k] = field[middle]
    count, own = len(parts), parts[0].shape[1]
    rows = [
        basis[pl.ds(pl.multiple_of((sector ^ (radial * count + j)) * own, 8), own), :]
        for j in range(count)
    ]
    modes = sine_modes(jnp.concatenate(rows, 0), [feedback * press[middle]])
    for j in range(count):
        parts[j][0] = modes[j * own : (j + 1) * own]


def wave_kernel(count, *refs):
    parts, (table, wave, pieces) = refs[:-3], refs[-3:]
    sector, radial = lax.axis_index("sector"), lax.axis_index("radial")
    for i, part in enumerate(parts):
        offset, j = divmod(i, count)
        pieces[sector ^ ((radial ^ offset) * count + j)] = part[...].reshape(part.shape[-2:])

    def store(lane, out):
        wave[:, lane] = out

    transformed([pieces[s] for s in range(pieces.shape[0])], table, store)


def transformed(values, table, store):
    sectors = len(values)
    quarter, half = sectors // 4, sectors // 2

    def joined(parts):
        return jnp.concatenate(parts, 1) if len(parts) > 1 else parts[0]

    even = [values[s] + values[s + half] for s in range(half)]
    odd = [values[s] - values[s + half] for s in range(half)]
    both = [even[s] + even[s + quarter] for s in range(quarter)]
    apart = [even[s] - even[s + quarter] for s in range(quarter)]
    at = 0
    for parts, pieces in zip((both, apart, odd), table_parts(table)):
        width = pieces[0].shape[1]
        store(slice(at, at + width), product(split(joined(parts)), pieces, NN))
        at += width


def table_parts(table):
    n_theta = table.shape[1]
    quarter, half = n_theta // 4, n_theta // 2
    top, bottom = slice(0, quarter), slice(quarter, quarter + half)
    columns = [slice(i * quarter, (i + 1) * quarter) for i in range(4)]
    return (
        (table[top, columns[0]], table[top, columns[1]]),
        (table[top, columns[2]], table[top, columns[3]]),
        (table[bottom, :half], table[bottom, half:]),
    )


def forward_kernel(edge, received, table, *refs):
    modes, pair, link = refs[-3:]
    sectors, columns, _ = received.shape
    radial_odd = lax.axis_index("radial") % 2 == 1

    def store(lane, out):
        modes[:, lane] = out
        first, last = out[:edge], out[columns - edge :]
        pair[:, lane] = jnp.where(radial_odd, first, last)
        link[:, lane] = jnp.where(radial_odd, last, first)

    transformed([received[s] for s in range(sectors)], table, store)


def solve_kernel(
    modes, pair, link, wave, impedance, fixed, weight, axial, table, send, solved
):
    radials = lax.axis_size("radial")
    radial = lax.axis_index("radial")
    sector = lax.axis_index("sector")
    columns, n_theta = modes.shape
    each = axial.shape[1]
    cells_radius = columns // each
    has_inner = (radial > 0).astype(F32)
    has_outer = (radial < radials - 1).astype(F32)
    radial_odd = radial % 2 == 1
    eigen = axial[sector]
    step = eigen.shape[1]
    total = cells_radius + 2 * HALO
    for block in range(n_theta // step):
        lane = slice(block * step, (block + 1) * step)
        row = 1.0 / (fixed[:, lane] + impedance[:, lane])
        inv = jnp.broadcast_to(row, (each, step))
        inv_inner, inv_outer = inv * has_inner, inv * has_outer
        last_scale = jnp.broadcast_to(row * weight[:, lane], (each, step))
        add = wave[:, lane]

        def row_of(i):
            i -= HALO
            if 0 <= i < cells_radius:
                return modes[i * each : (i + 1) * each, lane]
            odd_one, even_one = (pair, link) if i < 0 else (link, pair)
            i = i + HALO if i < 0 else i - cells_radius
            rows = slice(i * each, (i + 1) * each)
            return jnp.where(radial_odd, odd_one[rows, lane], even_one[rows, lane])

        def scale_of(i):
            if i < HALO:
                return inv_inner
            return inv if i < HALO + cells_radius else inv_outer

        right = [row_of(i) + add for i in range(total)]
        x = [right[i] * scale_of(i) for i in range(total)]
        for sweep in range(1, SWEEPS):
            fresh = [None] * total
            for i in range(sweep, total - sweep):
                scale = last_scale if sweep == SWEEPS - 1 else scale_of(i)
                fresh[i] = (right[i] + (x[i + 1] + x[i - 1]) + eigen * x[i]) * scale
            x = fresh
        for i in range(cells_radius):
            solved[i * each : (i + 1) * each, lane] = x[i + HALO]

    sectors, _, width = send.shape
    outs, at = [], 0
    for pieces in table_parts(table):
        lane = slice(at, at + pieces[0].shape[1])
        outs.append(product(split(solved[:, lane]), pieces, NT))
        at = lane.stop
    both, apart, odd = outs
    even = jnp.concatenate([both + apart, both - apart], 1)
    for s in range(sectors // 2):
        lane = slice(s * width, (s + 1) * width)
        send[s] = even[:, lane] + odd[:, lane]
        send[s + sectors // 2] = even[:, lane] - odd[:, lane]


def pressure_kernel(received, basis, pressure_out, pressure, sems):
    sectors = received.shape[0]
    cells_radius = pressure.shape[1]
    own = received.shape[1] // cells_radius
    high, low = split(basis[...])
    right = jnp.concatenate(
        [jnp.concatenate([high, low], 1), jnp.concatenate([high, jnp.zeros_like(low)], 1)], 0
    )
    cells_axial = high.shape[1]
    copies = []
    for r in range(cells_radius):
        rows = [received[d, r * own : (r + 1) * own, :] for d in range(sectors)]
        modes = jnp.concatenate(rows, 0)
        left = jnp.concatenate(split(modes.T), 1)
        out = lax.dot_general(left, right, (NN, ((), ())), preferred_element_type=F32)
        flat(pressure)[plane(pressure.shape, r), :] = out[:, :cells_axial] + out[:, cells_axial:]
        if r % 8 == 7:
            rows = pl.ds(r - 7, 8)
            copy = pltpu.make_async_copy(
                pressure.at[:, rows, :], pressure_out.at[:, rows, :], sems.at[r // 8]
            )
            copy.start()
            copies.append(copy)
    for copy in copies:
        copy.wait()


def impedance_kernel(impedance, _, rows):
    half = impedance.shape[1] - 1
    count = half // 4
    pieces, rest = [], jnp.broadcast_to(impedance[:, :half], (8, half))
    for _ in range(3):
        piece = rest.astype(BF16)
        pieces.append(piece)
        rest = rest - piece.astype(F32)
    index = lax.broadcasted_iota(jnp.int32, (half, count), 0)
    target = 4 * lax.broadcasted_iota(jnp.int32, (half, count), 1)
    by_four = []
    for q in range(4):
        pick = (index == target + q).astype(F32).astype(BF16)
        parts = [
            lax.dot_general(piece, pick, (NN, ((), ())), preferred_element_type=F32)
            for piece in pieces
        ]
        by_four.append((parts[0] + (parts[1] + parts[2]))[:1])
    q0, q1, q2, q3 = by_four
    lanes = lax.broadcasted_iota(jnp.int32, (1, count), 1)
    last = jnp.broadcast_to(impedance[:, half:], (1, count))
    rows[...] = jnp.concatenate([q0, jnp.where(lanes == 0, last, q0), q2, q2, q1, q3, q1, q3], 1)


def add_kernel(left, right, out):
    out[...] = left[...] + right[...]


def step_kernel(
    n_theta, mouth_azimuth, mouth_radius, density, swirl, radial_pair, radial_link, sector_pair,
    sector_link, density_next, forcing
):
    flow_rows(n_theta, mouth_azimuth, mouth_radius, density, swirl, forcing)
    add_halos(forcing, radial_pair, radial_link, sector_pair, sector_link)
    density_next[...] = density[...] + time_step * forcing[...]


def call(kernel, outs, ins, scratch=(), limit=12 * 1024 * 1024, **more):
    moved = sum(math.prod(o.shape) * 4 for o in outs)
    return pl.pallas_call(
        kernel,
        out_shape=outs,
        in_specs=ins,
        out_specs=more.pop("out_specs", [VMEM] * len(outs)),
        scratch_shapes=list(scratch),
        cost_estimate=pl.CostEstimate(flops=0, bytes_accessed=3 * moved, transcendentals=0),
        compiler_params=pltpu.CompilerParams(vmem_limit_bytes=limit),
        **more,
    )


def shape(*dims):
    return jax.ShapeDtypeStruct(dims, F32)


def paired(pair, link, axis, closed):
    count = lax.axis_size(axis)
    first = [(i, i ^ 1) for i in range(count)]
    second = [(i, (i + 1) % count) for i in range(1, count if closed else count - 1, 2)]
    second += [(j, i) for i, j in second]
    return lax.ppermute(pair, axis, first), lax.ppermute(link, axis, second)


def swapped(value, axis, bits):
    return lax.ppermute(value, axis, [(i, i ^ bits) for i in range(lax.axis_size(axis))])


def halves_of_sum(value, axis, step=1):
    if step >= lax.axis_size(axis):
        return value, jnp.zeros_like(value)
    while True:
        other = swapped(value, axis, step)
        step *= 2
        if step >= lax.axis_size(axis):
            return value, other
        value = added(value, other)


def spread_part(part, j, count):
    sectors, radials = lax.axis_size("sector"), lax.axis_size("radial")
    pairs = [
        (s * radials + r, (s ^ (r * count + j)) * radials + r)
        for s in range(sectors)
        for r in range(radials)
    ]
    return lax.ppermute(part, ("sector", "radial"), pairs)


def added(left, right):
    return call(add_kernel, [shape(*left.shape)], [VMEM] * 2, limit=4 * 1024 * 1024)(left, right)[0]


def in_hbm(value):
    return pltpu.with_memory_space_constraint(value, pltpu.HBM)


def in_vmem(value):
    return pltpu.with_memory_space_constraint(value, pltpu.VMEM)


def exchanged(value):
    return lax.all_to_all(value, "sector", split_axis=0, concat_axis=0, tiled=True)


def section(density, swirl, heat_rate, acoustic, mode_impedance, mouth_azimuth, mouth_radius):
    sectors = lax.axis_size("sector")
    radials = lax.axis_size("radial")
    cells_theta, cells_radius, cells_axial = density.shape
    n_theta = cells_theta * sectors
    n_radius = cells_radius * radials
    own = cells_axial // sectors
    columns = cells_radius * own
    edge = HALO * own

    basis, eigen = axial_tables(cells_axial)
    basis = jnp.asarray(basis.astype(np.float32))
    eigen = jnp.asarray(
        np.broadcast_to(eigen.reshape(sectors, own, 1), (sectors, own, 128)).astype(np.float32)
    )
    parts = [halves(table) for table in azimuth_tables(n_theta)]
    table = jnp.asarray(
        np.concatenate(
            [np.concatenate(parts[0] + parts[1], 1), np.concatenate(parts[2], 1)], 0
        )
    )
    fixed, weight = diagonal_tables(n_theta)
    fixed, weight = jnp.asarray(fixed)[None, :], jnp.asarray(weight)[None, :]
    (impedance,) = call(impedance_kernel, [shape(1, n_theta)], [VMEM] * 2)(
        mode_impedance[None, :], table
    )

    packed = 2 * cells_radius + 4 * EDGE
    row_block = shape(cells_theta, cells_axial)
    pair, link = call(
        edges_kernel,
        [shape(packed, cells_axial)] * 2,
        [HBM] * 4,
        [
            pltpu.VMEM((2, EDGE, cells_radius, cells_axial), F32),
            pltpu.VMEM((2, EDGE, cells_radius, cells_axial), F32),
            pltpu.VMEM((2, 1, cells_radius, cells_axial), F32),
            pltpu.VMEM((2, 3, EDGE, cells_axial), F32),
            pltpu.SemaphoreType.DMA((8,)),
        ],
    )(*[in_hbm(value) for value in (density, swirl, heat_rate, acoustic)])
    sector_halo = paired(pair, link, "sector", True)
    edge_rows = pair
    partial, heat, pair, link = call(
        lambda *refs: flow_kernel(n_theta, *refs),
        [shape(*density.shape)] + [row_block] * 3,
        [SMEM] * 2 + [VMEM] * 3 + [HBM],
    )(mouth_azimuth, mouth_radius, density, swirl, heat_rate, edge_rows)
    radial_halo = paired(pair, link, "radial", False)
    send, heat = call(
        first_kernel,
        [
            pltpu.HBM((sectors, columns, cells_theta), F32),
            shape(cells_theta + 2 * EDGE, cells_axial),
        ],
        [VMEM] * 7,
        [
            pltpu.VMEM(density.shape, F32),
            pltpu.VMEM((sectors, columns, cells_theta), F32),
            pltpu.SemaphoreType.DMA((cells_radius // GROUP,)),
        ],
        out_specs=[HBM, VMEM],
    )(partial, heat, *radial_halo, *sector_halo, basis)
    received = exchanged(send)

    count = sectors // radials
    acoustic_next, *parts = call(
        lambda *refs: acoustic_kernel(n_radius, *refs),
        [shape(*acoustic.shape)] + [shape(1, own, cells_theta)] * count,
        [VMEM] * 6,
    )(*halves_of_sum(heat, "radial"), acoustic, *sector_halo, basis)
    parts = [spread_part(part, j, count) for j, part in enumerate(parts)]
    step = 1
    while step < radials:
        parts += [swapped(value, "radial", step) for value in parts]
        step *= 2
    (wave,) = call(
        lambda *refs: wave_kernel(count, *refs),
        [shape(own, n_theta)],
        [VMEM] * (sectors + 1),
        [pltpu.VMEM((sectors, own, cells_theta), F32)],
    )(*parts, table)
    (density_next,) = call(
        lambda *refs: step_kernel(n_theta, *refs),
        [shape(*density.shape)],
        [SMEM] * 2 + [VMEM] * 6,
        [pltpu.VMEM(density.shape, F32)],
    )(mouth_azimuth, mouth_radius, density, swirl, *radial_halo, *sector_halo)

    modes, pair, link = call(
        lambda *refs: forward_kernel(edge, *refs),
        [shape(columns, n_theta), shape(edge, n_theta), shape(edge, n_theta)],
        [VMEM] * 2 + [HBM] * 3,
    )(in_vmem(received), table, in_hbm(density_next), in_hbm(acoustic_next), impedance)
    (send,) = call(
        solve_kernel,
        [shape(sectors, columns, cells_theta)],
        [VMEM] * 9,
        [pltpu.VMEM((columns, n_theta), F32)],
    )(modes, *paired(pair, link, "radial", False), wave, impedance, fixed, weight, eigen, table)
    (pressure,) = call(
        pressure_kernel,
        [shape(*density.shape)],
        [VMEM] * 2,
        [pltpu.VMEM(density.shape, F32), pltpu.SemaphoreType.DMA((cells_radius // 8,))],
        out_specs=[HBM],
    )(exchanged(send), basis)
    return density_next, pressure, acoustic_next


def solution(mesh):
    return jax.shard_map(
        section,
        mesh=mesh,
        in_specs=(
            P("sector", "radial", None),
            P("sector", "radial", None),
            P("sector", "radial", None),
            P(None, "sector", None),
            P(),
            P(),
            P(),
        ),
        out_specs=(
            P("sector", "radial", None),
            P("sector", "radial", None),
            P(None, "sector", None),
        ),
        check_vma=False,
    )
```
